128 devices in a mesh: ctx: 16 (over y, z), pack: 8 (over x, core).
Axes of the slice: x: 4, y: 4, z: 4, core: 2. Of those that a mesh axis runs over, the one named last changes fastest.
Arguments:
- hidden: bfloat16 [32768, 2048], P(('ctx', 'pack')), may hold values from -4 to 4
- first_keys: bfloat16 [32768, 2048], P('ctx', 'pack'), may hold values from -400 to 400
- first_values: bfloat16 [32768, 2048], P('ctx', 'pack'), may hold values from -18 to 18
- w_query: bfloat16 [2048, 2048], P(None, 'pack'), may hold values from -0.125 to 0.125
- w_out: bfloat16 [2048, 2048], P('pack'), may hold values from -0.125 to 0.125
- norm_gain: float32 [2048], replicated, may hold values from 0.1 to 1.9
- router_weight: float32 [2048], replicated, may hold values from -0.5 to 0.5
- route_list: int32 [16, 512], P('ctx'), may hold values from 0 to 2047, as said below
- pack_order: int32 [16, 512], P('ctx'), may hold values from 0 to 511, each once within a row
- pattern: int32 [16, 12], replicated, may hold values from 0 to 15
Outputs:
- hidden_out: bfloat16 [32768, 2048], P(('ctx', 'pack'))
- packed_states: bfloat16 [8192, 2048], P(('ctx', 'pack'))
The draws below stay inside these ranges and needn't reach their ends.
Inputs may be any that keep to these rules, and one draw needn't show every extreme that they name: `route_list`: each row lists 512 distinct span-local positions in ascending order. At most 96 of a row's positions lie among the 256 tokens of one device, and in every row some device holds exactly 96.
All inputs are finite; a program needn't handle non-finite values.
Results may differ from the reference program's by a relative error of at most 0.023.
Values may be sent and summed in bfloat16 or wider, within the bound.
A program may use at most 128 MiB of HBM per device.

```python
import math
import jax
import jax.numpy as jnp
from jax import lax

D = 2048
HEADS = 16
HD = 128
NSEL = 12
TOK_DEV = 256
CH = 2048
SEQ = 32768
Q_CH = 512
N_CTX = 16
N_PACK = 8


def draw_route_list(key, part):
    key_counts = jax.random.fold_in(key, 101)
    key_top = jax.random.fold_in(key, 202)
    key_pick = jax.random.fold_in(key, 303)
    shifts = jax.random.randint(key_counts, (N_CTX, N_PACK), 0, TOK_DEV // 8 + 1)
    top_lane = jax.random.randint(key_top, (N_CTX, 1), 0, N_PACK)
    lane_ids = jnp.arange(N_PACK, dtype=jnp.int32)[None, :]
    shifts = jnp.where(lane_ids == top_lane, TOK_DEV // 8, jnp.where(lane_ids == (top_lane + 1) % N_PACK, 0, shifts))
    counts = TOK_DEV // 4 + shifts - jnp.roll(shifts, -1, axis=1)
    scores = jax.random.randint(key_pick, (N_CTX, N_PACK, TOK_DEV), 0, 1 << 20) * TOK_DEV + jnp.arange(TOK_DEV, dtype=jnp.int32)[None, None, :]
    ranks = jnp.argsort(jnp.argsort(scores, axis=-1), axis=-1)
    chosen = (ranks < counts[:, :, None]).reshape(N_CTX, CH)
    sort_keys = jnp.where(chosen, 0, CH) + jnp.arange(CH, dtype=jnp.int32)[None, :]
    listed = jnp.argsort(sort_keys, axis=1)[:, :Q_CH]
    return listed.astype(jnp.int32)


def draw_first_keys(key, part):
    base = jax.random.normal(key, (SEQ, D), jnp.float32)
    drawn = jnp.clip(base, -6.0, 6.0) * 2.0
    return drawn.astype(jnp.bfloat16)


def plant(array, stream_key, low, high):
    dims = array.shape
    spot = [jax.random.randint(jax.random.fold_in(stream_key, axis), (), 0, dims[axis]) for axis in range(len(dims))]
    array = array.at[tuple(spot)].set(low)
    longest = dims.index(max(dims))
    spot[longest] = (spot[longest] + 1) % dims[longest]
    return array.at[tuple(spot)].set(high)


def shard_levels(rng, shape, split, least, top_value):
    def one(axis_at, parts):
        steps = jax.random.uniform(jax.random.fold_in(jax.random.fold_in(rng, 6), axis_at), (parts,), jnp.float32, least / len(split), top_value / len(split))
        return jnp.repeat(jnp.exp(steps), shape[axis_at] // parts).reshape((-1,) + (1,) * (len(shape) - axis_at - 1))

    loudness = one(*split[0])
    for cut in split[1:]:
        loudness = loudness * one(*cut)
    return loudness


def scatter_about(stream_key, extent, deviation, reach, shards=(), kind=jnp.bfloat16):
    loudness = shard_levels(stream_key, extent, shards, -0.22, 0.18) if shards else 1.0
    entries = jax.random.normal(stream_key, extent, jnp.float32) * deviation * loudness
    return jnp.minimum(jnp.maximum(entries, -reach), reach).astype(kind)


def setup_inputs(seed: int = 0) -> dict:
    seeds = jax.random.split(jax.random.key(seed), 11)
    return {
        "hidden": scatter_about(seeds[0], (SEQ, D), 0.25, 4.0, ((0, 128),)),
        "first_keys": draw_first_keys(jax.random.fold_in(seeds[10], 71), 0),
        "first_values": scatter_about(seeds[2], (SEQ, D), 3.0, 18.0, ((0, 16), (1, 8))),
        "w_query": scatter_about(seeds[3], (D, D), D ** -0.5, 0.125, ((1, 8),)),
        "w_out": scatter_about(seeds[4], (D, D), D ** -0.5, 0.125, ((0, 8),)),
        "norm_gain": jnp.clip(1.0 + 0.18 * jax.random.normal(seeds[5], (D,), jnp.float32), 0.1, 1.9),
        "router_weight": scatter_about(seeds[6], (D,), (D // 16) ** -0.5, 0.5, (), jnp.float32),
        "route_list": draw_route_list(jax.random.fold_in(seeds[10], 71), 0),
        "pack_order": jax.vmap(lambda own: jax.random.permutation(own, Q_CH))(jax.random.split(seeds[8], N_CTX)).reshape((N_CTX, Q_CH)).astype(jnp.int32),
        "pattern": plant(jax.random.randint(seeds[9], (N_CTX, NSEL), 0, N_CTX), jax.random.fold_in(seeds[9], 1), 0, N_CTX - 1).astype(jnp.int32),
    }


epsilon = 1e-06
very_negative = -1e+30

def rotate(projected, position, head_count):
    row_count = projected.shape[0]
    head_size = projected.shape[1] // head_count
    half_size = head_size // 2
    frequency = 10000.0 ** (-jnp.arange(half_size, dtype=jnp.float32) * 2.0 / head_size)
    angle = position.astype(jnp.float32)[:, None] * frequency[None, :]
    cosine = jnp.cos(angle)[:, None, :]
    sine_part = jnp.sin(angle)[:, None, :]
    shaped = projected.reshape(row_count, head_count, head_size)
    front_half = shaped[..., :half_size]
    back_half = shaped[..., half_size:]
    turned = jnp.concatenate([front_half * cosine - back_half * sine_part, back_half * cosine + front_half * sine_part], axis=-1)
    return turned.reshape(row_count, head_count * head_size)

def partial_block(query_heads, key_heads, value_heads, allowed):
    scale_factor = 1.0 / math.sqrt(query_heads.shape[2])
    scores = jnp.einsum('qhd,khd->hqk', query_heads.astype(jnp.float32), key_heads.astype(jnp.float32)) * scale_factor
    if allowed is not None:
        scores = jnp.where(allowed[None], scores, very_negative)
    row_peak = lax.optimization_barrier(jnp.max(scores, axis=-1))
    weights = jnp.exp(scores - row_peak[..., None])
    if allowed is not None:
        weights = jnp.where(allowed[None], weights, 0.0)
    weight_sum = lax.optimization_barrier(jnp.sum(weights, axis=-1))
    rounded = weights.astype(jnp.bfloat16)
    summed = jnp.einsum('hqk,khd->qhd', rounded.astype(jnp.float32), value_heads.astype(jnp.float32))
    return (row_peak, weight_sum, summed)

def merge(former, latter):
    new_peak = jnp.maximum(former[0], latter[0])
    former_scale = jnp.exp(former[0] - new_peak)
    latter_scale = jnp.exp(latter[0] - new_peak)
    weight_sum = former_scale * former[1] + latter_scale * latter[1]
    summed = jnp.transpose(former_scale)[:, :, None] * former[2] + jnp.transpose(latter_scale)[:, :, None] * latter[2]
    return (new_peak, weight_sum, summed)

def reference(hidden, first_keys, first_values, w_query, w_out, norm_gain, router_weight, route_list, pack_order, pattern):
    picked = jnp.take_along_axis(route_list, pack_order, axis=1)
    position = (picked + (jnp.arange(N_CTX, dtype=jnp.int32) * CH)[:, None]).reshape(-1).astype(jnp.int32)
    routed_rows = hidden[position]
    rows_float = routed_rows.astype(jnp.float32)
    gate_value = jax.nn.sigmoid(jnp.dot(rows_float, router_weight, precision=lax.Precision.HIGHEST))
    mean_square = lax.optimization_barrier(jnp.mean(rows_float * rows_float, axis=-1, keepdims=True))
    normed = (rows_float * lax.rsqrt(mean_square + epsilon) * norm_gain).astype(jnp.bfloat16)
    queries = rotate(jnp.dot(normed, w_query, preferred_element_type=jnp.float32), position, HEADS).astype(jnp.bfloat16)

    def one_span(span_idx):
        query_heads = lax.dynamic_slice_in_dim(queries, span_idx * Q_CH, Q_CH, 0).reshape(Q_CH, HEADS, HD)
        query_pos = lax.dynamic_slice_in_dim(position, span_idx * Q_CH, Q_CH, 0)
        own_keys = lax.dynamic_slice_in_dim(first_keys, span_idx * CH, CH, 0).reshape(CH, HEADS, HD)
        own_values = lax.dynamic_slice_in_dim(first_values, span_idx * CH, CH, 0).reshape(CH, HEADS, HD)
        key_pos = span_idx * CH + jnp.arange(CH, dtype=jnp.int32)
        running = partial_block(query_heads, own_keys, own_values, key_pos[None, :] <= query_pos[:, None])
        wanted = pattern[span_idx]

        def visit(block_idx, held):
            block_idx = block_idx.astype(jnp.int32)
            active = jnp.logical_and(block_idx < span_idx, jnp.any(wanted == block_idx))

            def take(inner):
                key_block = lax.dynamic_slice_in_dim(first_keys, block_idx * CH, CH, 0).reshape(CH, HEADS, HD)
                value_block = lax.dynamic_slice_in_dim(first_values, block_idx * CH, CH, 0).reshape(CH, HEADS, HD)
                return merge(inner, partial_block(query_heads, key_block, value_block, None))
            return lax.cond(active, take, lambda inner: inner, held)
        running = lax.fori_loop(jnp.int32(0), jnp.int32(N_CTX), visit, running)
        attended = running[2] / jnp.transpose(running[1])[:, :, None]
        return attended.reshape(Q_CH, D).astype(jnp.bfloat16)
    attended = lax.map(one_span, jnp.arange(N_CTX, dtype=jnp.int32)).reshape(N_CTX * Q_CH, D)
    mixed = jnp.dot(attended, w_out, preferred_element_type=jnp.float32)
    packed_states = (rows_float + gate_value[:, None] * mixed).astype(jnp.bfloat16)
    hidden_out = hidden.at[position].set(packed_states)
    return (hidden_out, packed_states)
```

```python
import functools
import math

import jax
import jax.numpy as jnp
import numpy as np
from jax import lax
from jax.experimental import pallas as pl
from jax.experimental.pallas import tpu as pltpu
from jax.sharding import PartitionSpec as P

HD = 128
EPS = 1e-6
NEG = -1e30
F32 = jnp.float32
BF16 = jnp.bfloat16
MESH = pl.DeviceIdType.MESH
LOG2E = 1.4426950408889634


def turn_table():
    lane = np.arange(HD) % (HD // 2)
    turns = 10000.0 ** (-2.0 * lane / HD) / (2.0 * math.pi)
    table = np.zeros((8, HD), np.float32)
    table[0] = np.mod(turns * 128.0, 1.0)
    table[1] = turns
    table[2] = np.where(np.arange(HD) < HD // 2, -1.0, 1.0)
    return table


def cos_sin(pos, table):
    hi = jnp.floor(pos * (1.0 / 128.0))
    low = pos - hi * 128.0
    u = hi * table[0:1]
    u = u - jnp.floor(u) + low * table[1:2]
    u = u - jnp.floor(u + 0.5)
    x = u * math.pi
    y = x * x
    s = 0.0
    for n in (11, 9, 7, 5, 3):
        s = (s + (-1.0) ** ((n - 1) // 2) / math.factorial(n)) * y
    s = (s + 1.0) * x
    c = 0.0
    for n in (12, 10, 8, 6, 4, 2):
        c = (c + (-1.0) ** (n // 2) / math.factorial(n)) * y
    c = c + 1.0
    return 1.0 - 2.0 * s * s, 2.0 * s * c


def body(
    n_ctx,
    n_pack,
    hidden,
    keys,
    values,
    w_query,
    w_out,
    gain,
    router,
    routes,
    order,
    pattern,
    table,
    hidden_out,
    packed,
    rows_all,
    q_pad,
    spread,
    slot_of,
    v_ext,
    q_buf,
    o_send,
    o_in,
    st_send,
    st_in,
    acc,
    att,
    w_all,
    a_send,
    a_in,
    res,
    gate,
    row_send,
    row_recv,
    wo_send,
    wo_recv,
    q_send_sem,
    q_recv_sem,
    o_send_sem,
    o_recv_sem,
    s_send_sem,
    s_recv_sem,
    a_send_sem,
    a_recv_sem,
    loc_sem,
):
    me_c = lax.axis_index("ctx")
    me_p = lax.axis_index("pack")
    tok = hidden.shape[0]
    width = hidden.shape[1]
    span = keys.shape[0]
    routed = routes.shape[1]
    cap = rows_all.shape[1]
    per_slot = routed // n_pack
    half = cap // 2
    sib = me_p + 1 - 2 * lax.rem(me_p, 2)
    right = lax.rem(me_p + 2, n_pack)
    left = lax.rem(me_p + n_pack - 2, n_pack)
    far = lax.rem(me_p + 4, n_pack)
    sib_left = lax.rem(sib + n_pack - 2, n_pack)
    sib_right = lax.rem(sib + 2, n_pack)
    sib_far = lax.rem(sib + 4, n_pack)

    barrier = pltpu.get_barrier_semaphore()

    def greet_ctx(i, _):
        peer = lax.rem(me_c + i, n_ctx)
        pl.semaphore_signal(barrier, inc=1, device_id=(peer, me_p), device_id_type=MESH)
        return 0

    def greet_pack(i, _):
        peer = lax.rem(me_p + i, n_pack)
        pl.semaphore_signal(barrier, inc=1, device_id=(me_c, peer), device_id_type=MESH)
        return 0

    lax.fori_loop(1, n_pack, greet_pack, 0)
    lax.fori_loop(1, n_ctx, greet_ctx, 0)

    rf = routes[...].astype(F32)
    lane_i = lax.broadcasted_iota(jnp.int32, (cap, routed), 1).astype(F32)
    sub_j = lax.broadcasted_iota(jnp.int32, (cap, routed), 0).astype(F32)

    def spread_of(block):
        low = (block * tok).astype(F32)
        start = jnp.sum(jnp.where(rf < low, 1.0, 0.0), axis=1, keepdims=True)
        end = jnp.sum(jnp.where(rf < low + tok, 1.0, 0.0), axis=1, keepdims=True)
        hit = jnp.logical_and(lane_i == sub_j + start, lane_i < end)
        pos = jnp.sum(jnp.where(hit, rf + 1.0, 0.0), axis=1, keepdims=True) - 1.0
        return jnp.where(hit, 1.0, 0.0), pos

    _, my_pos = spread_of(me_p)
    lane_t = lax.broadcasted_iota(jnp.int32, (cap, tok), 1).astype(F32)
    pick = jnp.where(lane_t == my_pos - (me_p * tok).astype(F32), 1.0, 0.0).astype(BF16)
    rows_all[me_p] = jnp.dot(pick, hidden[...], preferred_element_type=F32).astype(BF16)

    pl.semaphore_wait(barrier, n_ctx + n_pack - 2)

    def row_copy(i, block, sub, peer):
        part = rows_all.at[block] if sub is None else rows_all.at[block, sub]
        return pltpu.make_async_remote_copy(
            src_ref=part,
            dst_ref=part,
            send_sem=row_send.at[i],
            recv_sem=row_recv.at[i],
            device_id=(me_c, peer),
            device_id_type=MESH,
        )

    first = pl.ds(0, half)
    second = pl.ds(half, half)
    to_right = row_copy(0, me_p, None, right)
    to_left = row_copy(1, me_p, None, left)
    to_sib = row_copy(2, me_p, None, sib)
    to_right.start()
    to_left.start()
    to_sib.start()

    own_w = pltpu.make_async_copy(w_out, w_all.at[pl.ds(me_p * tok, tok)], loc_sem)
    own_w.start()

    gain_row = gain[...]
    trig = table[...]
    base = (me_c * span).astype(F32)

    for b in range(n_pack):
        hit, _ = spread_of(jnp.int32(b))
        spread[pl.ds(b * cap, cap), :] = hit.astype(BF16)
    for h in range(2):
        v_ext[h, 0:HD, :] = jnp.transpose(values[:, h * HD : (h + 1) * HD])
        v_ext[h, HD:, :] = jnp.ones((v_ext.shape[1] - HD, span), BF16)
    order_col = jnp.transpose(jnp.broadcast_to(order[...].astype(F32), (HD, routed)))[:, 0:1]
    lane_s = lax.broadcasted_iota(jnp.int32, (routed, routed), 1).astype(F32)
    slot_of[...] = jnp.where(lane_s == order_col, 1.0, 0.0).astype(BF16)

    def project(block):
        rows = rows_all[block].astype(F32)
        mean_square = jnp.mean(rows * rows, axis=1, keepdims=True)
        normed = (rows * lax.rsqrt(mean_square + EPS) * gain_row).astype(BF16)
        proj = jnp.dot(normed, w_query[...], preferred_element_type=F32)
        _, pos = spread_of(block)
        cosine, sine = cos_sin(pos + base, trig)
        sine = sine * trig[2:3]
        start = pl.multiple_of(block * cap, cap)
        for h in range(2):
            part = proj[:, h * HD : (h + 1) * HD]
            turned = part * cosine + pltpu.roll(part, HD // 2, 1) * sine
            q_pad[pl.ds(start, cap), h * HD : (h + 1) * HD] = turned.astype(BF16)

    project(me_p)
    row_copy(0, left, None, right).wait_recv()
    fwd_right = row_copy(3, left, first, right)
    fwd_right.start()
    fwd_sib_left = row_copy(4, left, None, sib)
    fwd_sib_left.start()
    row_copy(1, right, None, left).wait_recv()
    fwd_left = row_copy(5, right, second, left)
    fwd_left.start()
    fwd_sib_right = row_copy(6, right, None, sib)
    fwd_sib_right.start()
    project(left)
    project(right)
    row_copy(2, sib, None, sib).wait_recv()
    project(sib)
    row_copy(4, sib_left, None, sib).wait_recv()
    project(sib_left)
    row_copy(6, sib_right, None, sib).wait_recv()
    project(sib_right)
    row_copy(3, far, first, right).wait_recv()
    row_copy(5, far, second, left).wait_recv()
    fwd_sib_far = row_copy(7, far, None, sib)
    fwd_sib_far.start()
    project(far)
    row_copy(7, sib_far, None, sib).wait_recv()
    project(sib_far)

    q_buf[me_c] = lax.dot_general(
        q_pad[...], spread[...], (((0,), (0,)), ((), ())), preferred_element_type=F32
    ).astype(BF16)

    def q_copy(c, k):
        return pltpu.make_async_remote_copy(
            src_ref=q_buf.at[c],
            dst_ref=q_buf.at[c],
            send_sem=q_send_sem.at[k],
            recv_sem=q_recv_sem.at[c],
            device_id=(k, me_p),
            device_id_type=MESH,
        )

    def send_q(k, _):
        q_copy(me_c, k).start()
        return 0

    lax.fori_loop(0, me_c, send_q, 0)

    w_half = tok // 2

    def w_copy(i, block, lo, size, peer):
        part = w_all.at[pl.ds(block * tok + lo, size)]
        return pltpu.make_async_remote_copy(
            src_ref=part,
            dst_ref=part,
            send_sem=wo_send.at[i],
            recv_sem=wo_recv.at[i],
            device_id=(me_c, peer),
            device_id_type=MESH,
        )

    own_w.wait()
    w_copy(0, me_p, 0, tok, right).start()
    w_copy(1, me_p, 0, tok, left).start()
    w_copy(2, me_p, 0, tok, sib).start()

    chunk = 512
    scale = LOG2E / math.sqrt(HD)
    key_iota = lax.broadcasted_iota(jnp.int32, (chunk, routed), 0).astype(F32)

    def attend(c, h, masked):
        cols = slice(h * HD, (h + 1) * HD)
        query = q_buf[c, cols, :]
        scores = []
        for i in range(span // chunk):
            s = jnp.dot(keys[i * chunk : (i + 1) * chunk, cols], query, preferred_element_type=F32)
            if masked:
                s = jnp.where(key_iota <= rf - float(i * chunk), s, NEG)
            scores.append(s)
        peak = functools.reduce(
            jnp.maximum, [jnp.max(s, axis=0, keepdims=True) for s in scores]
        )
        peak = peak * scale
        out = 0.0
        for i, s in enumerate(scores):
            weights = jnp.exp2(s * scale - peak).astype(BF16)
            out = out + jnp.dot(
                v_ext[h, :, i * chunk : (i + 1) * chunk], weights, preferred_element_type=F32
            )
        total = out[HD : HD + 1]
        return out[:HD] / total, peak + jnp.log2(total)

    for h in range(2):
        out, lse = attend(me_c, h, True)
        acc[h * HD : (h + 1) * HD, :] = out
        st_in[me_c, h : h + 1, :] = lse

    def o_copy(c, k):
        return pltpu.make_async_remote_copy(
            src_ref=o_send.at[c],
            dst_ref=o_in.at[k],
            send_sem=o_send_sem.at[c],
            recv_sem=o_recv_sem.at[k],
            device_id=(c, me_p),
            device_id_type=MESH,
        )

    def s_copy(c, k):
        return pltpu.make_async_remote_copy(
            src_ref=st_send.at[c],
            dst_ref=st_in.at[k],
            send_sem=s_send_sem.at[c],
            recv_sem=s_recv_sem.at[k],
            device_id=(c, me_p),
            device_id_type=MESH,
        )

    def serve(c, _):
        q_copy(c, me_c).wait_recv()
        st_send[c] = jnp.zeros((8, routed), F32)
        for h in range(2):
            out, lse = attend(c, h, False)
            o_send[c, h * HD : (h + 1) * HD, :] = out.astype(BF16)
            st_send[c, h : h + 1, :] = lse
        o_copy(c, me_c).start()
        s_copy(c, me_c).start()
        return 0

    cut = jnp.minimum(me_c + 1 + 5, n_ctx)
    lax.fori_loop(me_c + 1, cut, serve, 0)

    w_copy(0, left, 0, tok, right).wait_recv()
    w_copy(3, left, 0, w_half, right).start()
    w_copy(4, left, 0, tok, sib).start()
    w_copy(1, right, 0, tok, left).wait_recv()
    w_copy(5, right, w_half, w_half, left).start()
    w_copy(6, right, 0, tok, sib).start()

    lax.fori_loop(cut, n_ctx, serve, 0)

    w_copy(3, far, 0, w_half, right).wait_recv()
    w_copy(5, far, w_half, w_half, left).wait_recv()
    w_copy(7, far, 0, tok, sib).start()

    slot_rows = pl.ds(pl.multiple_of(me_p * per_slot, per_slot), per_slot)
    from_pad = lax.dot_general(
        slot_of[slot_rows, :], spread[...], (((1,), (1,)), ((), ())), preferred_element_type=F32
    ).astype(BF16)
    flat = n_pack * cap
    for n in range(0, width, 512):
        picked = 0.0
        for b in range(n_pack):
            picked = picked + jnp.dot(
                from_pad[:, b * cap : (b + 1) * cap],
                rows_all[b, :, n : n + 512],
                preferred_element_type=F32,
            )
        res[0:per_slot, n : n + 512] = picked
    res[per_slot:, :] = rows_all[me_p].astype(F32)
    gate[...] = jnp.broadcast_to(
        jax.nn.sigmoid(jnp.sum(res[...] * router[...], axis=1, keepdims=True)), gate.shape
    )

    wanted = pattern[pl.ds(me_c, 1), :]

    def merge(i, state):
        peak0, peak1, den0, den1 = state
        k = me_c - 1 - i
        o_copy(me_c, k).wait_recv()
        s_copy(me_c, k).wait_recv()
        hit = jnp.max(jnp.where(wanted == k, 1.0, 0.0), axis=1, keepdims=True)
        out = []
        for h, peak, den in ((0, peak0, den0), (1, peak1, den1)):
            rows = slice(h * HD, (h + 1) * HD)
            lse = jnp.where(hit > 0.5, st_in[k, h : h + 1, :], NEG)
            top = jnp.maximum(peak, lse)
            a = jnp.exp2(peak - top)
            b = jnp.exp2(lse - top)
            acc[rows, :] = acc[rows, :] * a + o_in[k, rows, :].astype(F32) * b
            out.append((top, den * a + b))
        return (out[0][0], out[1][0], out[0][1], out[1][1])

    ones = jnp.ones((1, routed), F32)
    _, _, den0, den1 = lax.fori_loop(
        0, me_c, merge, (st_in[me_c, 0:1, :], st_in[me_c, 1:2, :], ones, ones)
    )
    att[0:HD, :] = (acc[0:HD, :] / den0).astype(BF16)
    att[HD:, :] = (acc[HD:, :] / den1).astype(BF16)

    by_slot = lax.dot_general(
        slot_of[...], att[...], (((1,), (1,)), ((), ())), preferred_element_type=F32
    ).astype(BF16)
    by_owner = lax.dot_general(
        spread[...], att[...], (((1,), (1,)), ((), ())), preferred_element_type=F32
    ).astype(BF16)
    for d in range(n_pack):
        a_send[d, 0:per_slot, :] = by_slot[d * per_slot : (d + 1) * per_slot]
        a_send[d, per_slot:, :] = by_owner[d * cap : (d + 1) * cap]

    def a_copy(src, dst):
        return pltpu.make_async_remote_copy(
            src_ref=a_send.at[dst],
            dst_ref=a_in.at[src],
            send_sem=a_send_sem.at[dst],
            recv_sem=a_recv_sem.at[src],
            device_id=(me_c, dst),
            device_id_type=MESH,
        )

    def send_a(i, _):
        a_copy(me_p, lax.rem(me_p + i, n_pack)).start()
        return 0

    lax.fori_loop(1, n_pack, send_a, 0)
    a_in[me_p] = a_send[me_p]

    w_copy(2, sib, 0, tok, sib).wait_recv()
    w_copy(4, sib_left, 0, tok, sib).wait_recv()
    w_copy(6, sib_right, 0, tok, sib).wait_recv()
    w_copy(7, sib_far, 0, tok, sib).wait_recv()

    def take_a(i, _):
        peer = lax.rem(me_p + i, n_pack)
        a_copy(peer, me_p).wait_recv()
        return 0

    lax.fori_loop(1, n_pack, take_a, 0)

    present = lax.dot_general(
        pick, jnp.ones((cap, HD), BF16), (((0,), (0,)), ((), ())), preferred_element_type=F32
    )[:, 0:1]
    for n in range(0, width, 512):
        cols = slice(n, n + 512)
        mixed = 0.0
        for b in range(n_pack):
            mixed = mixed + jnp.dot(
                a_in[b], w_all[b * tok : (b + 1) * tok, cols], preferred_element_type=F32
            )
        updated = (res[:, cols] + gate[:, 0:1] * mixed).astype(BF16)
        packed[:, cols] = updated[0:per_slot]
        placed = lax.dot_general(
            pick, updated[per_slot:], (((0,), (0,)), ((), ())), preferred_element_type=F32
        )
        hidden_out[:, cols] = jnp.where(present > 0.5, placed.astype(BF16), hidden[:, cols])

    to_right.wait_send()
    to_left.wait_send()
    to_sib.wait_send()
    fwd_right.wait_send()
    fwd_left.wait_send()
    fwd_sib_left.wait_send()
    fwd_sib_right.wait_send()
    fwd_sib_far.wait_send()
    w_copy(0, me_p, 0, tok, right).wait_send()
    w_copy(1, me_p, 0, tok, left).wait_send()
    w_copy(2, me_p, 0, tok, sib).wait_send()
    w_copy(3, left, 0, w_half, right).wait_send()
    w_copy(4, left, 0, tok, sib).wait_send()
    w_copy(5, right, w_half, w_half, left).wait_send()
    w_copy(6, right, 0, tok, sib).wait_send()
    w_copy(7, far, 0, tok, sib).wait_send()

    def sent_q(k, _):
        q_copy(me_c, k).wait_send()
        return 0

    lax.fori_loop(0, me_c, sent_q, 0)

    def sent_o(c, _):
        o_copy(c, me_c).wait_send()
        s_copy(c, me_c).wait_send()
        return 0

    lax.fori_loop(me_c + 1, n_ctx, sent_o, 0)

    def sent_a(i, _):
        a_copy(me_p, lax.rem(me_p + i, n_pack)).wait_send()
        return 0

    lax.fori_loop(1, n_pack, sent_a, 0)


def local(n_ctx, n_pack, *args):
    hidden, keys, values, w_query, w_out, gain, router, routes, order, pattern = args
    tok, width = hidden.shape
    span, heads = keys.shape
    routed = routes.shape[1]
    cap = 3 * tok // 8
    per_slot = routed // n_pack
    both = per_slot + cap
    vmem = pl.BlockSpec(memory_space=pltpu.VMEM)
    dma = pltpu.SemaphoreType.DMA
    return pl.pallas_call(
        functools.partial(body, n_ctx, n_pack),
        out_shape=(
            jax.ShapeDtypeStruct((tok, width), BF16),
            jax.ShapeDtypeStruct((per_slot, width), BF16),
        ),
        in_specs=[vmem] * 11,
        out_specs=(vmem, vmem),
        scratch_shapes=[
            pltpu.VMEM((n_pack, cap, width), BF16),
            pltpu.VMEM((n_pack * cap, heads), BF16),
            pltpu.VMEM((n_pack * cap, routed), BF16),
            pltpu.VMEM((routed, routed), BF16),
            pltpu.VMEM((2, HD + 16, span), BF16),
            pltpu.VMEM((n_ctx, heads, routed), BF16),
            pltpu.VMEM((n_ctx, heads, routed), BF16),
            pltpu.VMEM((n_ctx, heads, routed), BF16),
            pltpu.VMEM((n_ctx, 8, routed), F32),
            pltpu.VMEM((n_ctx, 8, routed), F32),
            pltpu.VMEM((heads, routed), F32),
            pltpu.VMEM((heads, routed), BF16),
            pltpu.VMEM((n_pack * tok, width), BF16),
            pltpu.VMEM((n_pack, both, heads), BF16),
            pltpu.VMEM((n_pack, both, heads), BF16),
            pltpu.VMEM((both, width), F32),
            pltpu.VMEM((both, HD), F32),
            dma((8,)),
            dma((8,)),
            dma((8,)),
            dma((8,)),
            dma((n_ctx,)),
            dma((n_ctx,)),
            dma((n_ctx,)),
            dma((n_ctx,)),
            dma((n_ctx,)),
            dma((n_ctx,)),
            dma((n_pack,)),
            dma((n_pack,)),
            dma,
        ],
        compiler_params=pltpu.CompilerParams(
            collective_id=0, has_side_effects=True, vmem_limit_bytes=60 << 20
        ),
        name="routed_attention",
    )(
        hidden,
        keys,
        values,
        w_query,
        w_out,
        gain.reshape(1, width),
        router.reshape(1, width),
        routes,
        order,
        pattern,
        jnp.asarray(turn_table()),
    )


def solution(mesh):
    return jax.shard_map(
        functools.partial(local, mesh.shape["ctx"], mesh.shape["pack"]),
        mesh=mesh,
        in_specs=(
            P(("ctx", "pack"), None),
            P("ctx", "pack"),
            P("ctx", "pack"),
            P(None, "pack"),
            P("pack", None),
            P(),
            P(),
            P("ctx", None),
            P("ctx", None),
            P(),
        ),
        out_specs=(P(("ctx", "pack"), None), P(("ctx", "pack"), None)),
        check_vma=False,
    )
```

```python
import functools
import math

import jax
import jax.numpy as jnp
import numpy as np
from jax import lax
from jax.experimental import pallas as pl
from jax.experimental.pallas import tpu as pltpu
from jax.sharding import PartitionSpec as P

HD = 128
EPS = 1e-6
NEG = -1e30
F32 = jnp.float32
BF16 = jnp.bfloat16
MESH = pl.DeviceIdType.MESH
LOG2E = 1.4426950408889634


def turn_table():
    lane = np.arange(HD) % (HD // 2)
    turns = 10000.0 ** (-2.0 * lane / HD) / (2.0 * math.pi)
    table = np.zeros((8, HD), np.float32)
    table[0] = np.mod(turns * 128.0, 1.0)
    table[1] = turns
    table[2] = np.where(np.arange(HD) < HD // 2, -1.0, 1.0)
    return table


def cos_sin(pos, table):
    hi = jnp.floor(pos * (1.0 / 128.0))
    low = pos - hi * 128.0
    u = hi * table[0:1]
    u = u - jnp.floor(u) + low * table[1:2]
    u = u - jnp.floor(u + 0.5)
    x = u * math.pi
    y = x * x
    s = 0.0
    for n in (11, 9, 7, 5, 3):
        s = (s + (-1.0) ** ((n - 1) // 2) / math.factorial(n)) * y
    s = (s + 1.0) * x
    c = 0.0
    for n in (12, 10, 8, 6, 4, 2):
        c = (c + (-1.0) ** (n // 2) / math.factorial(n)) * y
    c = c + 1.0
    return 1.0 - 2.0 * s * s, 2.0 * s * c


def body(
    n_ctx,
    n_pack,
    hidden,
    keys,
    values,
    w_query,
    w_out,
    gain,
    router,
    routes,
    order,
    pattern,
    table,
    hidden_out,
    packed,
    rows_all,
    q_pad,
    spread,
    slot_of,
    kbuf,
    vbuf,
    q_buf,
    o_send,
    o_in,
    st_send,
    st_in,
    own,
    own_st,
    acc,
    att,
    w_all,
    a_send,
    a_in,
    res,
    gate,
    row_send,
    row_recv,
    wo_send,
    wo_recv,
    kv_send,
    kv_recv,
    q_send_sem,
    q_recv_sem,
    o_send_sem,
    o_recv_sem,
    s_send_sem,
    s_recv_sem,
    a_send_sem,
    a_recv_sem,
    loc_sem,
):
    me_c = lax.axis_index("ctx")
    me_p = lax.axis_index("pack")
    tok = hidden.shape[0]
    width = hidden.shape[1]
    span = keys.shape[0]
    routed = routes.shape[1]
    cap = rows_all.shape[1]
    per_slot = routed // n_pack
    half = cap // 2
    sib = me_p + 1 - 2 * lax.rem(me_p, 2)
    right = lax.rem(me_p + 2, n_pack)
    left = lax.rem(me_p + n_pack - 2, n_pack)
    far = lax.rem(me_p + 4, n_pack)
    sib_left = lax.rem(sib + n_pack - 2, n_pack)
    sib_right = lax.rem(sib + 2, n_pack)
    sib_far = lax.rem(sib + 4, n_pack)

    barrier = pltpu.get_barrier_semaphore()

    side = math.isqrt(n_ctx)
    y = me_c // side
    z = lax.rem(me_c, side)
    core = lax.rem(me_p, 2)

    def along_z(step):
        return y * side + lax.rem(z + step, side)

    def along_y(step):
        return lax.rem(y + step, side) * side + z

    def greet(c, p):
        pl.semaphore_signal(barrier, inc=1, device_id=(c, p), device_id_type=MESH)

    def greet_pack(i, _):
        greet(me_c, lax.rem(me_p + i, n_pack))
        return 0

    def greet_ctx(i, _):
        greet(along_y(i), me_p)
        greet(along_z(i), me_p)
        return 0

    lax.fori_loop(1, n_pack, greet_pack, 0)
    lax.fori_loop(1, side, greet_ctx, 0)

    rf = routes[...].astype(F32)
    lane_i = lax.broadcasted_iota(jnp.int32, (cap, routed), 1).astype(F32)
    sub_j = lax.broadcasted_iota(jnp.int32, (cap, routed), 0).astype(F32)

    def spread_of(block):
        low = (block * tok).astype(F32)
        start = jnp.sum(jnp.where(rf < low, 1.0, 0.0), axis=1, keepdims=True)
        end = jnp.sum(jnp.where(rf < low + tok, 1.0, 0.0), axis=1, keepdims=True)
        hit = jnp.logical_and(lane_i == sub_j + start, lane_i < end)
        pos = jnp.sum(jnp.where(hit, rf + 1.0, 0.0), axis=1, keepdims=True) - 1.0
        return jnp.where(hit, 1.0, 0.0), pos

    _, my_pos = spread_of(me_p)
    lane_t = lax.broadcasted_iota(jnp.int32, (cap, tok), 1).astype(F32)
    pick = jnp.where(lane_t == my_pos - (me_p * tok).astype(F32), 1.0, 0.0).astype(BF16)
    rows_all[me_p] = jnp.dot(pick, hidden[...], preferred_element_type=F32).astype(BF16)

    pl.semaphore_wait(barrier, 2 * (side - 1) + n_pack - 1)

    def row_copy(i, block, sub, peer):
        part = rows_all.at[block] if sub is None else rows_all.at[block, sub]
        return pltpu.make_async_remote_copy(
            src_ref=part,
            dst_ref=part,
            send_sem=row_send.at[i],
            recv_sem=row_recv.at[i],
            device_id=(me_c, peer),
            device_id_type=MESH,
        )

    first = pl.ds(0, half)
    second = pl.ds(half, half)
    to_right = row_copy(0, me_p, None, right)
    to_left = row_copy(1, me_p, None, left)
    to_sib = row_copy(2, me_p, None, sib)
    to_right.start()
    to_left.start()
    to_sib.start()

    key_ring = (along_y, along_z)
    key_at = (y, z)
    ahead = 1 + 2 * core
    behind = side - ahead

    def k_copy(h, j, i, step):
        part = kbuf.at[h, j]
        return pltpu.make_async_remote_copy(
            src_ref=part,
            dst_ref=part,
            send_sem=kv_send.at[h * 3 + i],
            recv_sem=kv_recv.at[h * side + j],
            device_id=(key_ring[h](step), me_p),
            device_id_type=MESH,
        )

    def v_copy(h, j, i, step):
        part = vbuf.at[h, j, 0:HD]
        return pltpu.make_async_remote_copy(
            src_ref=part,
            dst_ref=part,
            send_sem=kv_send.at[6 + h * 3 + i],
            recv_sem=kv_recv.at[2 * side + h * side + j],
            device_id=(key_ring[h](step), me_p),
            device_id_type=MESH,
        )

    for h in range(2):
        kbuf[h, key_at[h]] = keys[:, h * HD : (h + 1) * HD]
        k_copy(h, key_at[h], 0, 1).start()
        k_copy(h, key_at[h], 1, side - 1).start()
    for h in range(2):
        vbuf[h, key_at[h], 0:HD, :] = jnp.transpose(values[:, h * HD : (h + 1) * HD])
        v_copy(h, key_at[h], 0, 1).start()
        v_copy(h, key_at[h], 1, side - 1).start()
        for j in range(side):
            vbuf[h, j, HD:, :] = jnp.ones((vbuf.shape[2] - HD, span), BF16)

    def key_block(h, step):
        return lax.rem(key_at[h] + step, side)

    own_w = pltpu.make_async_copy(w_out, w_all.at[pl.ds(me_p * tok, tok)], loc_sem)
    own_w.start()

    gain_row = gain[...]
    trig = table[...]
    base = (me_c * span).astype(F32)

    for b in range(n_pack):
        hit, _ = spread_of(jnp.int32(b))
        spread[pl.ds(b * cap, cap), :] = hit.astype(BF16)
    order_col = jnp.transpose(jnp.broadcast_to(order[...].astype(F32), (HD, routed)))[:, 0:1]
    lane_s = lax.broadcasted_iota(jnp.int32, (routed, routed), 1).astype(F32)
    slot_of[...] = jnp.where(lane_s == order_col, 1.0, 0.0).astype(BF16)

    def project(block):
        rows = rows_all[block].astype(F32)
        mean_square = jnp.mean(rows * rows, axis=1, keepdims=True)
        normed = (rows * lax.rsqrt(mean_square + EPS) * gain_row).astype(BF16)
        proj = jnp.dot(normed, w_query[...], preferred_element_type=F32)
        _, pos = spread_of(block)
        cosine, sine = cos_sin(pos + base, trig)
        sine = sine * trig[2:3]
        start = pl.multiple_of(block * cap, cap)
        for h in range(2):
            part = proj[:, h * HD : (h + 1) * HD]
            turned = part * cosine + pltpu.roll(part, HD // 2, 1) * sine
            q_pad[pl.ds(start, cap), h * HD : (h + 1) * HD] = turned.astype(BF16)

    project(me_p)
    row_copy(0, left, None, right).wait_recv()
    fwd_right = row_copy(3, left, first, right)
    fwd_right.start()
    fwd_sib_left = row_copy(4, left, None, sib)
    fwd_sib_left.start()
    row_copy(1, right, None, left).wait_recv()
    fwd_left = row_copy(5, right, second, left)
    fwd_left.start()
    fwd_sib_right = row_copy(6, right, None, sib)
    fwd_sib_right.start()
    project(left)
    project(right)
    for h in range(2):
        k_copy(h, key_block(h, behind), 0, behind).wait_recv()
        k_copy(h, key_block(h, behind), 2, ahead).start()
    row_copy(2, sib, None, sib).wait_recv()
    project(sib)
    row_copy(4, sib_left, None, sib).wait_recv()
    project(sib_left)
    row_copy(6, sib_right, None, sib).wait_recv()
    project(sib_right)
    row_copy(3, far, first, right).wait_recv()
    row_copy(5, far, second, left).wait_recv()
    fwd_sib_far = row_copy(7, far, None, sib)
    fwd_sib_far.start()
    project(far)
    row_copy(7, sib_far, None, sib).wait_recv()
    project(sib_far)

    query = lax.dot_general(
        q_pad[...], spread[...], (((0,), (0,)), ((), ())), preferred_element_type=F32
    ).astype(BF16)
    q_buf[0, z] = query[0:HD]
    q_buf[1, y] = query[HD:]
    q_ring = (along_z, along_y)
    q_at = (z, y)

    def q_copy(h, src, step):
        return pltpu.make_async_remote_copy(
            src_ref=q_buf.at[h, src],
            dst_ref=q_buf.at[h, src],
            send_sem=q_send_sem.at[h * side + step],
            recv_sem=q_recv_sem.at[h * side + src],
            device_id=(q_ring[h](step), me_p),
            device_id_type=MESH,
        )

    for step in (1, 3, 2):
        for h in range(2):
            q_copy(h, q_at[h], step).start()
    for h in range(2):
        v_copy(h, key_block(h, behind), 0, behind).wait_recv()
        v_copy(h, key_block(h, behind), 2, ahead).start()

    w_half = tok // 2

    def w_copy(i, block, lo, size, peer):
        part = w_all.at[pl.ds(block * tok + lo, size)]
        return pltpu.make_async_remote_copy(
            src_ref=part,
            dst_ref=part,
            send_sem=wo_send.at[i],
            recv_sem=wo_recv.at[i],
            device_id=(me_c, peer),
            device_id_type=MESH,
        )

    own_w.wait()
    w_copy(0, me_p, 0, tok, right).start()
    w_copy(1, me_p, 0, tok, left).start()
    w_copy(2, me_p, 0, tok, sib).start()

    chunk = 512
    scale = LOG2E / math.sqrt(HD)
    key_iota = lax.broadcasted_iota(jnp.int32, (chunk, routed), 0).astype(F32)

    def attend(h, t, j, masked):
        query = q_buf[h, t]
        scores = []
        for i in range(span // chunk):
            s = jnp.dot(
                kbuf[h, j, i * chunk : (i + 1) * chunk, :], query, preferred_element_type=F32
            )
            if masked:
                s = jnp.where(key_iota <= rf - float(i * chunk), s, NEG)
            scores.append(s)
        peak = functools.reduce(
            jnp.maximum, [jnp.max(s, axis=0, keepdims=True) for s in scores]
        )
        peak = peak * scale
        out = 0.0
        for i, s in enumerate(scores):
            weights = jnp.exp2(s * scale - peak).astype(BF16)
            out = out + jnp.dot(
                vbuf[h, j, :, i * chunk : (i + 1) * chunk], weights, preferred_element_type=F32
            )
        total = out[HD : HD + 1]
        return out[:HD] / total, peak + jnp.log2(total)

    def less(a, b):
        return (b - a + side - 1) // side

    def same(a, b):
        return 1 - less(a, b) - less(b, a)

    def blend(h, one, two):
        return one + h * (two - one)

    def visit(h, t, peak, den):
        count = blend(h, y + less(z, t), side * less(y, t) + z * same(y, t))
        span_q = blend(h, y * side + t, t * side + z)
        wanted = pattern[pl.ds(span_q, 1), :]

        def one(j, state):
            peak, den = state
            span_k = blend(h, j * side + z, y * side + j)
            hit = jnp.max(jnp.where(wanted == span_k, 1.0, 0.0), axis=1, keepdims=True)
            out, lse = attend(h, t, j, False)
            lse = jnp.where(hit > 0.5, lse, NEG)
            top = jnp.maximum(peak, lse)
            a = jnp.exp2(peak - top)
            b = jnp.exp2(lse - top) * hit
            acc[...] = acc[...] * a + out * b
            return top, den * a + b

        return lax.fori_loop(0, count, one, (peak, den))

    def begin(h, _):
        out, lse = attend(h, blend(h, z, y), blend(h, y, z), True)
        own[h] = out
        own_st[h, 0:1, :] = lse
        return 0

    lax.fori_loop(0, 2, begin, 0)

    for h in range(2):
        k_copy(h, key_block(h, ahead), 0, ahead).wait_recv()
        v_copy(h, key_block(h, ahead), 0, ahead).wait_recv()
        k_copy(h, key_block(h, 2), 0, behind).wait_recv()
        v_copy(h, key_block(h, 2), 0, behind).wait_recv()

    ones = jnp.ones((1, routed), F32)

    def finish_own(h, _):
        acc[...] = own[h]
        peak, den = visit(h, blend(h, z, y), own_st[h, 0:1, :], ones)
        own[h] = acc[...]
        own_st[h, 0:1, :] = peak
        own_st[h, 1:2, :] = den
        return 0

    lax.fori_loop(0, 2, finish_own, 0)

    def o_copy(h, src, dst):
        return pltpu.make_async_remote_copy(
            src_ref=o_send.at[h, dst],
            dst_ref=o_in.at[h, src],
            send_sem=o_send_sem.at[h * side + dst],
            recv_sem=o_recv_sem.at[h * side + src],
            device_id=(blend(h, y * side + dst, dst * side + z), me_p),
            device_id_type=MESH,
        )

    def s_copy(h, src, dst):
        return pltpu.make_async_remote_copy(
            src_ref=st_send.at[h, dst],
            dst_ref=st_in.at[h, src],
            send_sem=s_send_sem.at[h * side + dst],
            recv_sem=s_recv_sem.at[h * side + src],
            device_id=(blend(h, y * side + dst, dst * side + z), me_p),
            device_id_type=MESH,
        )

    def serve(i, _):
        step = i // 2
        h = lax.rem(i, 2)
        at = blend(h, z, y)
        t = lax.rem(at + step, side)
        pltpu.make_async_remote_copy(
            src_ref=q_buf.at[h, t],
            dst_ref=q_buf.at[h, t],
            send_sem=q_send_sem.at[h * side + step],
            recv_sem=q_recv_sem.at[h * side + t],
            device_id=(blend(h, along_z(step), along_y(step)), me_p),
            device_id_type=MESH,
        ).wait_recv()
        acc[...] = jnp.zeros((HD, routed), F32)
        peak, den = visit(h, t, ones * NEG, ones * 0.0)
        o_send[h, t] = (acc[...] / jnp.where(den > 0.0, den, 1.0)).astype(BF16)
        st_send[h, t] = jnp.broadcast_to(
            jnp.where(den > 0.0, peak + jnp.log2(den), NEG), (8, routed)
        )
        o_copy(h, at, t).start()
        s_copy(h, at, t).start()
        return 0

    lax.fori_loop(2, 6, serve, 0)

    w_copy(0, left, 0, tok, right).wait_recv()
    w_copy(3, left, 0, w_half, right).start()
    w_copy(4, left, 0, tok, sib).start()
    w_copy(1, right, 0, tok, left).wait_recv()
    w_copy(5, right, w_half, w_half, left).start()
    w_copy(6, right, 0, tok, sib).start()

    lax.fori_loop(6, 2 * side, serve, 0)

    w_copy(3, far, 0, w_half, right).wait_recv()
    w_copy(5, far, w_half, w_half, left).wait_recv()
    w_copy(7, far, 0, tok, sib).start()

    slot_rows = pl.ds(pl.multiple_of(me_p * per_slot, per_slot), per_slot)
    from_pad = lax.dot_general(
        slot_of[slot_rows, :], spread[...], (((1,), (1,)), ((), ())), preferred_element_type=F32
    ).astype(BF16)
    flat = n_pack * cap
    for n in range(0, width, 512):
        picked = 0.0
        for b in range(n_pack):
            picked = picked + jnp.dot(
                from_pad[:, b * cap : (b + 1) * cap],
                rows_all[b, :, n : n + 512],
                preferred_element_type=F32,
            )
        res[0:per_slot, n : n + 512] = picked
    res[per_slot:, :] = rows_all[me_p].astype(F32)
    gate[...] = jnp.broadcast_to(
        jax.nn.sigmoid(jnp.sum(res[...] * router[...], axis=1, keepdims=True)), gate.shape
    )

    for h in range(2):
        peak, den = own_st[h, 0:1, :], own_st[h, 1:2, :]
        total = own[h]
        for step in (3, 2, 1):
            src = lax.rem(q_at[h] + step, side)
            o_copy(h, src, q_at[h]).wait_recv()
            s_copy(h, src, q_at[h]).wait_recv()
            lse = st_in[h, src, 0:1, :]
            top = jnp.maximum(peak, lse)
            a = jnp.exp2(peak - top)
            b = jnp.exp2(lse - top)
            total = total * a + o_in[h, src].astype(F32) * b
            peak, den = top, den * a + b
        att[h * HD : (h + 1) * HD, :] = (total / den).astype(BF16)

    by_slot = lax.dot_general(
        slot_of[...], att[...], (((1,), (1,)), ((), ())), preferred_element_type=F32
    ).astype(BF16)
    by_owner = lax.dot_general(
        spread[...], att[...], (((1,), (1,)), ((), ())), preferred_element_type=F32
    ).astype(BF16)
    for d in range(n_pack):
        a_send[d, 0:per_slot, :] = by_slot[d * per_slot : (d + 1) * per_slot]
        a_send[d, per_slot:, :] = by_owner[d * cap : (d + 1) * cap]

    def a_copy(src, dst):
        return pltpu.make_async_remote_copy(
            src_ref=a_send.at[dst],
            dst_ref=a_in.at[src],
            send_sem=a_send_sem.at[dst],
            recv_sem=a_recv_sem.at[src],
            device_id=(me_c, dst),
            device_id_type=MESH,
        )

    def send_a(i, _):
        a_copy(me_p, lax.rem(me_p + i, n_pack)).start()
        return 0

    lax.fori_loop(1, n_pack, send_a, 0)
    a_in[me_p] = a_send[me_p]

    w_copy(2, sib, 0, tok, sib).wait_recv()
    w_copy(4, sib_left, 0, tok, sib).wait_recv()
    w_copy(6, sib_right, 0, tok, sib).wait_recv()
    w_copy(7, sib_far, 0, tok, sib).wait_recv()

    def take_a(i, _):
        peer = lax.rem(me_p + i, n_pack)
        a_copy(peer, me_p).wait_recv()
        return 0

    lax.fori_loop(1, n_pack, take_a, 0)

    present = lax.dot_general(
        pick, jnp.ones((cap, HD), BF16), (((0,), (0,)), ((), ())), preferred_element_type=F32
    )[:, 0:1]
    for n in range(0, width, 512):
        cols = slice(n, n + 512)
        mixed = 0.0
        for b in range(n_pack):
            mixed = mixed + jnp.dot(
                a_in[b], w_all[b * tok : (b + 1) * tok, cols], preferred_element_type=F32
            )
        updated = (res[:, cols] + gate[:, 0:1] * mixed).astype(BF16)
        packed[:, cols] = updated[0:per_slot]
        placed = lax.dot_general(
            pick, updated[per_slot:], (((0,), (0,)), ((), ())), preferred_element_type=F32
        )
        hidden_out[:, cols] = jnp.where(present > 0.5, placed.astype(BF16), hidden[:, cols])

    to_right.wait_send()
    to_left.wait_send()
    to_sib.wait_send()
    fwd_right.wait_send()
    fwd_left.wait_send()
    fwd_sib_left.wait_send()
    fwd_sib_right.wait_send()
    fwd_sib_far.wait_send()
    w_copy(0, me_p, 0, tok, right).wait_send()
    w_copy(1, me_p, 0, tok, left).wait_send()
    w_copy(2, me_p, 0, tok, sib).wait_send()
    w_copy(3, left, 0, w_half, right).wait_send()
    w_copy(4, left, 0, tok, sib).wait_send()
    w_copy(5, right, w_half, w_half, left).wait_send()
    w_copy(6, right, 0, tok, sib).wait_send()
    w_copy(7, far, 0, tok, sib).wait_send()

    for h in range(2):
        k_copy(h, key_at[h], 0, 1).wait_send()
        k_copy(h, key_at[h], 1, side - 1).wait_send()
        k_copy(h, key_block(h, behind), 2, ahead).wait_send()
        v_copy(h, key_at[h], 0, 1).wait_send()
        v_copy(h, key_at[h], 1, side - 1).wait_send()
        v_copy(h, key_block(h, behind), 2, ahead).wait_send()
        for step in (1, 2, 3):
            dst = lax.rem(q_at[h] + step, side)
            q_copy(h, q_at[h], step).wait_send()
            o_copy(h, q_at[h], dst).wait_send()
            s_copy(h, q_at[h], dst).wait_send()

    def sent_a(i, _):
        a_copy(me_p, lax.rem(me_p + i, n_pack)).wait_send()
        return 0

    lax.fori_loop(1, n_pack, sent_a, 0)


def local(n_ctx, n_pack, *args):
    hidden, keys, values, w_query, w_out, gain, router, routes, order, pattern = args
    tok, width = hidden.shape
    span, heads = keys.shape
    routed = routes.shape[1]
    cap = 3 * tok // 8
    per_slot = routed // n_pack
    both = per_slot + cap
    side = math.isqrt(n_ctx)
    vmem = pl.BlockSpec(memory_space=pltpu.VMEM)
    dma = pltpu.SemaphoreType.DMA
    return pl.pallas_call(
        functools.partial(body, n_ctx, n_pack),
        out_shape=(
            jax.ShapeDtypeStruct((tok, width), BF16),
            jax.ShapeDtypeStruct((per_slot, width), BF16),
        ),
        in_specs=[vmem] * 11,
        out_specs=(vmem, vmem),
        scratch_shapes=[
            pltpu.VMEM((n_pack, cap, width), BF16),
            pltpu.VMEM((n_pack * cap, heads), BF16),
            pltpu.VMEM((n_pack * cap, routed), BF16),
            pltpu.VMEM((routed, routed), BF16),
            pltpu.VMEM((2, side, span, HD), BF16),
            pltpu.VMEM((2, side, HD + 16, span), BF16),
            pltpu.VMEM((2, side, HD, routed), BF16),
            pltpu.VMEM((2, side, HD, routed), BF16),
            pltpu.VMEM((2, side, HD, routed), BF16),
            pltpu.VMEM((2, side, 8, routed), F32),
            pltpu.VMEM((2, side, 8, routed), F32),
            pltpu.VMEM((2, HD, routed), F32),
            pltpu.VMEM((2, 8, routed), F32),
            pltpu.VMEM((HD, routed), F32),
            pltpu.VMEM((heads, routed), BF16),
            pltpu.VMEM((n_pack * tok, width), BF16),
            pltpu.VMEM((n_pack, both, heads), BF16),
            pltpu.VMEM((n_pack, both, heads), BF16),
            pltpu.VMEM((both, width), F32),
            pltpu.VMEM((both, HD), F32),
            dma((8,)),
            dma((8,)),
            dma((8,)),
            dma((8,)),
            dma((12,)),
            dma((4 * side,)),
            dma((2 * side,)),
            dma((2 * side,)),
            dma((2 * side,)),
            dma((2 * side,)),
            dma((2 * side,)),
            dma((2 * side,)),
            dma((n_pack,)),
            dma((n_pack,)),
            dma,
        ],
        compiler_params=pltpu.CompilerParams(
            collective_id=0, has_side_effects=True, vmem_limit_bytes=60 << 20
        ),
        name="routed_attention",
    )(
        hidden,
        keys,
        values,
        w_query,
        w_out,
        gain.reshape(1, width),
        router.reshape(1, width),
        routes,
        order,
        pattern,
        jnp.asarray(turn_table()),
    )


def solution(mesh):
    return jax.shard_map(
        functools.partial(local, mesh.shape["ctx"], mesh.shape["pack"]),
        mesh=mesh,
        in_specs=(
            P(("ctx", "pack"), None),
            P("ctx", "pack"),
            P("ctx", "pack"),
            P(None, "pack"),
            P("pack", None),
            P(),
            P(),
            P("ctx", None),
            P("ctx", None),
            P(),
        ),
        out_specs=(P(("ctx", "pack"), None), P(("ctx", "pack"), None)),
        check_vma=False,
    )
```

```python
import functools
import math

import jax
import jax.numpy as jnp
import numpy as np
from jax import lax
from jax.experimental import pallas as pl
from jax.experimental.pallas import tpu as pltpu
from jax.sharding import PartitionSpec as P

HD = 128
EPS = 1e-6
NEG = -1e30
F32 = jnp.float32
BF16 = jnp.bfloat16
MESH = pl.DeviceIdType.MESH
LOG2E = 1.4426950408889634


def turn_table():
    lane = np.arange(HD) % (HD // 2)
    turns = 10000.0 ** (-2.0 * lane / HD) / (2.0 * math.pi)
    table = np.zeros((8, HD), np.float32)
    table[0] = np.mod(turns * 128.0, 1.0)
    table[1] = turns
    table[2] = np.where(np.arange(HD) < HD // 2, -1.0, 1.0)
    return table


def cos_sin(pos, table):
    hi = jnp.floor(pos * (1.0 / 128.0))
    low = pos - hi * 128.0
    u = hi * table[0:1]
    u = u - jnp.floor(u) + low * table[1:2]
    u = u - jnp.floor(u + 0.5)
    x = u * math.pi
    y = x * x
    s = 0.0
    for n in (11, 9, 7, 5, 3):
        s = (s + (-1.0) ** ((n - 1) // 2) / math.factorial(n)) * y
    s = (s + 1.0) * x
    c = 0.0
    for n in (12, 10, 8, 6, 4, 2):
        c = (c + (-1.0) ** (n // 2) / math.factorial(n)) * y
    c = c + 1.0
    return 1.0 - 2.0 * s * s, 2.0 * s * c


def body(
    n_ctx,
    n_pack,
    hidden,
    keys,
    values,
    w_query,
    w_out,
    gain,
    router,
    routes,
    order,
    pattern,
    table,
    hidden_out,
    packed,
    rows_all,
    q_pad,
    spread,
    gather,
    slot_of,
    pos_col,
    kbuf,
    vbuf,
    q_buf,
    o_send,
    o_in,
    st_send,
    st_in,
    acc,
    state,
    att,
    w_all,
    a_send,
    a_in,
    res,
    gate,
    row_send,
    row_recv,
    wo_send,
    wo_recv,
    kv_send,
    kv_recv,
    q_send_sem,
    q_recv_sem,
    o_send_sem,
    o_recv_sem,
    s_send_sem,
    s_recv_sem,
    a_send_sem,
    a_recv_sem,
    loc_sem,
):
    me_c = lax.axis_index("ctx")
    me_p = lax.axis_index("pack")
    tok = hidden.shape[0]
    width = hidden.shape[1]
    span = keys.shape[0]
    routed = routes.shape[1]
    cap = rows_all.shape[1]
    per_slot = routed // n_pack
    half = cap // 2
    sib = me_p + 1 - 2 * lax.rem(me_p, 2)
    right = lax.rem(me_p + 2, n_pack)
    left = lax.rem(me_p + n_pack - 2, n_pack)
    far = lax.rem(me_p + 4, n_pack)
    sib_left = lax.rem(sib + n_pack - 2, n_pack)
    sib_right = lax.rem(sib + 2, n_pack)
    sib_far = lax.rem(sib + 4, n_pack)

    barrier = pltpu.get_barrier_semaphore()

    side = math.isqrt(n_ctx)
    y = me_c // side
    z = lax.rem(me_c, side)
    core = lax.rem(me_p, 2)

    def along_z(step):
        return y * side + lax.rem(z + step, side)

    def along_y(step):
        return lax.rem(y + step, side) * side + z

    def greet(c, p):
        pl.semaphore_signal(barrier, inc=1, device_id=(c, p), device_id_type=MESH)

    def greet_pack(i, _):
        greet(me_c, lax.rem(me_p + i, n_pack))
        return 0

    def greet_ctx(i, _):
        greet(along_y(i), me_p)
        greet(along_z(i), me_p)
        return 0

    lax.fori_loop(1, n_pack, greet_pack, 0)
    lax.fori_loop(1, side, greet_ctx, 0)

    rf = routes[...].astype(F32)
    lane_i = lax.broadcasted_iota(jnp.int32, (cap, routed), 1).astype(F32)
    sub_j = lax.broadcasted_iota(jnp.int32, (cap, routed), 0).astype(F32)

    def spread_of(block):
        low = (block * tok).astype(F32)
        start = jnp.sum(jnp.where(rf < low, 1.0, 0.0), axis=1, keepdims=True)
        end = jnp.sum(jnp.where(rf < low + tok, 1.0, 0.0), axis=1, keepdims=True)
        hit = jnp.logical_and(lane_i == sub_j + start, lane_i < end)
        pos = jnp.sum(jnp.where(hit, rf + 1.0, 0.0), axis=1, keepdims=True) - 1.0
        return jnp.where(hit, 1.0, 0.0), pos

    _, my_pos = spread_of(me_p)
    lane_t = lax.broadcasted_iota(jnp.int32, (cap, tok), 1).astype(F32)
    pick = jnp.where(lane_t == my_pos - (me_p * tok).astype(F32), 1.0, 0.0).astype(BF16)
    rows_all[me_p] = jnp.dot(pick, hidden[...], preferred_element_type=F32).astype(BF16)

    pl.semaphore_wait(barrier, 2 * (side - 1) + n_pack - 1)

    def row_copy(i, block, sub, peer):
        part = rows_all.at[block] if sub is None else rows_all.at[block, sub]
        return pltpu.make_async_remote_copy(
            src_ref=part,
            dst_ref=part,
            send_sem=row_send.at[i],
            recv_sem=row_recv.at[i],
            device_id=(me_c, peer),
            device_id_type=MESH,
        )

    first = pl.ds(0, half)
    second = pl.ds(half, half)
    to_right = row_copy(0, me_p, None, right)
    to_left = row_copy(1, me_p, None, left)
    to_sib = row_copy(2, me_p, None, sib)
    to_right.start()
    to_left.start()
    to_sib.start()

    key_ring = (along_y, along_z)
    key_at = (y, z)
    ahead = 1 + 2 * core
    behind = side - ahead

    def k_copy(h, j, i, step):
        part = kbuf.at[h, j]
        return pltpu.make_async_remote_copy(
            src_ref=part,
            dst_ref=part,
            send_sem=kv_send.at[h * 3 + i],
            recv_sem=kv_recv.at[h * side + j],
            device_id=(key_ring[h](step), me_p),
            device_id_type=MESH,
        )

    def v_copy(h, j, i, step):
        part = vbuf.at[h, j, :, pl.ds(0, HD)]
        return pltpu.make_async_remote_copy(
            src_ref=part,
            dst_ref=part,
            send_sem=kv_send.at[6 + h * 3 + i],
            recv_sem=kv_recv.at[2 * side + h * side + j],
            device_id=(key_ring[h](step), me_p),
            device_id_type=MESH,
        )

    for h in range(2):
        kbuf[h, key_at[h]] = keys[:, h * HD : (h + 1) * HD]
        k_copy(h, key_at[h], 0, 1).start()
        k_copy(h, key_at[h], 1, side - 1).start()
    for h in range(2):
        vbuf[h, key_at[h], :, 0:HD] = values[:, h * HD : (h + 1) * HD]
        v_copy(h, key_at[h], 0, 1).start()
        v_copy(h, key_at[h], 1, side - 1).start()
    for h in range(2):
        for j in range(side):
            vbuf[h, j, :, HD:] = jnp.ones((span, HD), BF16)

    def key_block(h, step):
        return lax.rem(key_at[h] + step, side)

    own_w = pltpu.make_async_copy(w_out, w_all.at[pl.ds(me_p * tok, tok)], loc_sem)
    own_w.start()

    gain_row = gain[...]
    trig = table[...]
    base = (me_c * span).astype(F32)

    for b in range(n_pack):
        hit, _ = spread_of(jnp.int32(b))
        spread[pl.ds(b * cap, cap), :] = hit.astype(BF16)
    flat = n_pack * cap
    lane_f = lax.broadcasted_iota(jnp.int32, (1, flat), 1).astype(F32)
    start_f = lane_f * 0.0
    end_f = lane_f * 0.0
    for b in range(n_pack):
        inside = jnp.logical_and(lane_f >= b * cap, lane_f < (b + 1) * cap)
        start = jnp.sum(jnp.where(rf < b * tok, 1.0, 0.0), axis=1, keepdims=True)
        end = jnp.sum(jnp.where(rf < (b + 1) * tok, 1.0, 0.0), axis=1, keepdims=True)
        start_f = jnp.where(inside, start + lane_f - b * cap, start_f)
        end_f = jnp.where(inside, end, end_f)
    row_i = lax.broadcasted_iota(jnp.int32, (routed, flat), 0).astype(F32)
    gather[...] = jnp.where(
        jnp.logical_and(row_i == start_f, row_i < end_f), 1.0, 0.0
    ).astype(BF16)
    pos_col[...] = jnp.transpose(jnp.broadcast_to(rf, (HD, routed)))
    order_col = jnp.transpose(jnp.broadcast_to(order[...].astype(F32), (HD, routed)))[:, 0:1]
    lane_s = lax.broadcasted_iota(jnp.int32, (routed, routed), 1).astype(F32)
    slot_of[...] = jnp.where(lane_s == order_col, 1.0, 0.0).astype(BF16)

    def project(block):
        rows = rows_all[block].astype(F32)
        mean_square = jnp.mean(rows * rows, axis=1, keepdims=True)
        normed = (rows * lax.rsqrt(mean_square + EPS) * gain_row).astype(BF16)
        proj = jnp.dot(normed, w_query[...], preferred_element_type=F32)
        _, pos = spread_of(block)
        cosine, sine = cos_sin(pos + base, trig)
        sine = sine * trig[2:3]
        start = pl.multiple_of(block * cap, cap)
        for h in range(2):
            part = proj[:, h * HD : (h + 1) * HD]
            turned = part * cosine + pltpu.roll(part, HD // 2, 1) * sine
            q_pad[pl.ds(start, cap), h * HD : (h + 1) * HD] = turned.astype(BF16)

    project(me_p)
    row_copy(0, left, None, right).wait_recv()
    fwd_right = row_copy(3, left, first, right)
    fwd_right.start()
    fwd_sib_left = row_copy(4, left, None, sib)
    fwd_sib_left.start()
    row_copy(1, right, None, left).wait_recv()
    fwd_left = row_copy(5, right, second, left)
    fwd_left.start()
    fwd_sib_right = row_copy(6, right, None, sib)
    fwd_sib_right.start()
    project(left)
    project(right)
    for h in range(2):
        k_copy(h, key_block(h, behind), 0, behind).wait_recv()
        k_copy(h, key_block(h, behind), 2, ahead).start()
    row_copy(2, sib, None, sib).wait_recv()
    project(sib)
    row_copy(4, sib_left, None, sib).wait_recv()
    project(sib_left)
    row_copy(6, sib_right, None, sib).wait_recv()
    project(sib_right)
    row_copy(3, far, first, right).wait_recv()
    row_copy(5, far, second, left).wait_recv()
    fwd_sib_far = row_copy(7, far, None, sib)
    fwd_sib_far.start()
    w_half = tok // 2

    def w_copy(i, block, lo, size, peer):
        part = w_all.at[pl.ds(block * tok + lo, size)]
        return pltpu.make_async_remote_copy(
            src_ref=part,
            dst_ref=part,
            send_sem=wo_send.at[i],
            recv_sem=wo_recv.at[i],
            device_id=(me_c, peer),
            device_id_type=MESH,
        )

    own_w.wait()
    w_copy(0, me_p, 0, tok, right).start()
    w_copy(1, me_p, 0, tok, left).start()
    w_copy(2, me_p, 0, tok, sib).start()

    project(far)
    row_copy(7, sib_far, None, sib).wait_recv()
    project(sib_far)

    query = jnp.dot(gather[...], q_pad[...], preferred_element_type=F32).astype(BF16)
    q_buf[0, z] = query[:, 0:HD]
    q_buf[1, y] = query[:, HD:]
    q_ring = (along_z, along_y)
    q_at = (z, y)

    def q_copy(h, src, step):
        return pltpu.make_async_remote_copy(
            src_ref=q_buf.at[h, src],
            dst_ref=q_buf.at[h, src],
            send_sem=q_send_sem.at[h * side + step],
            recv_sem=q_recv_sem.at[h * side + src],
            device_id=(q_ring[h](step), me_p),
            device_id_type=MESH,
        )

    for step in (1, 3, 2):
        for h in range(2):
            q_copy(h, q_at[h], step).start()
    for h in range(2):
        v_copy(h, key_block(h, behind), 0, behind).wait_recv()
        v_copy(h, key_block(h, behind), 2, ahead).start()

    chunk = 512
    tile = 256
    scale = LOG2E / math.sqrt(HD)

    def less(a, b):
        return (b - a + side - 1) // side

    def same(a, b):
        return 1 - less(a, b) - less(b, a)

    def blend(h, one, two):
        return one + h * (two - one)

    def step_in(h, t, j, own):
        if own:
            lane_k = lax.broadcasted_iota(jnp.int32, (tile, chunk), 1).astype(F32)
        else:
            span_q = blend(h, y * side + t, t * side + z)
            span_k = blend(h, j * side + z, y * side + j)
            wanted = pattern[pl.ds(span_q, 1), :]
            hit = jnp.max(jnp.where(wanted == span_k, 1.0, 0.0), axis=1, keepdims=True)

        def score(r, i):
            s = lax.dot_general(
                q_buf[h, t, r : r + tile, :],
                kbuf[h, j, i : i + chunk, :],
                (((1,), (1,)), ((), ())),
                preferred_element_type=F32,
            )
            if own:
                s = jnp.where(lane_k <= pos_col[r : r + tile, 0:1] - float(i), s, NEG)
            return s

        scores = [score(0, i) for i in range(0, span, chunk)]
        for r in range(0, routed, tile):
            peak = functools.reduce(
                jnp.maximum, [jnp.max(s, axis=1, keepdims=True) for s in scores]
            )
            peak = peak * scale
            later = []
            out = 0.0
            for n, i in enumerate(range(0, span, chunk)):
                if r + tile < routed:
                    later.append(score(r + tile, i))
                weights = jnp.exp2(scores[n] * scale - peak).astype(BF16)
                out = out + jnp.dot(
                    weights, vbuf[h, j, i : i + chunk, :], preferred_element_type=F32
                )
            rows = slice(r, r + tile)
            if own:
                acc[h, t, rows, :] = out[:, 0:HD]
                state[0, h, t, rows, :] = jnp.broadcast_to(peak, (tile, HD))
                state[1, h, t, rows, :] = out[:, HD:]
            else:
                peak = jnp.where(hit > 0.5, peak, NEG)
                former = state[0, h, t, rows, :]
                top = jnp.maximum(former, peak)
                a = jnp.exp2(former - top)
                b = jnp.exp2(peak - top) * hit
                acc[h, t, rows, :] = acc[h, t, rows, :] * a + out[:, 0:HD] * b
                state[0, h, t, rows, :] = top
                state[1, h, t, rows, :] = state[1, h, t, rows, :] * a + out[:, HD:] * b
            scores = later

    def slot(h, step):
        return lax.rem(blend(h, z, y) + step, side)

    def block(h, step):
        return lax.rem(blend(h, y, z) + step, side)

    def sees(h, t, j):
        by_row = less(j, y) + same(j, y) * less(z, t)
        by_col = less(y, t) + same(y, t) * less(j, z)
        return blend(h, by_row, by_col)

    def begin(h, _):
        for step in range(1, side):
            t = slot(h, step)
            acc[h, t] = jnp.zeros((routed, HD), F32)
            state[0, h, t] = jnp.full((routed, HD), NEG, F32)
            state[1, h, t] = jnp.zeros((routed, HD), F32)
        step_in(h, slot(h, 0), block(h, 0), True)
        return 0

    lax.fori_loop(0, 2, begin, 0)

    def own_block(i, _):
        step = 1 + i // 2
        h = lax.rem(i, 2)
        t = slot(h, step)
        pltpu.make_async_remote_copy(
            src_ref=q_buf.at[h, t],
            dst_ref=q_buf.at[h, t],
            send_sem=q_send_sem.at[h * side + step],
            recv_sem=q_recv_sem.at[h * side + t],
            device_id=(blend(h, along_z(step), along_y(step)), me_p),
            device_id_type=MESH,
        ).wait_recv()
        j = block(h, 0)

        @pl.when(sees(h, t, j) == 1)
        def _():
            step_in(h, t, j, False)

        return 0

    lax.fori_loop(0, 2 * (side - 1), own_block, 0)

    for h in range(2):
        k_copy(h, key_block(h, ahead), 0, ahead).wait_recv()
        v_copy(h, key_block(h, ahead), 0, ahead).wait_recv()

    def near_blocks(i, _):
        h = lax.rem(i, 2)
        t = slot(h, lax.rem(i // 2, side))
        j = block(h, 1 + 2 * (i // (2 * side)))

        @pl.when(sees(h, t, j) == 1)
        def _():
            step_in(h, t, j, False)

        return 0

    lax.fori_loop(0, 4 * side, near_blocks, 0)

    w_copy(0, left, 0, tok, right).wait_recv()
    w_copy(3, left, 0, w_half, right).start()
    w_copy(4, left, 0, tok, sib).start()
    w_copy(1, right, 0, tok, left).wait_recv()
    w_copy(5, right, w_half, w_half, left).start()
    w_copy(6, right, 0, tok, sib).start()

    for h in range(2):
        k_copy(h, key_block(h, 2), 0, behind).wait_recv()
        v_copy(h, key_block(h, 2), 0, behind).wait_recv()

    def o_copy(h, src, dst):
        return pltpu.make_async_remote_copy(
            src_ref=o_send.at[h, dst],
            dst_ref=o_in.at[h, src],
            send_sem=o_send_sem.at[h * side + dst],
            recv_sem=o_recv_sem.at[h * side + src],
            device_id=(blend(h, y * side + dst, dst * side + z), me_p),
            device_id_type=MESH,
        )

    def s_copy(h, src, dst):
        return pltpu.make_async_remote_copy(
            src_ref=st_send.at[h, dst],
            dst_ref=st_in.at[h, src],
            send_sem=s_send_sem.at[h * side + dst],
            recv_sem=s_recv_sem.at[h * side + src],
            device_id=(blend(h, y * side + dst, dst * side + z), me_p),
            device_id_type=MESH,
        )

    def far_block(i, _):
        h = lax.rem(i, 2)
        turn = i // 2
        step = lax.rem(turn + 1, side - 1) + 1
        at = slot(h, 0)
        t = slot(h, step)
        j = block(h, 2)

        @pl.when(sees(h, t, j) == 1)
        def _():
            step_in(h, t, j, False)

        den = state[1, h, t]
        o_send[h, t] = (acc[h, t] / jnp.where(den > 0.0, den, 1.0)).astype(BF16)
        lse = jnp.where(den > 0.0, state[0, h, t] + jnp.log2(den), NEG)
        st_send[h, t] = jnp.transpose(lse)[0:8]
        o_copy(h, at, t).start()
        s_copy(h, at, t).start()
        return 0

    lax.fori_loop(0, 2 * (side - 1), far_block, 0)

    def far_own(h, _):
        t = slot(h, 0)
        j = block(h, 2)

        @pl.when(sees(h, t, j) == 1)
        def _():
            step_in(h, t, j, False)

        return 0

    lax.fori_loop(0, 2, far_own, 0)

    w_copy(3, far, 0, w_half, right).wait_recv()
    w_copy(5, far, w_half, w_half, left).wait_recv()
    w_copy(7, far, 0, tok, sib).start()

    slot_rows = pl.ds(pl.multiple_of(me_p * per_slot, per_slot), per_slot)
    from_pad = jnp.dot(
        slot_of[slot_rows, :], gather[...], preferred_element_type=F32
    ).astype(BF16)
    for n in range(0, width, 512):
        picked = 0.0
        for b in range(n_pack):
            picked = picked + jnp.dot(
                from_pad[:, b * cap : (b + 1) * cap],
                rows_all[b, :, n : n + 512],
                preferred_element_type=F32,
            )
        res[0:per_slot, n : n + 512] = picked
    res[per_slot:, :] = rows_all[me_p].astype(F32)
    gate[...] = jnp.broadcast_to(
        jax.nn.sigmoid(jnp.sum(res[...] * router[...], axis=1, keepdims=True)), gate.shape
    )

    for h in range(2):
        peak, den = state[0, h, q_at[h]], state[1, h, q_at[h]]
        total = acc[h, q_at[h]]
        for step in (2, 1, 3):
            src = lax.rem(q_at[h] + step, side)
            o_copy(h, src, q_at[h]).wait_recv()
            s_copy(h, src, q_at[h]).wait_recv()
            lse = jnp.transpose(jnp.broadcast_to(st_in[h, src, 0:1, :], (HD, routed)))
            top = jnp.maximum(peak, lse)
            a = jnp.exp2(peak - top)
            b = jnp.exp2(lse - top)
            total = total * a + o_in[h, src].astype(F32) * b
            peak, den = top, den * a + b
        att[:, h * HD : (h + 1) * HD] = (total / den).astype(BF16)

    by_slot = jnp.dot(slot_of[...], att[...], preferred_element_type=F32).astype(BF16)
    by_owner = jnp.dot(spread[...], att[...], preferred_element_type=F32).astype(BF16)
    for d in range(n_pack):
        a_send[d, 0:per_slot, :] = by_slot[d * per_slot : (d + 1) * per_slot]
        a_send[d, per_slot:, :] = by_owner[d * cap : (d + 1) * cap]

    def a_copy(src, dst):
        return pltpu.make_async_remote_copy(
            src_ref=a_send.at[dst],
            dst_ref=a_in.at[src],
            send_sem=a_send_sem.at[dst],
            recv_sem=a_recv_sem.at[src],
            device_id=(me_c, dst),
            device_id_type=MESH,
        )

    def send_a(i, _):
        a_copy(me_p, lax.rem(me_p + i, n_pack)).start()
        return 0

    lax.fori_loop(1, n_pack, send_a, 0)
    a_in[me_p] = a_send[me_p]

    w_copy(2, sib, 0, tok, sib).wait_recv()
    w_copy(4, sib_left, 0, tok, sib).wait_recv()
    w_copy(6, sib_right, 0, tok, sib).wait_recv()
    w_copy(7, sib_far, 0, tok, sib).wait_recv()

    def take_a(i, _):
        peer = lax.rem(me_p + i, n_pack)
        a_copy(peer, me_p).wait_recv()
        return 0

    lax.fori_loop(1, n_pack, take_a, 0)

    present = lax.dot_general(
        pick, jnp.ones((cap, HD), BF16), (((0,), (0,)), ((), ())), preferred_element_type=F32
    )[:, 0:1]
    for n in range(0, width, 512):
        cols = slice(n, n + 512)
        mixed = 0.0
        for b in range(n_pack):
            mixed = mixed + jnp.dot(
                a_in[b], w_all[b * tok : (b + 1) * tok, cols], preferred_element_type=F32
            )
        updated = (res[:, cols] + gate[:, 0:1] * mixed).astype(BF16)
        packed[:, cols] = updated[0:per_slot]
        placed = lax.dot_general(
            pick, updated[per_slot:], (((0,), (0,)), ((), ())), preferred_element_type=F32
        )
        hidden_out[:, cols] = jnp.where(present > 0.5, placed.astype(BF16), hidden[:, cols])

    to_right.wait_send()
    to_left.wait_send()
    to_sib.wait_send()
    fwd_right.wait_send()
    fwd_left.wait_send()
    fwd_sib_left.wait_send()
    fwd_sib_right.wait_send()
    fwd_sib_far.wait_send()
    w_copy(0, me_p, 0, tok, right).wait_send()
    w_copy(1, me_p, 0, tok, left).wait_send()
    w_copy(2, me_p, 0, tok, sib).wait_send()
    w_copy(3, left, 0, w_half, right).wait_send()
    w_copy(4, left, 0, tok, sib).wait_send()
    w_copy(5, right, w_half, w_half, left).wait_send()
    w_copy(6, right, 0, tok, sib).wait_send()
    w_copy(7, far, 0, tok, sib).wait_send()

    for h in range(2):
        k_copy(h, key_at[h], 0, 1).wait_send()
        k_copy(h, key_at[h], 1, side - 1).wait_send()
        k_copy(h, key_block(h, behind), 2, ahead).wait_send()
        v_copy(h, key_at[h], 0, 1).wait_send()
        v_copy(h, key_at[h], 1, side - 1).wait_send()
        v_copy(h, key_block(h, behind), 2, ahead).wait_send()
        for step in (1, 2, 3):
            dst = lax.rem(q_at[h] + step, side)
            q_copy(h, q_at[h], step).wait_send()
            o_copy(h, q_at[h], dst).wait_send()
            s_copy(h, q_at[h], dst).wait_send()

    def sent_a(i, _):
        a_copy(me_p, lax.rem(me_p + i, n_pack)).wait_send()
        return 0

    lax.fori_loop(1, n_pack, sent_a, 0)


def local(n_ctx, n_pack, *args):
    hidden, keys, values, w_query, w_out, gain, router, routes, order, pattern = args
    tok, width = hidden.shape
    span, heads = keys.shape
    routed = routes.shape[1]
    cap = 3 * tok // 8
    per_slot = routed // n_pack
    both = per_slot + cap
    side = math.isqrt(n_ctx)
    vmem = pl.BlockSpec(memory_space=pltpu.VMEM)
    dma = pltpu.SemaphoreType.DMA
    return pl.pallas_call(
        functools.partial(body, n_ctx, n_pack),
        out_shape=(
            jax.ShapeDtypeStruct((tok, width), BF16),
            jax.ShapeDtypeStruct((per_slot, width), BF16),
        ),
        in_specs=[vmem] * 11,
        out_specs=(vmem, vmem),
        scratch_shapes=[
            pltpu.VMEM((n_pack, cap, width), BF16),
            pltpu.VMEM((n_pack * cap, heads), BF16),
            pltpu.VMEM((n_pack * cap, routed), BF16),
            pltpu.VMEM((routed, n_pack * cap), BF16),
            pltpu.VMEM((routed, routed), BF16),
            pltpu.VMEM((routed, HD), F32),
            pltpu.VMEM((2, side, span, HD), BF16),
            pltpu.VMEM((2, side, span, 2 * HD), BF16),
            pltpu.VMEM((2, side, routed, HD), BF16),
            pltpu.VMEM((2, side, routed, HD), BF16),
            pltpu.VMEM((2, side, routed, HD), BF16),
            pltpu.VMEM((2, side, 8, routed), F32),
            pltpu.VMEM((2, side, 8, routed), F32),
            pltpu.VMEM((2, side, routed, HD), F32),
            pltpu.VMEM((2, 2, side, routed, HD), F32),
            pltpu.VMEM((routed, heads), BF16),
            pltpu.VMEM((n_pack * tok, width), BF16),
            pltpu.VMEM((n_pack, both, heads), BF16),
            pltpu.VMEM((n_pack, both, heads), BF16),
            pltpu.VMEM((both, width), F32),
            pltpu.VMEM((both, HD), F32),
            dma((8,)),
            dma((8,)),
            dma((8,)),
            dma((8,)),
            dma((12,)),
            dma((4 * side,)),
            dma((2 * side,)),
            dma((2 * side,)),
            dma((2 * side,)),
            dma((2 * side,)),
            dma((2 * side,)),
            dma((2 * side,)),
            dma((n_pack,)),
            dma((n_pack,)),
            dma,
        ],
        compiler_params=pltpu.CompilerParams(
            collective_id=0, has_side_effects=True, vmem_limit_bytes=60 << 20
        ),
        name="routed_attention",
    )(
        hidden,
        keys,
        values,
        w_query,
        w_out,
        gain.reshape(1, width),
        router.reshape(1, width),
        routes,
        order,
        pattern,
        jnp.asarray(turn_table()),
    )


def solution(mesh):
    return jax.shard_map(
        functools.partial(local, mesh.shape["ctx"], mesh.shape["pack"]),
        mesh=mesh,
        in_specs=(
            P(("ctx", "pack"), None),
            P("ctx", "pack"),
            P("ctx", "pack"),
            P(None, "pack"),
            P("pack", None),
            P(),
            P(),
            P("ctx", None),
            P("ctx", None),
            P(),
        ),
        out_specs=(P(("ctx", "pack"), None), P(("ctx", "pack"), None)),
        check_vma=False,
    )
```

```python
import functools
import math

import jax
import jax.numpy as jnp
import numpy as np
from jax import lax
from jax.experimental import pallas as pl
from jax.experimental.pallas import tpu as pltpu
from jax.sharding import PartitionSpec as P

HD = 128
EPS = 1e-6
NEG = -1e30
F32 = jnp.float32
BF16 = jnp.bfloat16
MESH = pl.DeviceIdType.MESH
LOG2E = 1.4426950408889634


def turn_table():
    lane = np.arange(HD) % (HD // 2)
    turns = 10000.0 ** (-2.0 * lane / HD) / (2.0 * math.pi)
    table = np.zeros((8, HD), np.float32)
    table[0] = np.mod(turns * 128.0, 1.0)
    table[1] = turns
    table[2] = np.where(np.arange(HD) < HD // 2, -1.0, 1.0)
    return table


def cos_sin(pos, table):
    hi = jnp.floor(pos * (1.0 / 128.0))
    low = pos - hi * 128.0
    u = hi * table[0:1]
    u = u - jnp.floor(u) + low * table[1:2]
    u = u - jnp.floor(u + 0.5)
    x = u * math.pi
    y = x * x
    s = 0.0
    for n in (11, 9, 7, 5, 3):
        s = (s + (-1.0) ** ((n - 1) // 2) / math.factorial(n)) * y
    s = (s + 1.0) * x
    c = 0.0
    for n in (12, 10, 8, 6, 4, 2):
        c = (c + (-1.0) ** (n // 2) / math.factorial(n)) * y
    c = c + 1.0
    return 1.0 - 2.0 * s * s, 2.0 * s * c


def body(
    n_ctx,
    n_pack,
    hidden,
    keys,
    values,
    w_query,
    w_out,
    gain,
    router,
    routes,
    order,
    pattern,
    table,
    hidden_out,
    packed,
    rows_all,
    q_pad,
    spread,
    gather,
    slot_of,
    pos_col,
    kbuf,
    vbuf,
    q_buf,
    o_send,
    o_in,
    st_send,
    st_in,
    acc,
    state,
    att,
    w_all,
    a_send,
    a_in,
    relay,
    mix,
    res,
    gate,
    row_send,
    row_recv,
    wo_send,
    wo_recv,
    kv_send,
    kv_recv,
    q_send_sem,
    q_recv_sem,
    o_send_sem,
    o_recv_sem,
    s_send_sem,
    s_recv_sem,
    a_send_sem,
    a_recv_sem,
    r_send_sem,
    r_recv_sem,
    loc_sem,
):
    me_c = lax.axis_index("ctx")
    me_p = lax.axis_index("pack")
    tok = hidden.shape[0]
    width = hidden.shape[1]
    span = keys.shape[0]
    routed = routes.shape[1]
    cap = rows_all.shape[1]
    per_slot = routed // n_pack
    half = cap // 2
    sib = me_p + 1 - 2 * lax.rem(me_p, 2)
    right = lax.rem(me_p + 2, n_pack)
    left = lax.rem(me_p + n_pack - 2, n_pack)
    far = lax.rem(me_p + 4, n_pack)
    sib_left = lax.rem(sib + n_pack - 2, n_pack)
    sib_right = lax.rem(sib + 2, n_pack)
    sib_far = lax.rem(sib + 4, n_pack)

    barrier = pltpu.get_barrier_semaphore()

    side = math.isqrt(n_ctx)
    y = me_c // side
    z = lax.rem(me_c, side)
    core = lax.rem(me_p, 2)

    def along_z(step):
        return y * side + lax.rem(z + step, side)

    def along_y(step):
        return lax.rem(y + step, side) * side + z

    def greet(c, p):
        pl.semaphore_signal(barrier, inc=1, device_id=(c, p), device_id_type=MESH)

    def greet_pack(i, _):
        greet(me_c, lax.rem(me_p + i, n_pack))
        return 0

    def greet_ctx(i, _):
        greet(along_y(i), me_p)
        greet(along_z(i), me_p)
        return 0

    lax.fori_loop(1, n_pack, greet_pack, 0)
    lax.fori_loop(1, side, greet_ctx, 0)

    rf = routes[...].astype(F32)
    lane_i = lax.broadcasted_iota(jnp.int32, (cap, routed), 1).astype(F32)
    sub_j = lax.broadcasted_iota(jnp.int32, (cap, routed), 0).astype(F32)

    def spread_of(block):
        low = (block * tok).astype(F32)
        start = jnp.sum(jnp.where(rf < low, 1.0, 0.0), axis=1, keepdims=True)
        end = jnp.sum(jnp.where(rf < low + tok, 1.0, 0.0), axis=1, keepdims=True)
        hit = jnp.logical_and(lane_i == sub_j + start, lane_i < end)
        pos = jnp.sum(jnp.where(hit, rf + 1.0, 0.0), axis=1, keepdims=True) - 1.0
        return jnp.where(hit, 1.0, 0.0), pos

    _, my_pos = spread_of(me_p)
    lane_t = lax.broadcasted_iota(jnp.int32, (cap, tok), 1).astype(F32)
    pick = jnp.where(lane_t == my_pos - (me_p * tok).astype(F32), 1.0, 0.0).astype(BF16)
    rows_all[me_p] = jnp.dot(pick, hidden[...], preferred_element_type=F32).astype(BF16)

    pl.semaphore_wait(barrier, 2 * (side - 1) + n_pack - 1)

    def row_copy(i, block, sub, peer):
        part = rows_all.at[block] if sub is None else rows_all.at[block, sub]
        return pltpu.make_async_remote_copy(
            src_ref=part,
            dst_ref=part,
            send_sem=row_send.at[i],
            recv_sem=row_recv.at[i],
            device_id=(me_c, peer),
            device_id_type=MESH,
        )

    first = pl.ds(0, half)
    second = pl.ds(half, half)
    to_right = row_copy(0, me_p, None, right)
    to_left = row_copy(1, me_p, None, left)
    to_sib = row_copy(2, me_p, None, sib)
    to_right.start()
    to_left.start()
    to_sib.start()

    key_ring = (along_y, along_z)
    key_at = (y, z)
    ahead = 1 + 2 * core
    behind = side - ahead

    def k_copy(h, j, i, step):
        part = kbuf.at[h, j]
        return pltpu.make_async_remote_copy(
            src_ref=part,
            dst_ref=part,
            send_sem=kv_send.at[h * 3 + i],
            recv_sem=kv_recv.at[h * side + j],
            device_id=(key_ring[h](step), me_p),
            device_id_type=MESH,
        )

    def v_copy(h, j, i, step):
        part = vbuf.at[h, j, :, pl.ds(0, HD)]
        return pltpu.make_async_remote_copy(
            src_ref=part,
            dst_ref=part,
            send_sem=kv_send.at[6 + h * 3 + i],
            recv_sem=kv_recv.at[2 * side + h * side + j],
            device_id=(key_ring[h](step), me_p),
            device_id_type=MESH,
        )

    for h in range(2):
        kbuf[h, key_at[h]] = keys[:, h * HD : (h + 1) * HD]
        k_copy(h, key_at[h], 0, 1).start()
        k_copy(h, key_at[h], 1, side - 1).start()
    for h in range(2):
        vbuf[h, key_at[h], :, 0:HD] = values[:, h * HD : (h + 1) * HD]
        v_copy(h, key_at[h], 0, 1).start()
        v_copy(h, key_at[h], 1, side - 1).start()
    for h in range(2):
        for j in range(side):
            vbuf[h, j, :, HD:] = jnp.ones((span, HD), BF16)

    def key_block(h, step):
        return lax.rem(key_at[h] + step, side)

    own_w = pltpu.make_async_copy(w_out, w_all.at[pl.ds(me_p * tok, tok)], loc_sem)
    own_w.start()

    gain_row = gain[...]
    trig = table[...]
    base = (me_c * span).astype(F32)

    for b in range(n_pack):
        hit, _ = spread_of(jnp.int32(b))
        spread[pl.ds(b * cap, cap), :] = hit.astype(BF16)
    flat = n_pack * cap
    lane_f = lax.broadcasted_iota(jnp.int32, (1, flat), 1).astype(F32)
    start_f = lane_f * 0.0
    end_f = lane_f * 0.0
    for b in range(n_pack):
        inside = jnp.logical_and(lane_f >= b * cap, lane_f < (b + 1) * cap)
        start = jnp.sum(jnp.where(rf < b * tok, 1.0, 0.0), axis=1, keepdims=True)
        end = jnp.sum(jnp.where(rf < (b + 1) * tok, 1.0, 0.0), axis=1, keepdims=True)
        start_f = jnp.where(inside, start + lane_f - b * cap, start_f)
        end_f = jnp.where(inside, end, end_f)
    row_i = lax.broadcasted_iota(jnp.int32, (routed, flat), 0).astype(F32)
    gather[...] = jnp.where(
        jnp.logical_and(row_i == start_f, row_i < end_f), 1.0, 0.0
    ).astype(BF16)
    pos_col[...] = jnp.transpose(jnp.broadcast_to(rf, (HD, routed)))
    order_col = jnp.transpose(jnp.broadcast_to(order[...].astype(F32), (HD, routed)))[:, 0:1]
    lane_s = lax.broadcasted_iota(jnp.int32, (routed, routed), 1).astype(F32)
    slot_of[...] = jnp.where(lane_s == order_col, 1.0, 0.0).astype(BF16)

    def project(block):
        rows = rows_all[block].astype(F32)
        mean_square = jnp.mean(rows * rows, axis=1, keepdims=True)
        normed = (rows * lax.rsqrt(mean_square + EPS) * gain_row).astype(BF16)
        proj = jnp.dot(normed, w_query[...], preferred_element_type=F32)
        _, pos = spread_of(block)
        cosine, sine = cos_sin(pos + base, trig)
        sine = sine * trig[2:3]
        start = pl.multiple_of(block * cap, cap)
        for h in range(2):
            part = proj[:, h * HD : (h + 1) * HD]
            turned = part * cosine + pltpu.roll(part, HD // 2, 1) * sine
            q_pad[pl.ds(start, cap), h * HD : (h + 1) * HD] = turned.astype(BF16)

    project(me_p)
    row_copy(0, left, None, right).wait_recv()
    fwd_right = row_copy(3, left, first, right)
    fwd_right.start()
    fwd_sib_left = row_copy(4, left, None, sib)
    fwd_sib_left.start()
    row_copy(1, right, None, left).wait_recv()
    fwd_left = row_copy(5, right, second, left)
    fwd_left.start()
    fwd_sib_right = row_copy(6, right, None, sib)
    fwd_sib_right.start()
    project(left)
    project(right)
    row_copy(2, sib, None, sib).wait_recv()
    project(sib)
    row_copy(4, sib_left, None, sib).wait_recv()
    project(sib_left)
    row_copy(6, sib_right, None, sib).wait_recv()
    project(sib_right)
    row_copy(3, far, first, right).wait_recv()
    row_copy(5, far, second, left).wait_recv()
    fwd_sib_far = row_copy(7, far, None, sib)
    fwd_sib_far.start()
    w_half = tok // 2

    def w_copy(i, block, lo, size, peer):
        part = w_all.at[pl.ds(block * tok + lo, size)]
        return pltpu.make_async_remote_copy(
            src_ref=part,
            dst_ref=part,
            send_sem=wo_send.at[i],
            recv_sem=wo_recv.at[i],
            device_id=(me_c, peer),
            device_id_type=MESH,
        )

    own_w.wait()
    w_copy(0, me_p, 0, tok, right).start()
    w_copy(1, me_p, 0, tok, left).start()

    project(far)
    row_copy(7, sib_far, None, sib).wait_recv()
    project(sib_far)

    query = jnp.dot(gather[...], q_pad[...], preferred_element_type=F32).astype(BF16)
    q_buf[0, z] = query[:, 0:HD]
    q_buf[1, y] = query[:, HD:]
    q_ring = (along_z, along_y)
    q_at = (z, y)

    def q_copy(h, src, step):
        return pltpu.make_async_remote_copy(
            src_ref=q_buf.at[h, src],
            dst_ref=q_buf.at[h, src],
            send_sem=q_send_sem.at[h * side + step],
            recv_sem=q_recv_sem.at[h * side + src],
            device_id=(q_ring[h](step), me_p),
            device_id_type=MESH,
        )

    for step in (1, 3):
        for h in range(2):
            q_copy(h, q_at[h], step).start()
    w_copy(2, me_p, 0, tok, sib).start()

    def q_forward(h):
        src = lax.rem(q_at[h] + behind, side)
        return pltpu.make_async_remote_copy(
            src_ref=q_buf.at[h, src],
            dst_ref=q_buf.at[h, src],
            send_sem=q_send_sem.at[h * side + 2],
            recv_sem=q_recv_sem.at[h * side + src],
            device_id=(q_ring[h](ahead), me_p),
            device_id_type=MESH,
        )

    chunk = 512
    tile = 256
    scale = LOG2E / math.sqrt(HD)

    def less(a, b):
        return (b - a + side - 1) // side

    def same(a, b):
        return 1 - less(a, b) - less(b, a)

    def blend(h, one, two):
        return one + h * (two - one)

    def step_in(h, t, j, own):
        if own:
            lane_k = lax.broadcasted_iota(jnp.int32, (tile, chunk), 1).astype(F32)
        else:
            span_q = blend(h, y * side + t, t * side + z)
            span_k = blend(h, j * side + z, y * side + j)
            wanted = pattern[pl.ds(span_q, 1), :]
            hit = jnp.max(jnp.where(wanted == span_k, 1.0, 0.0), axis=1, keepdims=True)

        def score(r, i):
            s = lax.dot_general(
                q_buf[h, t, r : r + tile, :],
                kbuf[h, j, i : i + chunk, :],
                (((1,), (1,)), ((), ())),
                preferred_element_type=F32,
            )
            if own:
                s = jnp.where(lane_k <= pos_col[r : r + tile, 0:1] - float(i), s, NEG)
            return s

        scores = [score(0, i) for i in range(0, span, chunk)]
        for r in range(0, routed, tile):
            peak = functools.reduce(
                jnp.maximum, [jnp.max(s, axis=1, keepdims=True) for s in scores]
            )
            peak = peak * scale
            later = []
            out = 0.0
            for n, i in enumerate(range(0, span, chunk)):
                if r + tile < routed:
                    later.append(score(r + tile, i))
                weights = jnp.exp2(scores[n] * scale - peak).astype(BF16)
                out = out + jnp.dot(
                    weights, vbuf[h, j, i : i + chunk, :], preferred_element_type=F32
                )
            rows = slice(r, r + tile)
            if own:
                acc[h, t, rows, :] = out[:, 0:HD]
                state[0, h, t, rows, :] = jnp.broadcast_to(peak, (tile, HD))
                state[1, h, t, rows, :] = out[:, HD:]
            else:
                peak = jnp.where(hit > 0.5, peak, NEG)
                former = state[0, h, t, rows, :]
                top = jnp.maximum(former, peak)
                a = jnp.exp2(former - top)
                b = jnp.exp2(peak - top) * hit
                acc[h, t, rows, :] = acc[h, t, rows, :] * a + out[:, 0:HD] * b
                state[0, h, t, rows, :] = top
                state[1, h, t, rows, :] = state[1, h, t, rows, :] * a + out[:, HD:] * b
            scores = later

    def slot(h, step):
        return lax.rem(blend(h, z, y) + step, side)

    def block(h, step):
        return lax.rem(blend(h, y, z) + step, side)

    def sees(h, t, j):
        by_row = less(j, y) + same(j, y) * less(z, t)
        by_col = less(y, t) + same(y, t) * less(j, z)
        return blend(h, by_row, by_col)

    def begin(h, _):
        for step in range(1, side):
            t = slot(h, step)
            acc[h, t] = jnp.zeros((routed, HD), F32)
            state[0, h, t] = jnp.full((routed, HD), NEG, F32)
            state[1, h, t] = jnp.zeros((routed, HD), F32)
        step_in(h, slot(h, 0), block(h, 0), True)
        return 0

    lax.fori_loop(0, 2, begin, 0)

    for h in range(2):
        q_copy(h, lax.rem(q_at[h] + behind, side), behind).wait_recv()
        q_forward(h).start()
    for h in range(2):
        q_copy(h, lax.rem(q_at[h] + ahead, side), ahead).wait_recv()

    def own_block(i, _):
        h = lax.rem(i, 2)
        turn = i // 2
        t = slot(h, turn + turn // 2 - 2 * (turn // 3))
        j = block(h, 0)

        @pl.when(sees(h, t, j) == 1)
        def _():
            step_in(h, t, j, False)

        return 0

    lax.fori_loop(2, 6, own_block, 0)

    for h in range(2):
        k_copy(h, key_block(h, behind), 0, behind).wait_recv()
        k_copy(h, key_block(h, behind), 2, ahead).start()
        v_copy(h, key_block(h, behind), 0, behind).wait_recv()
        v_copy(h, key_block(h, behind), 2, ahead).start()
    for h in range(2):
        q_copy(h, lax.rem(q_at[h] + 2, side), behind).wait_recv()

    lax.fori_loop(6, 8, own_block, 0)

    for h in range(2):
        k_copy(h, key_block(h, ahead), 0, ahead).wait_recv()
        v_copy(h, key_block(h, ahead), 0, ahead).wait_recv()

    def near_blocks(i, _):
        h = lax.rem(i, 2)
        turn = lax.rem(i // 2, side)
        t = slot(h, turn + turn // 2 - 2 * (turn // 3))
        j = block(h, 1 + 2 * (i // (2 * side)))

        @pl.when(sees(h, t, j) == 1)
        def _():
            step_in(h, t, j, False)

        return 0

    lax.fori_loop(0, 4 * side, near_blocks, 0)

    w_copy(0, left, 0, tok, right).wait_recv()
    w_copy(3, left, 0, w_half, right).start()
    w_copy(4, left, 0, tok, sib).start()
    w_copy(1, right, 0, tok, left).wait_recv()
    w_copy(5, right, w_half, w_half, left).start()
    w_copy(6, right, 0, tok, sib).start()

    for h in range(2):
        k_copy(h, key_block(h, 2), 0, behind).wait_recv()
        v_copy(h, key_block(h, 2), 0, behind).wait_recv()

    def o_copy(h, src, dst):
        return pltpu.make_async_remote_copy(
            src_ref=o_send.at[h, dst],
            dst_ref=o_in.at[h, src],
            send_sem=o_send_sem.at[h * side + dst],
            recv_sem=o_recv_sem.at[h * side + src],
            device_id=(blend(h, y * side + dst, dst * side + z), me_p),
            device_id_type=MESH,
        )

    def s_copy(h, src, dst):
        return pltpu.make_async_remote_copy(
            src_ref=st_send.at[h, dst],
            dst_ref=st_in.at[h, src],
            send_sem=s_send_sem.at[h * side + dst],
            recv_sem=s_recv_sem.at[h * side + src],
            device_id=(blend(h, y * side + dst, dst * side + z), me_p),
            device_id_type=MESH,
        )

    def far_block(i, _):
        h = lax.rem(i, 2)
        turn = i // 2
        step = lax.rem(turn + 1, side - 1) + 1
        at = slot(h, 0)
        t = slot(h, step)
        j = block(h, 2)

        @pl.when(sees(h, t, j) == 1)
        def _():
            step_in(h, t, j, False)

        den = state[1, h, t]
        o_send[h, t] = (acc[h, t] / jnp.where(den > 0.0, den, 1.0)).astype(BF16)
        lse = jnp.where(den > 0.0, state[0, h, t] + jnp.log2(den), NEG)
        st_send[h, t] = jnp.transpose(lse)[0:8]
        o_copy(h, at, t).start()
        s_copy(h, at, t).start()
        return 0

    lax.fori_loop(0, 2 * (side - 1), far_block, 0)

    def far_own(h, _):
        t = slot(h, 0)
        j = block(h, 2)

        @pl.when(sees(h, t, j) == 1)
        def _():
            step_in(h, t, j, False)

        return 0

    lax.fori_loop(0, 2, far_own, 0)

    w_copy(3, far, 0, w_half, right).wait_recv()
    w_copy(5, far, w_half, w_half, left).wait_recv()
    w_copy(7, far, 0, tok, sib).start()

    slot_rows = pl.ds(pl.multiple_of(me_p * per_slot, per_slot), per_slot)
    from_pad = jnp.dot(
        slot_of[slot_rows, :], gather[...], preferred_element_type=F32
    ).astype(BF16)
    for n in range(0, width, 512):
        picked = 0.0
        for b in range(n_pack):
            picked = picked + jnp.dot(
                from_pad[:, b * cap : (b + 1) * cap],
                rows_all[b, :, n : n + 512],
                preferred_element_type=F32,
            )
        res[0:per_slot, n : n + 512] = picked
    res[per_slot:, :] = rows_all[me_p].astype(F32)
    gate[...] = jnp.broadcast_to(
        jax.nn.sigmoid(jnp.sum(res[...] * router[...], axis=1, keepdims=True)), gate.shape
    )

    for h in range(2):
        peak, den = state[0, h, q_at[h]], state[1, h, q_at[h]]
        total = acc[h, q_at[h]]
        for step in (2, 1, 3):
            src = lax.rem(q_at[h] + step, side)
            o_copy(h, src, q_at[h]).wait_recv()
            s_copy(h, src, q_at[h]).wait_recv()
            lse = jnp.transpose(jnp.broadcast_to(st_in[h, src, 0:1, :], (HD, routed)))
            top = jnp.maximum(peak, lse)
            a = jnp.exp2(peak - top)
            b = jnp.exp2(lse - top)
            total = total * a + o_in[h, src].astype(F32) * b
            peak, den = top, den * a + b
        att[:, h * HD : (h + 1) * HD] = (total / den).astype(BF16)

    by_slot = jnp.dot(slot_of[...], att[...], preferred_element_type=F32).astype(BF16)
    by_owner = jnp.dot(spread[...], att[...], preferred_element_type=F32).astype(BF16)
    for d in range(n_pack):
        a_send[d, 0:per_slot, :] = by_slot[d * per_slot : (d + 1) * per_slot]
        a_send[d, per_slot:, :] = by_owner[d * cap : (d + 1) * cap]

    def a_copy(src, dst):
        return pltpu.make_async_remote_copy(
            src_ref=a_send.at[dst],
            dst_ref=a_in.at[src],
            send_sem=a_send_sem.at[dst],
            recv_sem=a_recv_sem.at[src],
            device_id=(me_c, dst),
            device_id_type=MESH,
        )

    def relay_copy(i, dst):
        return pltpu.make_async_remote_copy(
            src_ref=a_send.at[dst],
            dst_ref=relay.at[i],
            send_sem=r_send_sem.at[i],
            recv_sem=r_recv_sem.at[i],
            device_id=(me_c, left),
            device_id_type=MESH,
        )

    def relay_on(i, dst):
        return pltpu.make_async_remote_copy(
            src_ref=relay.at[i],
            dst_ref=a_in.at[right],
            send_sem=r_send_sem.at[2 + i],
            recv_sem=a_recv_sem.at[right],
            device_id=(me_c, dst),
            device_id_type=MESH,
        )

    @pl.when(core == 0)
    def _():
        a_copy(me_p, far).start()
        a_copy(me_p, sib_far).start()

    @pl.when(core == 1)
    def _():
        relay_copy(0, far).start()
        relay_copy(1, sib_far).start()

    a_copy(me_p, right).start()
    a_copy(me_p, left).start()
    a_copy(me_p, sib_right).start()
    a_copy(me_p, sib_left).start()
    a_copy(me_p, sib).start()

    def add(rows, b, first):
        for n in range(0, width, 512):
            cols = slice(n, n + 512)
            part = jnp.dot(
                rows, w_all[pl.ds(b * tok, tok), cols], preferred_element_type=F32
            )
            mix[:, cols] = part if first else mix[:, cols] + part

    add(a_send[me_p], me_p, True)
    w_copy(2, sib, 0, tok, sib).wait_recv()
    a_copy(sib, me_p).wait_recv()
    add(a_in[sib], sib, False)

    @pl.when(core == 1)
    def _():
        relay_copy(0, far).wait_recv()
        relay_on(0, left).start()
        relay_copy(1, sib_far).wait_recv()
        relay_on(1, sib_left).start()

    w_copy(4, sib_left, 0, tok, sib).wait_recv()
    w_copy(6, sib_right, 0, tok, sib).wait_recv()
    w_copy(7, sib_far, 0, tok, sib).wait_recv()
    for b in (right, left, sib_right, sib_left, far, sib_far):
        a_copy(b, me_p).wait_recv()
        add(a_in[b], b, False)

    present = lax.dot_general(
        pick, jnp.ones((cap, HD), BF16), (((0,), (0,)), ((), ())), preferred_element_type=F32
    )[:, 0:1]
    for n in range(0, width, 512):
        cols = slice(n, n + 512)
        updated = (res[:, cols] + gate[:, 0:1] * mix[:, cols]).astype(BF16)
        packed[:, cols] = updated[0:per_slot]
        placed = lax.dot_general(
            pick, updated[per_slot:], (((0,), (0,)), ((), ())), preferred_element_type=F32
        )
        hidden_out[:, cols] = jnp.where(present > 0.5, placed.astype(BF16), hidden[:, cols])

    to_right.wait_send()
    to_left.wait_send()
    to_sib.wait_send()
    fwd_right.wait_send()
    fwd_left.wait_send()
    fwd_sib_left.wait_send()
    fwd_sib_right.wait_send()
    fwd_sib_far.wait_send()
    w_copy(0, me_p, 0, tok, right).wait_send()
    w_copy(1, me_p, 0, tok, left).wait_send()
    w_copy(2, me_p, 0, tok, sib).wait_send()
    w_copy(3, left, 0, w_half, right).wait_send()
    w_copy(4, left, 0, tok, sib).wait_send()
    w_copy(5, right, w_half, w_half, left).wait_send()
    w_copy(6, right, 0, tok, sib).wait_send()
    w_copy(7, far, 0, tok, sib).wait_send()

    for h in range(2):
        k_copy(h, key_at[h], 0, 1).wait_send()
        k_copy(h, key_at[h], 1, side - 1).wait_send()
        k_copy(h, key_block(h, behind), 2, ahead).wait_send()
        v_copy(h, key_at[h], 0, 1).wait_send()
        v_copy(h, key_at[h], 1, side - 1).wait_send()
        v_copy(h, key_block(h, behind), 2, ahead).wait_send()
        q_copy(h, q_at[h], 1).wait_send()
        q_copy(h, q_at[h], 3).wait_send()
        q_forward(h).wait_send()
        for step in (1, 2, 3):
            dst = lax.rem(q_at[h] + step, side)
            o_copy(h, q_at[h], dst).wait_send()
            s_copy(h, q_at[h], dst).wait_send()

    a_copy(me_p, right).wait_send()
    a_copy(me_p, left).wait_send()
    a_copy(me_p, sib_right).wait_send()
    a_copy(me_p, sib_left).wait_send()
    a_copy(me_p, sib).wait_send()

    @pl.when(core == 0)
    def _():
        a_copy(me_p, far).wait_send()
        a_copy(me_p, sib_far).wait_send()

    @pl.when(core == 1)
    def _():
        relay_copy(0, far).wait_send()
        relay_copy(1, sib_far).wait_send()
        relay_on(0, left).wait_send()
        relay_on(1, sib_left).wait_send()


def local(n_ctx, n_pack, *args):
    hidden, keys, values, w_query, w_out, gain, router, routes, order, pattern = args
    tok, width = hidden.shape
    span, heads = keys.shape
    routed = routes.shape[1]
    cap = 3 * tok // 8
    per_slot = routed // n_pack
    both = per_slot + cap
    side = math.isqrt(n_ctx)
    vmem = pl.BlockSpec(memory_space=pltpu.VMEM)
    dma = pltpu.SemaphoreType.DMA
    return pl.pallas_call(
        functools.partial(body, n_ctx, n_pack),
        out_shape=(
            jax.ShapeDtypeStruct((tok, width), BF16),
            jax.ShapeDtypeStruct((per_slot, width), BF16),
        ),
        in_specs=[vmem] * 11,
        out_specs=(vmem, vmem),
        scratch_shapes=[
            pltpu.VMEM((n_pack, cap, width), BF16),
            pltpu.VMEM((n_pack * cap, heads), BF16),
            pltpu.VMEM((n_pack * cap, routed), BF16),
            pltpu.VMEM((routed, n_pack * cap), BF16),
            pltpu.VMEM((routed, routed), BF16),
            pltpu.VMEM((routed, HD), F32),
            pltpu.VMEM((2, side, span, HD), BF16),
            pltpu.VMEM((2, side, span, 2 * HD), BF16),
            pltpu.VMEM((2, side, routed, HD), BF16),
            pltpu.VMEM((2, side, routed, HD), BF16),
            pltpu.VMEM((2, side, routed, HD), BF16),
            pltpu.VMEM((2, side, 8, routed), F32),
            pltpu.VMEM((2, side, 8, routed), F32),
            pltpu.VMEM((2, side, routed, HD), F32),
            pltpu.VMEM((2, 2, side, routed, HD), F32),
            pltpu.VMEM((routed, heads), BF16),
            pltpu.VMEM((n_pack * tok, width), BF16),
            pltpu.VMEM((n_pack, both, heads), BF16),
            pltpu.VMEM((n_pack, both, heads), BF16),
            pltpu.VMEM((2, both, heads), BF16),
            pltpu.VMEM((both, width), F32),
            pltpu.VMEM((both, width), F32),
            pltpu.VMEM((both, HD), F32),
            dma((8,)),
            dma((8,)),
            dma((8,)),
            dma((8,)),
            dma((12,)),
            dma((4 * side,)),
            dma((2 * side,)),
            dma((2 * side,)),
            dma((2 * side,)),
            dma((2 * side,)),
            dma((2 * side,)),
            dma((2 * side,)),
            dma((n_pack,)),
            dma((n_pack,)),
            dma((4,)),
            dma((2,)),
            dma,
        ],
        compiler_params=pltpu.CompilerParams(
            collective_id=0, has_side_effects=True, vmem_limit_bytes=60 << 20
        ),
        name="routed_attention",
    )(
        hidden,
        keys,
        values,
        w_query,
        w_out,
        gain.reshape(1, width),
        router.reshape(1, width),
        routes,
        order,
        pattern,
        jnp.asarray(turn_table()),
    )


def solution(mesh):
    return jax.shard_map(
        functools.partial(local, mesh.shape["ctx"], mesh.shape["pack"]),
        mesh=mesh,
        in_specs=(
            P(("ctx", "pack"), None),
            P("ctx", "pack"),
            P("ctx", "pack"),
            P(None, "pack"),
            P("pack", None),
            P(),
            P(),
            P("ctx", None),
            P("ctx", None),
            P(),
        ),
        out_specs=(P(("ctx", "pack"), None), P(("ctx", "pack"), None)),
        check_vma=False,
    )
```

```python
import functools
import math

import jax
import jax.numpy as jnp
import numpy as np
from jax import lax
from jax.experimental import pallas as pl
from jax.experimental.pallas import tpu as pltpu
from jax.sharding import PartitionSpec as P

HD = 128
EPS = 1e-6
NEG = -1e30
F32 = jnp.float32
BF16 = jnp.bfloat16
MESH = pl.DeviceIdType.MESH
LOG2E = 1.4426950408889634


def turn_table():
    lane = np.arange(HD) % (HD // 2)
    turns = 10000.0 ** (-2.0 * lane / HD) / (2.0 * math.pi)
    table = np.zeros((8, HD), np.float32)
    table[0] = np.mod(turns * 128.0, 1.0)
    table[1] = turns
    table[2] = np.where(np.arange(HD) < HD // 2, -1.0, 1.0)
    return table


def cos_sin(pos, table):
    hi = jnp.floor(pos * (1.0 / 128.0))
    low = pos - hi * 128.0
    u = hi * table[0:1]
    u = u - jnp.floor(u) + low * table[1:2]
    u = u - jnp.floor(u + 0.5)
    x = u * math.pi
    y = x * x
    s = 0.0
    for n in (11, 9, 7, 5, 3):
        s = (s + (-1.0) ** ((n - 1) // 2) / math.factorial(n)) * y
    s = (s + 1.0) * x
    c = 0.0
    for n in (12, 10, 8, 6, 4, 2):
        c = (c + (-1.0) ** (n // 2) / math.factorial(n)) * y
    c = c + 1.0
    return 1.0 - 2.0 * s * s, 2.0 * s * c


def body(
    n_ctx,
    n_pack,
    hidden,
    keys,
    values,
    w_query,
    w_out,
    gain,
    router,
    routes,
    order,
    pattern,
    table,
    hidden_out,
    packed,
    rows_all,
    w_q,
    q_pad,
    spread,
    gather,
    slot_of,
    pos_col,
    kbuf,
    vbuf,
    q_buf,
    o_send,
    o_in,
    st_send,
    st_in,
    acc,
    state,
    att,
    w_all,
    a_send,
    a_in,
    relay,
    mix,
    res,
    gate,
    row_send,
    row_recv,
    wo_send,
    wo_recv,
    kv_send,
    kv_recv,
    q_send_sem,
    q_recv_sem,
    o_send_sem,
    o_recv_sem,
    s_send_sem,
    s_recv_sem,
    a_send_sem,
    a_recv_sem,
    r_send_sem,
    r_recv_sem,
    loc_sem,
    kv_sem,
):
    me_c = lax.axis_index("ctx")
    me_p = lax.axis_index("pack")
    tok = hidden.shape[0]
    width = hidden.shape[1]
    span = keys.shape[0]
    routed = routes.shape[1]
    cap = rows_all.shape[1]
    per_slot = routed // n_pack
    half = cap // 2
    sib = me_p + 1 - 2 * lax.rem(me_p, 2)
    right = lax.rem(me_p + 2, n_pack)
    left = lax.rem(me_p + n_pack - 2, n_pack)
    far = lax.rem(me_p + 4, n_pack)
    sib_left = lax.rem(sib + n_pack - 2, n_pack)
    sib_right = lax.rem(sib + 2, n_pack)
    sib_far = lax.rem(sib + 4, n_pack)

    barrier = pltpu.get_barrier_semaphore()

    side = math.isqrt(n_ctx)
    y = me_c // side
    z = lax.rem(me_c, side)
    core = lax.rem(me_p, 2)

    def along_z(step):
        return y * side + lax.rem(z + step, side)

    def along_y(step):
        return lax.rem(y + step, side) * side + z

    def greet(c, p):
        pl.semaphore_signal(barrier, inc=1, device_id=(c, p), device_id_type=MESH)

    def greet_pack(i, _):
        greet(me_c, lax.rem(me_p + i, n_pack))
        return 0

    def greet_ctx(i, _):
        greet(along_y(i), me_p)
        greet(along_z(i), me_p)
        return 0

    lax.fori_loop(1, n_pack, greet_pack, 0)
    lax.fori_loop(1, side, greet_ctx, 0)

    own_w = pltpu.make_async_copy(w_out, w_all.at[pl.ds(me_p * tok, tok)], loc_sem)
    own_q = pltpu.make_async_copy(w_query, w_q, kv_sem.at[4])
    own_k = []
    own_v = []
    for h in range(2):
        cols = pl.ds(h * HD, HD)
        at = (y, z)[h]
        own_k.append(pltpu.make_async_copy(keys.at[:, cols], kbuf.at[h, at], kv_sem.at[h]))
        own_v.append(
            pltpu.make_async_copy(
                values.at[:, cols], vbuf.at[h, at, :, pl.ds(0, HD)], kv_sem.at[2 + h]
            )
        )
    for copy in own_k + own_v + [own_q, own_w]:
        copy.start()

    rf = routes[...].astype(F32)
    lane_i = lax.broadcasted_iota(jnp.int32, (cap, routed), 1).astype(F32)
    sub_j = lax.broadcasted_iota(jnp.int32, (cap, routed), 0).astype(F32)

    def spread_of(block):
        low = (block * tok).astype(F32)
        start = jnp.sum(jnp.where(rf < low, 1.0, 0.0), axis=1, keepdims=True)
        end = jnp.sum(jnp.where(rf < low + tok, 1.0, 0.0), axis=1, keepdims=True)
        hit = jnp.logical_and(lane_i == sub_j + start, lane_i < end)
        pos = jnp.sum(jnp.where(hit, rf + 1.0, 0.0), axis=1, keepdims=True) - 1.0
        return jnp.where(hit, 1.0, 0.0), pos

    _, my_pos = spread_of(me_p)
    lane_t = lax.broadcasted_iota(jnp.int32, (cap, tok), 1).astype(F32)
    pick = jnp.where(lane_t == my_pos - (me_p * tok).astype(F32), 1.0, 0.0).astype(BF16)
    rows_all[me_p] = jnp.dot(pick, hidden[...], preferred_element_type=F32).astype(BF16)

    pl.semaphore_wait(barrier, 2 * (side - 1) + n_pack - 1)

    def row_copy(i, block, sub, peer):
        part = rows_all.at[block] if sub is None else rows_all.at[block, sub]
        return pltpu.make_async_remote_copy(
            src_ref=part,
            dst_ref=part,
            send_sem=row_send.at[i],
            recv_sem=row_recv.at[i],
            device_id=(me_c, peer),
            device_id_type=MESH,
        )

    first = pl.ds(0, half)
    second = pl.ds(half, half)
    to_right = row_copy(0, me_p, None, right)
    to_left = row_copy(1, me_p, None, left)
    to_sib = row_copy(2, me_p, None, sib)
    to_right.start()
    to_left.start()
    to_sib.start()

    key_ring = (along_y, along_z)
    key_at = (y, z)
    ahead = 1 + 2 * core
    behind = side - ahead

    def k_copy(h, j, i, step):
        part = kbuf.at[h, j]
        return pltpu.make_async_remote_copy(
            src_ref=part,
            dst_ref=part,
            send_sem=kv_send.at[h * 3 + i],
            recv_sem=kv_recv.at[h * side + j],
            device_id=(key_ring[h](step), me_p),
            device_id_type=MESH,
        )

    def v_copy(h, j, i, step):
        part = vbuf.at[h, j, :, pl.ds(0, HD)]
        return pltpu.make_async_remote_copy(
            src_ref=part,
            dst_ref=part,
            send_sem=kv_send.at[6 + h * 3 + i],
            recv_sem=kv_recv.at[2 * side + h * side + j],
            device_id=(key_ring[h](step), me_p),
            device_id_type=MESH,
        )

    for h in range(2):
        own_k[h].wait()
        k_copy(h, key_at[h], 0, 1).start()
        k_copy(h, key_at[h], 1, side - 1).start()
    for h in range(2):
        own_v[h].wait()
        v_copy(h, key_at[h], 0, 1).start()
        v_copy(h, key_at[h], 1, side - 1).start()
    for h in range(2):
        for j in range(side):
            vbuf[h, j, :, HD:] = jnp.ones((span, HD), BF16)

    def key_block(h, step):
        return lax.rem(key_at[h] + step, side)


    gain_row = gain[...]
    trig = table[...]
    base = (me_c * span).astype(F32)

    for b in range(n_pack):
        hit, _ = spread_of(jnp.int32(b))
        spread[pl.ds(b * cap, cap), :] = hit.astype(BF16)
    flat = n_pack * cap
    lane_f = lax.broadcasted_iota(jnp.int32, (1, flat), 1).astype(F32)
    start_f = lane_f * 0.0
    end_f = lane_f * 0.0
    for b in range(n_pack):
        inside = jnp.logical_and(lane_f >= b * cap, lane_f < (b + 1) * cap)
        start = jnp.sum(jnp.where(rf < b * tok, 1.0, 0.0), axis=1, keepdims=True)
        end = jnp.sum(jnp.where(rf < (b + 1) * tok, 1.0, 0.0), axis=1, keepdims=True)
        start_f = jnp.where(inside, start + lane_f - b * cap, start_f)
        end_f = jnp.where(inside, end, end_f)
    row_i = lax.broadcasted_iota(jnp.int32, (routed, flat), 0).astype(F32)
    gather[...] = jnp.where(
        jnp.logical_and(row_i == start_f, row_i < end_f), 1.0, 0.0
    ).astype(BF16)
    pos_col[...] = jnp.transpose(jnp.broadcast_to(rf, (HD, routed)))
    order_col = jnp.transpose(jnp.broadcast_to(order[...].astype(F32), (HD, routed)))[:, 0:1]
    lane_s = lax.broadcasted_iota(jnp.int32, (routed, routed), 1).astype(F32)
    slot_of[...] = jnp.where(lane_s == order_col, 1.0, 0.0).astype(BF16)

    def project(block):
        rows = rows_all[block].astype(F32)
        mean_square = jnp.mean(rows * rows, axis=1, keepdims=True)
        normed = (rows * lax.rsqrt(mean_square + EPS) * gain_row).astype(BF16)
        proj = jnp.dot(normed, w_q[...], preferred_element_type=F32)
        _, pos = spread_of(block)
        cosine, sine = cos_sin(pos + base, trig)
        sine = sine * trig[2:3]
        start = pl.multiple_of(block * cap, cap)
        for h in range(2):
            part = proj[:, h * HD : (h + 1) * HD]
            turned = part * cosine + pltpu.roll(part, HD // 2, 1) * sine
            q_pad[pl.ds(start, cap), h * HD : (h + 1) * HD] = turned.astype(BF16)

    own_q.wait()
    project(me_p)
    row_copy(0, left, None, right).wait_recv()
    fwd_right = row_copy(3, left, first, right)
    fwd_right.start()
    fwd_sib_left = row_copy(4, left, None, sib)
    fwd_sib_left.start()
    row_copy(1, right, None, left).wait_recv()
    fwd_left = row_copy(5, right, second, left)
    fwd_left.start()
    fwd_sib_right = row_copy(6, right, None, sib)
    fwd_sib_right.start()
    project(left)
    project(right)
    row_copy(2, sib, None, sib).wait_recv()
    project(sib)
    row_copy(4, sib_left, None, sib).wait_recv()
    project(sib_left)
    row_copy(6, sib_right, None, sib).wait_recv()
    project(sib_right)
    row_copy(3, far, first, right).wait_recv()
    row_copy(5, far, second, left).wait_recv()
    fwd_sib_far = row_copy(7, far, None, sib)
    fwd_sib_far.start()
    w_half = tok // 2

    def w_copy(i, block, lo, size, peer):
        part = w_all.at[pl.ds(block * tok + lo, size)]
        return pltpu.make_async_remote_copy(
            src_ref=part,
            dst_ref=part,
            send_sem=wo_send.at[i],
            recv_sem=wo_recv.at[i],
            device_id=(me_c, peer),
            device_id_type=MESH,
        )

    own_w.wait()
    w_copy(0, me_p, 0, tok, right).start()
    w_copy(1, me_p, 0, tok, left).start()

    project(far)
    row_copy(7, sib_far, None, sib).wait_recv()
    project(sib_far)

    query = jnp.dot(gather[...], q_pad[...], preferred_element_type=F32).astype(BF16)
    q_buf[0, z] = query[:, 0:HD]
    q_buf[1, y] = query[:, HD:]
    q_ring = (along_z, along_y)
    q_at = (z, y)

    def q_copy(h, src, step):
        return pltpu.make_async_remote_copy(
            src_ref=q_buf.at[h, src],
            dst_ref=q_buf.at[h, src],
            send_sem=q_send_sem.at[h * side + step],
            recv_sem=q_recv_sem.at[h * side + src],
            device_id=(q_ring[h](step), me_p),
            device_id_type=MESH,
        )

    for step in (1, 3):
        for h in range(2):
            q_copy(h, q_at[h], step).start()
    w_copy(2, me_p, 0, tok, sib).start()

    def q_forward(h):
        src = lax.rem(q_at[h] + behind, side)
        return pltpu.make_async_remote_copy(
            src_ref=q_buf.at[h, src],
            dst_ref=q_buf.at[h, src],
            send_sem=q_send_sem.at[h * side + 2],
            recv_sem=q_recv_sem.at[h * side + src],
            device_id=(q_ring[h](ahead), me_p),
            device_id_type=MESH,
        )

    chunk = 512
    tile = 256
    scale = LOG2E / math.sqrt(HD)

    def less(a, b):
        return (b - a + side - 1) // side

    def same(a, b):
        return 1 - less(a, b) - less(b, a)

    def blend(h, one, two):
        return one + h * (two - one)

    def step_in(h, t, j, own):
        if own:
            lane_k = lax.broadcasted_iota(jnp.int32, (tile, chunk), 1).astype(F32)
        else:
            span_q = blend(h, y * side + t, t * side + z)
            span_k = blend(h, j * side + z, y * side + j)
            wanted = pattern[pl.ds(span_q, 1), :]
            hit = jnp.max(jnp.where(wanted == span_k, 1.0, 0.0), axis=1, keepdims=True)

        def score(r, i):
            s = lax.dot_general(
                q_buf[h, t, r : r + tile, :],
                kbuf[h, j, i : i + chunk, :],
                (((1,), (1,)), ((), ())),
                preferred_element_type=F32,
            )
            if own:
                s = jnp.where(lane_k <= pos_col[r : r + tile, 0:1] - float(i), s, NEG)
            return s

        scores = [score(0, i) for i in range(0, span, chunk)]
        for r in range(0, routed, tile):
            peak = functools.reduce(
                jnp.maximum, [jnp.max(s, axis=1, keepdims=True) for s in scores]
            )
            peak = peak * scale
            later = []
            out = 0.0
            for n, i in enumerate(range(0, span, chunk)):
                if r + tile < routed:
                    later.append(score(r + tile, i))
                weights = jnp.exp2(scores[n] * scale - peak).astype(BF16)
                out = out + jnp.dot(
                    weights, vbuf[h, j, i : i + chunk, :], preferred_element_type=F32
                )
            rows = slice(r, r + tile)
            if own:
                acc[h, t, rows, :] = out[:, 0:HD]
                state[0, h, t, rows, :] = jnp.broadcast_to(peak, (tile, HD))
                state[1, h, t, rows, :] = out[:, HD:]
            else:
                peak = jnp.where(hit > 0.5, peak, NEG)
                former = state[0, h, t, rows, :]
                top = jnp.maximum(former, peak)
                a = jnp.exp2(former - top)
                b = jnp.exp2(peak - top) * hit
                acc[h, t, rows, :] = acc[h, t, rows, :] * a + out[:, 0:HD] * b
                state[0, h, t, rows, :] = top
                state[1, h, t, rows, :] = state[1, h, t, rows, :] * a + out[:, HD:] * b
            scores = later

    def slot(h, step):
        return lax.rem(blend(h, z, y) + step, side)

    def block(h, step):
        return lax.rem(blend(h, y, z) + step, side)

    def sees(h, t, j):
        by_row = less(j, y) + same(j, y) * less(z, t)
        by_col = less(y, t) + same(y, t) * less(j, z)
        return blend(h, by_row, by_col)

    def begin(h, _):
        for step in range(1, side):
            t = slot(h, step)
            acc[h, t] = jnp.zeros((routed, HD), F32)
            state[0, h, t] = jnp.full((routed, HD), NEG, F32)
            state[1, h, t] = jnp.zeros((routed, HD), F32)
        step_in(h, slot(h, 0), block(h, 0), True)
        return 0

    lax.fori_loop(0, 2, begin, 0)

    for h in range(2):
        q_copy(h, lax.rem(q_at[h] + behind, side), behind).wait_recv()
        q_forward(h).start()
    for h in range(2):
        q_copy(h, lax.rem(q_at[h] + ahead, side), ahead).wait_recv()

    def own_block(i, _):
        h = lax.rem(i, 2)
        turn = i // 2
        t = slot(h, turn + turn // 2 - 2 * (turn // 3))
        j = block(h, 0)

        @pl.when(sees(h, t, j) == 1)
        def _():
            step_in(h, t, j, False)

        return 0

    lax.fori_loop(2, 6, own_block, 0)

    for h in range(2):
        k_copy(h, key_block(h, behind), 0, behind).wait_recv()
        k_copy(h, key_block(h, behind), 2, ahead).start()
        v_copy(h, key_block(h, behind), 0, behind).wait_recv()
        v_copy(h, key_block(h, behind), 2, ahead).start()
    for h in range(2):
        q_copy(h, lax.rem(q_at[h] + 2, side), behind).wait_recv()

    lax.fori_loop(6, 8, own_block, 0)

    for h in range(2):
        k_copy(h, key_block(h, ahead), 0, ahead).wait_recv()
        v_copy(h, key_block(h, ahead), 0, ahead).wait_recv()

    def near_blocks(i, _):
        h = lax.rem(i, 2)
        turn = lax.rem(i // 2, side)
        t = slot(h, turn + turn // 2 - 2 * (turn // 3))
        j = block(h, 1 + 2 * (i // (2 * side)))

        @pl.when(sees(h, t, j) == 1)
        def _():
            step_in(h, t, j, False)

        return 0

    lax.fori_loop(0, 3 * side, near_blocks, 0)

    w_copy(0, left, 0, tok, right).wait_recv()
    w_copy(3, left, 0, w_half, right).start()
    w_copy(4, left, 0, tok, sib).start()
    w_copy(1, right, 0, tok, left).wait_recv()
    w_copy(5, right, w_half, w_half, left).start()
    w_copy(6, right, 0, tok, sib).start()

    lax.fori_loop(3 * side, 4 * side, near_blocks, 0)

    for h in range(2):
        k_copy(h, key_block(h, 2), 0, behind).wait_recv()
        v_copy(h, key_block(h, 2), 0, behind).wait_recv()

    def o_copy(h, src, dst):
        return pltpu.make_async_remote_copy(
            src_ref=o_send.at[h, dst],
            dst_ref=o_in.at[h, src],
            send_sem=o_send_sem.at[h * side + dst],
            recv_sem=o_recv_sem.at[h * side + src],
            device_id=(blend(h, y * side + dst, dst * side + z), me_p),
            device_id_type=MESH,
        )

    def s_copy(h, src, dst):
        return pltpu.make_async_remote_copy(
            src_ref=st_send.at[h, dst],
            dst_ref=st_in.at[h, src],
            send_sem=s_send_sem.at[h * side + dst],
            recv_sem=s_recv_sem.at[h * side + src],
            device_id=(blend(h, y * side + dst, dst * side + z), me_p),
            device_id_type=MESH,
        )

    def far_block(i, _):
        h = lax.rem(i, 2)
        turn = i // 2
        step = lax.rem(turn + 1, side - 1) + 1
        at = slot(h, 0)
        t = slot(h, step)
        j = block(h, 2)

        @pl.when(sees(h, t, j) == 1)
        def _():
            step_in(h, t, j, False)

        den = state[1, h, t]
        o_send[h, t] = (acc[h, t] / jnp.where(den > 0.0, den, 1.0)).astype(BF16)
        lse = jnp.where(den > 0.0, state[0, h, t] + jnp.log2(den), NEG)
        st_send[h, t] = jnp.transpose(lse)[0:8]
        o_copy(h, at, t).start()
        s_copy(h, at, t).start()
        return 0

    lax.fori_loop(0, 2 * (side - 1), far_block, 0)

    def far_own(h, _):
        t = slot(h, 0)
        j = block(h, 2)

        @pl.when(sees(h, t, j) == 1)
        def _():
            step_in(h, t, j, False)

        return 0

    lax.fori_loop(0, 2, far_own, 0)


    slot_rows = pl.ds(pl.multiple_of(me_p * per_slot, per_slot), per_slot)
    from_pad = jnp.dot(
        slot_of[slot_rows, :], gather[...], preferred_element_type=F32
    ).astype(BF16)
    for n in range(0, width, 512):
        picked = 0.0
        for b in range(n_pack):
            picked = picked + jnp.dot(
                from_pad[:, b * cap : (b + 1) * cap],
                rows_all[b, :, n : n + 512],
                preferred_element_type=F32,
            )
        res[0:per_slot, n : n + 512] = picked
    res[per_slot:, :] = rows_all[me_p].astype(F32)
    gate[...] = jnp.broadcast_to(
        jax.nn.sigmoid(jnp.sum(res[...] * router[...], axis=1, keepdims=True)), gate.shape
    )

    for h in range(2):
        peak, den = state[0, h, q_at[h]], state[1, h, q_at[h]]
        total = acc[h, q_at[h]]
        for step in (2, 1, 3):
            src = lax.rem(q_at[h] + step, side)
            o_copy(h, src, q_at[h]).wait_recv()
            s_copy(h, src, q_at[h]).wait_recv()
            lse = jnp.transpose(jnp.broadcast_to(st_in[h, src, 0:1, :], (HD, routed)))
            top = jnp.maximum(peak, lse)
            a = jnp.exp2(peak - top)
            b = jnp.exp2(lse - top)
            total = total * a + o_in[h, src].astype(F32) * b
            peak, den = top, den * a + b
        att[:, h * HD : (h + 1) * HD] = (total / den).astype(BF16)

    by_slot = jnp.dot(slot_of[...], att[...], preferred_element_type=F32).astype(BF16)
    by_owner = jnp.dot(spread[...], att[...], preferred_element_type=F32).astype(BF16)
    for d in range(n_pack):
        a_send[d, 0:per_slot, :] = by_slot[d * per_slot : (d + 1) * per_slot]
        a_send[d, per_slot:, :] = by_owner[d * cap : (d + 1) * cap]

    def a_copy(src, dst):
        return pltpu.make_async_remote_copy(
            src_ref=a_send.at[dst],
            dst_ref=a_in.at[src],
            send_sem=a_send_sem.at[dst],
            recv_sem=a_recv_sem.at[src],
            device_id=(me_c, dst),
            device_id_type=MESH,
        )

    def relay_copy(i, dst):
        return pltpu.make_async_remote_copy(
            src_ref=a_send.at[dst],
            dst_ref=relay.at[i],
            send_sem=r_send_sem.at[i],
            recv_sem=r_recv_sem.at[i],
            device_id=(me_c, left),
            device_id_type=MESH,
        )

    def relay_on(i, dst):
        return pltpu.make_async_remote_copy(
            src_ref=relay.at[i],
            dst_ref=a_in.at[right],
            send_sem=r_send_sem.at[2 + i],
            recv_sem=a_recv_sem.at[right],
            device_id=(me_c, dst),
            device_id_type=MESH,
        )

    @pl.when(core == 0)
    def _():
        a_copy(me_p, far).start()
        a_copy(me_p, sib_far).start()

    @pl.when(core == 1)
    def _():
        relay_copy(0, far).start()
        relay_copy(1, sib_far).start()

    a_copy(me_p, right).start()
    a_copy(me_p, left).start()
    a_copy(me_p, sib_right).start()
    a_copy(me_p, sib_left).start()
    a_copy(me_p, sib).start()

    def add(rows, b, first):
        for n in range(0, width, 512):
            cols = slice(n, n + 512)
            part = jnp.dot(
                rows, w_all[pl.ds(b * tok, tok), cols], preferred_element_type=F32
            )
            mix[:, cols] = part if first else mix[:, cols] + part

    w_copy(3, far, 0, w_half, right).wait_recv()
    w_copy(5, far, w_half, w_half, left).wait_recv()
    w_copy(7, far, 0, tok, sib).start()

    add(a_send[me_p], me_p, True)
    w_copy(2, sib, 0, tok, sib).wait_recv()
    a_copy(sib, me_p).wait_recv()
    add(a_in[sib], sib, False)

    @pl.when(core == 1)
    def _():
        relay_copy(0, far).wait_recv()
        relay_on(0, left).start()
        relay_copy(1, sib_far).wait_recv()
        relay_on(1, sib_left).start()

    late = {2: (6, sib_right), 3: (4, sib_left), 5: (7, sib_far)}
    for n, b in enumerate((right, left, sib_right, sib_left, far, sib_far)):
        if n in late:
            w_copy(late[n][0], late[n][1], 0, tok, sib).wait_recv()
        a_copy(b, me_p).wait_recv()
        add(a_in[b], b, False)

    present = lax.dot_general(
        pick, jnp.ones((cap, HD), BF16), (((0,), (0,)), ((), ())), preferred_element_type=F32
    )[:, 0:1]
    for n in range(0, width, 512):
        cols = slice(n, n + 512)
        updated = (res[:, cols] + gate[:, 0:1] * mix[:, cols]).astype(BF16)
        packed[:, cols] = updated[0:per_slot]
        placed = lax.dot_general(
            pick, updated[per_slot:], (((0,), (0,)), ((), ())), preferred_element_type=F32
        )
        hidden_out[:, cols] = jnp.where(present > 0.5, placed.astype(BF16), hidden[:, cols])

    to_right.wait_send()
    to_left.wait_send()
    to_sib.wait_send()
    fwd_right.wait_send()
    fwd_left.wait_send()
    fwd_sib_left.wait_send()
    fwd_sib_right.wait_send()
    fwd_sib_far.wait_send()
    w_copy(0, me_p, 0, tok, right).wait_send()
    w_copy(1, me_p, 0, tok, left).wait_send()
    w_copy(2, me_p, 0, tok, sib).wait_send()
    w_copy(3, left, 0, w_half, right).wait_send()
    w_copy(4, left, 0, tok, sib).wait_send()
    w_copy(5, right, w_half, w_half, left).wait_send()
    w_copy(6, right, 0, tok, sib).wait_send()
    w_copy(7, far, 0, tok, sib).wait_send()

    for h in range(2):
        k_copy(h, key_at[h], 0, 1).wait_send()
        k_copy(h, key_at[h], 1, side - 1).wait_send()
        k_copy(h, key_block(h, behind), 2, ahead).wait_send()
        v_copy(h, key_at[h], 0, 1).wait_send()
        v_copy(h, key_at[h], 1, side - 1).wait_send()
        v_copy(h, key_block(h, behind), 2, ahead).wait_send()
        q_copy(h, q_at[h], 1).wait_send()
        q_copy(h, q_at[h], 3).wait_send()
        q_forward(h).wait_send()
        for step in (1, 2, 3):
            dst = lax.rem(q_at[h] + step, side)
            o_copy(h, q_at[h], dst).wait_send()
            s_copy(h, q_at[h], dst).wait_send()

    a_copy(me_p, right).wait_send()
    a_copy(me_p, left).wait_send()
    a_copy(me_p, sib_right).wait_send()
    a_copy(me_p, sib_left).wait_send()
    a_copy(me_p, sib).wait_send()

    @pl.when(core == 0)
    def _():
        a_copy(me_p, far).wait_send()
        a_copy(me_p, sib_far).wait_send()

    @pl.when(core == 1)
    def _():
        relay_copy(0, far).wait_send()
        relay_copy(1, sib_far).wait_send()
        relay_on(0, left).wait_send()
        relay_on(1, sib_left).wait_send()


def local(n_ctx, n_pack, *args):
    hidden, keys, values, w_query, w_out, gain, router, routes, order, pattern = args
    tok, width = hidden.shape
    span, heads = keys.shape
    routed = routes.shape[1]
    cap = 3 * tok // 8
    per_slot = routed // n_pack
    both = per_slot + cap
    side = math.isqrt(n_ctx)
    vmem = pl.BlockSpec(memory_space=pltpu.VMEM)
    dma = pltpu.SemaphoreType.DMA
    return pl.pallas_call(
        functools.partial(body, n_ctx, n_pack),
        out_shape=(
            jax.ShapeDtypeStruct((tok, width), BF16),
            jax.ShapeDtypeStruct((per_slot, width), BF16),
        ),
        in_specs=[vmem] + [pl.BlockSpec(memory_space=pl.ANY)] * 4 + [vmem] * 6,
        out_specs=(vmem, vmem),
        scratch_shapes=[
            pltpu.VMEM((n_pack, cap, width), BF16),
            pltpu.VMEM((width, heads), BF16),
            pltpu.VMEM((n_pack * cap, heads), BF16),
            pltpu.VMEM((n_pack * cap, routed), BF16),
            pltpu.VMEM((routed, n_pack * cap), BF16),
            pltpu.VMEM((routed, routed), BF16),
            pltpu.VMEM((routed, HD), F32),
            pltpu.VMEM((2, side, span, HD), BF16),
            pltpu.VMEM((2, side, span, 2 * HD), BF16),
            pltpu.VMEM((2, side, routed, HD), BF16),
            pltpu.VMEM((2, side, routed, HD), BF16),
            pltpu.VMEM((2, side, routed, HD), BF16),
            pltpu.VMEM((2, side, 8, routed), F32),
            pltpu.VMEM((2, side, 8, routed), F32),
            pltpu.VMEM((2, side, routed, HD), F32),
            pltpu.VMEM((2, 2, side, routed, HD), F32),
            pltpu.VMEM((routed, heads), BF16),
            pltpu.VMEM((n_pack * tok, width), BF16),
            pltpu.VMEM((n_pack, both, heads), BF16),
            pltpu.VMEM((n_pack, both, heads), BF16),
            pltpu.VMEM((2, both, heads), BF16),
            pltpu.VMEM((both, width), F32),
            pltpu.VMEM((both, width), F32),
            pltpu.VMEM((both, HD), F32),
            dma((8,)),
            dma((8,)),
            dma((8,)),
            dma((8,)),
            dma((12,)),
            dma((4 * side,)),
            dma((2 * side,)),
            dma((2 * side,)),
            dma((2 * side,)),
            dma((2 * side,)),
            dma((2 * side,)),
            dma((2 * side,)),
            dma((n_pack,)),
            dma((n_pack,)),
            dma((4,)),
            dma((2,)),
            dma,
            dma((5,)),
        ],
        compiler_params=pltpu.CompilerParams(
            collective_id=0, has_side_effects=True, vmem_limit_bytes=60 << 20
        ),
        name="routed_attention",
    )(
        hidden,
        keys,
        values,
        w_query,
        w_out,
        gain.reshape(1, width),
        router.reshape(1, width),
        routes,
        order,
        pattern,
        jnp.asarray(turn_table()),
    )


def solution(mesh):
    return jax.shard_map(
        functools.partial(local, mesh.shape["ctx"], mesh.shape["pack"]),
        mesh=mesh,
        in_specs=(
            P(("ctx", "pack"), None),
            P("ctx", "pack"),
            P("ctx", "pack"),
            P(None, "pack"),
            P("pack", None),
            P(),
            P(),
            P("ctx", None),
            P("ctx", None),
            P(),
        ),
        out_specs=(P(("ctx", "pack"), None), P(("ctx", "pack"), None)),
        check_vma=False,
    )
```

```python
import functools
import math

import jax
import jax.numpy as jnp
import numpy as np
from jax import lax
from jax.experimental import pallas as pl
from jax.experimental.pallas import tpu as pltpu
from jax.sharding import PartitionSpec as P

HD = 128
EPS = 1e-6
NEG = -1e30
F32 = jnp.float32
BF16 = jnp.bfloat16
MESH = pl.DeviceIdType.MESH
LOG2E = 1.4426950408889634


def turn_table():
    lane = np.arange(HD) % (HD // 2)
    turns = 10000.0 ** (-2.0 * lane / HD) / (2.0 * math.pi)
    table = np.zeros((8, HD), np.float32)
    table[0] = np.mod(turns * 128.0, 1.0)
    table[1] = turns
    table[2] = np.where(np.arange(HD) < HD // 2, -1.0, 1.0)
    return table


def cos_sin(pos, table):
    hi = jnp.floor(pos * (1.0 / 128.0))
    low = pos - hi * 128.0
    u = hi * table[0:1]
    u = u - jnp.floor(u) + low * table[1:2]
    u = u - jnp.floor(u + 0.5)
    x = u * math.pi
    y = x * x
    s = 0.0
    for n in (11, 9, 7, 5, 3):
        s = (s + (-1.0) ** ((n - 1) // 2) / math.factorial(n)) * y
    s = (s + 1.0) * x
    c = 0.0
    for n in (12, 10, 8, 6, 4, 2):
        c = (c + (-1.0) ** (n // 2) / math.factorial(n)) * y
    c = c + 1.0
    return 1.0 - 2.0 * s * s, 2.0 * s * c


def body(
    n_ctx,
    n_pack,
    hidden,
    keys,
    values,
    w_query,
    w_out,
    gain,
    router,
    routes,
    order,
    pattern,
    table,
    fresh,
    picked_out,
    rows_all,
    w_q,
    q_pad,
    spread,
    gather,
    slot_of,
    pos_col,
    kbuf,
    vbuf,
    q_buf,
    o_send,
    o_in,
    st_send,
    st_in,
    acc,
    state,
    att,
    w_all,
    a_send,
    a_in,
    relay,
    mix,
    res,
    gate,
    row_send,
    row_recv,
    wo_send,
    wo_recv,
    kv_send,
    kv_recv,
    q_send_sem,
    q_recv_sem,
    o_send_sem,
    o_recv_sem,
    s_send_sem,
    s_recv_sem,
    a_send_sem,
    a_recv_sem,
    r_send_sem,
    r_recv_sem,
    loc_sem,
    kv_sem,
):
    me_c = lax.axis_index("ctx")
    me_p = lax.axis_index("pack")
    tok = hidden.shape[0]
    width = hidden.shape[1]
    span = keys.shape[0]
    routed = routes.shape[1]
    cap = rows_all.shape[1]
    per_slot = routed // n_pack
    half = cap // 2
    sib = me_p + 1 - 2 * lax.rem(me_p, 2)
    right = lax.rem(me_p + 2, n_pack)
    left = lax.rem(me_p + n_pack - 2, n_pack)
    far = lax.rem(me_p + 4, n_pack)
    sib_left = lax.rem(sib + n_pack - 2, n_pack)
    sib_right = lax.rem(sib + 2, n_pack)
    sib_far = lax.rem(sib + 4, n_pack)

    barrier = pltpu.get_barrier_semaphore()

    side = math.isqrt(n_ctx)
    y = me_c // side
    z = lax.rem(me_c, side)
    core = lax.rem(me_p, 2)

    def along_z(step):
        return y * side + lax.rem(z + step, side)

    def along_y(step):
        return lax.rem(y + step, side) * side + z

    def greet(c, p):
        pl.semaphore_signal(barrier, inc=1, device_id=(c, p), device_id_type=MESH)

    def greet_pack(i, _):
        greet(me_c, lax.rem(me_p + i, n_pack))
        return 0

    def greet_ctx(i, _):
        greet(along_y(i), me_p)
        greet(along_z(i), me_p)
        return 0

    lax.fori_loop(1, n_pack, greet_pack, 0)
    lax.fori_loop(1, side, greet_ctx, 0)

    own_w = pltpu.make_async_copy(w_out, w_all.at[pl.ds(me_p * tok, tok)], loc_sem)
    own_q = pltpu.make_async_copy(w_query, w_q, kv_sem.at[4])
    own_k = []
    own_v = []
    for h in range(2):
        cols = pl.ds(h * HD, HD)
        at = (y, z)[h]
        own_k.append(pltpu.make_async_copy(keys.at[:, cols], kbuf.at[h, at], kv_sem.at[h]))
        own_v.append(
            pltpu.make_async_copy(
                values.at[:, cols], vbuf.at[h, at, :, pl.ds(0, HD)], kv_sem.at[2 + h]
            )
        )
    for copy in own_k + own_v + [own_q, own_w]:
        copy.start()

    rf = routes[...].astype(F32)
    lane_i = lax.broadcasted_iota(jnp.int32, (cap, routed), 1).astype(F32)
    sub_j = lax.broadcasted_iota(jnp.int32, (cap, routed), 0).astype(F32)

    def spread_of(block):
        low = (block * tok).astype(F32)
        start = jnp.sum(jnp.where(rf < low, 1.0, 0.0), axis=1, keepdims=True)
        end = jnp.sum(jnp.where(rf < low + tok, 1.0, 0.0), axis=1, keepdims=True)
        hit = jnp.logical_and(lane_i == sub_j + start, lane_i < end)
        pos = jnp.sum(jnp.where(hit, rf + 1.0, 0.0), axis=1, keepdims=True) - 1.0
        return jnp.where(hit, 1.0, 0.0), pos

    _, my_pos = spread_of(me_p)
    lane_t = lax.broadcasted_iota(jnp.int32, (cap, tok), 1).astype(F32)
    pick = jnp.where(lane_t == my_pos - (me_p * tok).astype(F32), 1.0, 0.0).astype(BF16)
    rows_all[me_p] = jnp.dot(pick, hidden[...], preferred_element_type=F32).astype(BF16)

    pl.semaphore_wait(barrier, 2 * (side - 1) + n_pack - 1)

    def row_copy(i, block, sub, peer):
        part = rows_all.at[block] if sub is None else rows_all.at[block, sub]
        return pltpu.make_async_remote_copy(
            src_ref=part,
            dst_ref=part,
            send_sem=row_send.at[i],
            recv_sem=row_recv.at[i],
            device_id=(me_c, peer),
            device_id_type=MESH,
        )

    first = pl.ds(0, half)
    second = pl.ds(half, half)
    to_right = row_copy(0, me_p, None, right)
    to_left = row_copy(1, me_p, None, left)
    to_sib = row_copy(2, me_p, None, sib)
    to_right.start()
    to_left.start()
    to_sib.start()

    key_ring = (along_y, along_z)
    key_at = (y, z)
    ahead = 1 + 2 * core
    behind = side - ahead

    def k_copy(h, j, i, step):
        part = kbuf.at[h, j]
        return pltpu.make_async_remote_copy(
            src_ref=part,
            dst_ref=part,
            send_sem=kv_send.at[h * 3 + i],
            recv_sem=kv_recv.at[h * side + j],
            device_id=(key_ring[h](step), me_p),
            device_id_type=MESH,
        )

    def v_copy(h, j, i, step):
        part = vbuf.at[h, j, :, pl.ds(0, HD)]
        return pltpu.make_async_remote_copy(
            src_ref=part,
            dst_ref=part,
            send_sem=kv_send.at[6 + h * 3 + i],
            recv_sem=kv_recv.at[2 * side + h * side + j],
            device_id=(key_ring[h](step), me_p),
            device_id_type=MESH,
        )

    for h in range(2):
        own_k[h].wait()
        k_copy(h, key_at[h], 0, 1).start()
        k_copy(h, key_at[h], 1, side - 1).start()
    for h in range(2):
        own_v[h].wait()
        v_copy(h, key_at[h], 0, 1).start()
        v_copy(h, key_at[h], 1, side - 1).start()
    for h in range(2):
        for j in range(side):
            vbuf[h, j, :, HD:] = jnp.ones((span, HD), BF16)

    def key_block(h, step):
        return lax.rem(key_at[h] + step, side)


    gain_row = gain[...]
    trig = table[...]
    base = (me_c * span).astype(F32)

    for b in range(n_pack):
        hit, _ = spread_of(jnp.int32(b))
        spread[pl.ds(b * cap, cap), :] = hit.astype(BF16)
    flat = n_pack * cap
    lane_f = lax.broadcasted_iota(jnp.int32, (1, flat), 1).astype(F32)
    start_f = lane_f * 0.0
    end_f = lane_f * 0.0
    for b in range(n_pack):
        inside = jnp.logical_and(lane_f >= b * cap, lane_f < (b + 1) * cap)
        start = jnp.sum(jnp.where(rf < b * tok, 1.0, 0.0), axis=1, keepdims=True)
        end = jnp.sum(jnp.where(rf < (b + 1) * tok, 1.0, 0.0), axis=1, keepdims=True)
        start_f = jnp.where(inside, start + lane_f - b * cap, start_f)
        end_f = jnp.where(inside, end, end_f)
    row_i = lax.broadcasted_iota(jnp.int32, (routed, flat), 0).astype(F32)
    gather[...] = jnp.where(
        jnp.logical_and(row_i == start_f, row_i < end_f), 1.0, 0.0
    ).astype(BF16)
    pos_col[...] = jnp.transpose(jnp.broadcast_to(rf, (HD, routed)))
    order_col = jnp.transpose(jnp.broadcast_to(order[...].astype(F32), (HD, routed)))[:, 0:1]
    lane_s = lax.broadcasted_iota(jnp.int32, (routed, routed), 1).astype(F32)
    slot_of[...] = jnp.where(lane_s == order_col, 1.0, 0.0).astype(BF16)

    scale = LOG2E / math.sqrt(HD)

    def project(block):
        rows = rows_all[block].astype(F32)
        mean_square = jnp.mean(rows * rows, axis=1, keepdims=True)
        normed = (rows * lax.rsqrt(mean_square + EPS) * gain_row).astype(BF16)
        proj = jnp.dot(normed, w_q[...], preferred_element_type=F32)
        _, pos = spread_of(block)
        cosine, sine = cos_sin(pos + base, trig)
        sine = sine * trig[2:3]
        start = pl.multiple_of(block * cap, cap)
        for h in range(2):
            part = proj[:, h * HD : (h + 1) * HD]
            turned = part * cosine + pltpu.roll(part, HD // 2, 1) * sine
            q_pad[pl.ds(start, cap), h * HD : (h + 1) * HD] = (turned * scale).astype(BF16)

    own_q.wait()
    project(me_p)
    row_copy(0, left, None, right).wait_recv()
    fwd_right = row_copy(3, left, first, right)
    fwd_right.start()
    fwd_sib_left = row_copy(4, left, None, sib)
    fwd_sib_left.start()
    row_copy(1, right, None, left).wait_recv()
    fwd_left = row_copy(5, right, second, left)
    fwd_left.start()
    fwd_sib_right = row_copy(6, right, None, sib)
    fwd_sib_right.start()
    project(left)
    project(right)
    row_copy(2, sib, None, sib).wait_recv()
    project(sib)
    row_copy(4, sib_left, None, sib).wait_recv()
    project(sib_left)
    row_copy(6, sib_right, None, sib).wait_recv()
    project(sib_right)
    row_copy(3, far, first, right).wait_recv()
    row_copy(5, far, second, left).wait_recv()
    fwd_sib_far = row_copy(7, far, None, sib)
    fwd_sib_far.start()
    w_half = tok // 2

    def w_copy(i, block, lo, size, peer):
        part = w_all.at[pl.ds(block * tok + lo, size)]
        return pltpu.make_async_remote_copy(
            src_ref=part,
            dst_ref=part,
            send_sem=wo_send.at[i],
            recv_sem=wo_recv.at[i],
            device_id=(me_c, peer),
            device_id_type=MESH,
        )

    own_w.wait()
    w_copy(0, me_p, 0, tok, right).start()
    w_copy(1, me_p, 0, tok, left).start()

    project(far)
    row_copy(7, sib_far, None, sib).wait_recv()
    project(sib_far)

    query = jnp.dot(gather[...], q_pad[...], preferred_element_type=F32).astype(BF16)
    q_buf[0, z] = query[:, 0:HD]
    q_buf[1, y] = query[:, HD:]
    q_ring = (along_z, along_y)
    q_at = (z, y)

    def q_copy(h, src, step):
        return pltpu.make_async_remote_copy(
            src_ref=q_buf.at[h, src],
            dst_ref=q_buf.at[h, src],
            send_sem=q_send_sem.at[h * side + step],
            recv_sem=q_recv_sem.at[h * side + src],
            device_id=(q_ring[h](step), me_p),
            device_id_type=MESH,
        )

    for step in (1, 3):
        for h in range(2):
            q_copy(h, q_at[h], step).start()
    w_copy(2, me_p, 0, tok, sib).start()

    def q_forward(h):
        src = lax.rem(q_at[h] + behind, side)
        return pltpu.make_async_remote_copy(
            src_ref=q_buf.at[h, src],
            dst_ref=q_buf.at[h, src],
            send_sem=q_send_sem.at[h * side + 2],
            recv_sem=q_recv_sem.at[h * side + src],
            device_id=(q_ring[h](ahead), me_p),
            device_id_type=MESH,
        )

    chunk = 512
    tile = 256
    def less(a, b):
        return (b - a + side - 1) // side

    def same(a, b):
        return 1 - less(a, b) - less(b, a)

    def blend(h, one, two):
        return one + h * (two - one)

    def step_in(h, t, j, own):
        if own:
            lane_k = lax.broadcasted_iota(jnp.int32, (tile, chunk), 1).astype(F32)
        else:
            span_q = blend(h, y * side + t, t * side + z)
            span_k = blend(h, j * side + z, y * side + j)
            wanted = pattern[pl.ds(span_q, 1), :]
            hit = jnp.max(jnp.where(wanted == span_k, 1.0, 0.0), axis=1, keepdims=True)

        def score(r, i):
            s = lax.dot_general(
                q_buf[h, t, r : r + tile, :],
                kbuf[h, j, i : i + chunk, :],
                (((1,), (1,)), ((), ())),
                preferred_element_type=F32,
            )
            if own:
                s = jnp.where(lane_k <= pos_col[r : r + tile, 0:1] - float(i), s, NEG)
            return s

        def starts(r):
            if not own:
                return list(range(0, span, chunk))
            return [
                i
                for i in range(0, span, chunk)
                if r + tile > routed - cap * pl.cdiv(span - i, tok)
            ]

        scores = [score(0, i) for i in starts(0)]
        for r in range(0, routed, tile):
            peak = functools.reduce(
                jnp.maximum, [jnp.max(s, axis=1, keepdims=True) for s in scores]
            )
            later = []
            ahead_of = starts(r + tile) if r + tile < routed else []
            out = 0.0
            for n, i in enumerate(starts(r)):
                if n < len(ahead_of):
                    later.append(score(r + tile, ahead_of[n]))
                weights = jnp.exp2(scores[n] - peak).astype(BF16)
                out = out + jnp.dot(
                    weights, vbuf[h, j, i : i + chunk, :], preferred_element_type=F32
                )
            for i in ahead_of[len(later) :]:
                later.append(score(r + tile, i))
            rows = slice(r, r + tile)
            if own:
                acc[h, t, rows, :] = out[:, 0:HD]
                state[0, h, t, rows, :] = jnp.broadcast_to(peak, (tile, HD))
                state[1, h, t, rows, :] = out[:, HD:]
            else:
                peak = jnp.where(hit > 0.5, peak, NEG)
                former = state[0, h, t, rows, :]
                top = jnp.maximum(former, peak)
                a = jnp.exp2(former - top)
                b = jnp.exp2(peak - top) * hit
                acc[h, t, rows, :] = acc[h, t, rows, :] * a + out[:, 0:HD] * b
                state[0, h, t, rows, :] = top
                state[1, h, t, rows, :] = state[1, h, t, rows, :] * a + out[:, HD:] * b
            scores = later

    def slot(h, step):
        return lax.rem(blend(h, z, y) + step, side)

    def block(h, step):
        return lax.rem(blend(h, y, z) + step, side)

    def sees(h, t, j):
        by_row = less(j, y) + same(j, y) * less(z, t)
        by_col = less(y, t) + same(y, t) * less(j, z)
        return blend(h, by_row, by_col)

    def begin(h, _):
        for step in range(1, side):
            t = slot(h, step)
            acc[h, t] = jnp.zeros((routed, HD), F32)
            state[0, h, t] = jnp.full((routed, HD), NEG, F32)
            state[1, h, t] = jnp.zeros((routed, HD), F32)
        step_in(h, slot(h, 0), block(h, 0), True)
        return 0

    lax.fori_loop(0, 2, begin, 0)

    for h in range(2):
        q_copy(h, lax.rem(q_at[h] + behind, side), behind).wait_recv()
        q_forward(h).start()
    for h in range(2):
        q_copy(h, lax.rem(q_at[h] + ahead, side), ahead).wait_recv()

    def own_block(i, _):
        h = lax.rem(i, 2)
        turn = i // 2
        t = slot(h, turn + turn // 2 - 2 * (turn // 3))
        j = block(h, 0)

        @pl.when(sees(h, t, j) == 1)
        def _():
            step_in(h, t, j, False)

        return 0

    lax.fori_loop(2, 6, own_block, 0)

    for h in range(2):
        k_copy(h, key_block(h, behind), 0, behind).wait_recv()
        k_copy(h, key_block(h, behind), 2, ahead).start()
        v_copy(h, key_block(h, behind), 0, behind).wait_recv()
        v_copy(h, key_block(h, behind), 2, ahead).start()
    for h in range(2):
        q_copy(h, lax.rem(q_at[h] + 2, side), behind).wait_recv()

    lax.fori_loop(6, 8, own_block, 0)

    for h in range(2):
        k_copy(h, key_block(h, ahead), 0, ahead).wait_recv()
        v_copy(h, key_block(h, ahead), 0, ahead).wait_recv()

    def near_blocks(i, _):
        h = lax.rem(i, 2)
        turn = lax.rem(i // 2, side)
        t = slot(h, turn + turn // 2 - 2 * (turn // 3))
        j = block(h, 1 + 2 * (i // (2 * side)))

        @pl.when(sees(h, t, j) == 1)
        def _():
            step_in(h, t, j, False)

        return 0

    lax.fori_loop(0, 3 * side, near_blocks, 0)

    w_copy(0, left, 0, tok, right).wait_recv()
    w_copy(3, left, 0, w_half, right).start()
    w_copy(4, left, 0, tok, sib).start()
    w_copy(1, right, 0, tok, left).wait_recv()
    w_copy(5, right, w_half, w_half, left).start()
    w_copy(6, right, 0, tok, sib).start()

    lax.fori_loop(3 * side, 4 * side, near_blocks, 0)

    for h in range(2):
        k_copy(h, key_block(h, 2), 0, behind).wait_recv()
        v_copy(h, key_block(h, 2), 0, behind).wait_recv()

    def o_copy(h, src, dst):
        return pltpu.make_async_remote_copy(
            src_ref=o_send.at[h, dst],
            dst_ref=o_in.at[h, src],
            send_sem=o_send_sem.at[h * side + dst],
            recv_sem=o_recv_sem.at[h * side + src],
            device_id=(blend(h, y * side + dst, dst * side + z), me_p),
            device_id_type=MESH,
        )

    def s_copy(h, src, dst):
        return pltpu.make_async_remote_copy(
            src_ref=st_send.at[h, dst],
            dst_ref=st_in.at[h, src],
            send_sem=s_send_sem.at[h * side + dst],
            recv_sem=s_recv_sem.at[h * side + src],
            device_id=(blend(h, y * side + dst, dst * side + z), me_p),
            device_id_type=MESH,
        )

    def far_block(i, _):
        h = lax.rem(i, 2)
        turn = i // 2
        step = lax.rem(turn + 1, side - 1) + 1
        at = slot(h, 0)
        t = slot(h, step)
        j = block(h, 2)

        @pl.when(sees(h, t, j) == 1)
        def _():
            step_in(h, t, j, False)

        den = state[1, h, t]
        o_send[h, t] = (acc[h, t] / jnp.where(den > 0.0, den, 1.0)).astype(BF16)
        lse = jnp.where(den > 0.0, state[0, h, t] + jnp.log2(den), NEG)
        st_send[h, t] = jnp.transpose(lse)[0:8]
        o_copy(h, at, t).start()
        s_copy(h, at, t).start()
        return 0

    lax.fori_loop(0, 2 * (side - 1), far_block, 0)

    def far_own(h, _):
        t = slot(h, 0)
        j = block(h, 2)

        @pl.when(sees(h, t, j) == 1)
        def _():
            step_in(h, t, j, False)

        return 0

    lax.fori_loop(0, 2, far_own, 0)


    slot_rows = pl.ds(pl.multiple_of(me_p * per_slot, per_slot), per_slot)
    from_pad = jnp.dot(
        slot_of[slot_rows, :], gather[...], preferred_element_type=F32
    ).astype(BF16)
    for n in range(0, width, 512):
        picked = 0.0
        for b in range(n_pack):
            picked = picked + jnp.dot(
                from_pad[:, b * cap : (b + 1) * cap],
                rows_all[b, :, n : n + 512],
                preferred_element_type=F32,
            )
        res[0:per_slot, n : n + 512] = picked
    res[per_slot:, :] = rows_all[me_p].astype(F32)
    gate[...] = jnp.broadcast_to(
        jax.nn.sigmoid(jnp.sum(res[...] * router[...], axis=1, keepdims=True)), gate.shape
    )

    for h in range(2):
        peak, den = state[0, h, q_at[h]], state[1, h, q_at[h]]
        total = acc[h, q_at[h]]
        for step in (2, 1, 3):
            src = lax.rem(q_at[h] + step, side)
            o_copy(h, src, q_at[h]).wait_recv()
            s_copy(h, src, q_at[h]).wait_recv()
            lse = jnp.transpose(jnp.broadcast_to(st_in[h, src, 0:1, :], (HD, routed)))
            top = jnp.maximum(peak, lse)
            a = jnp.exp2(peak - top)
            b = jnp.exp2(lse - top)
            total = total * a + o_in[h, src].astype(F32) * b
            peak, den = top, den * a + b
        att[:, h * HD : (h + 1) * HD] = (total / den).astype(BF16)

    by_slot = jnp.dot(slot_of[...], att[...], preferred_element_type=F32).astype(BF16)
    by_owner = jnp.dot(spread[...], att[...], preferred_element_type=F32).astype(BF16)
    for d in range(n_pack):
        a_send[d, 0:per_slot, :] = by_slot[d * per_slot : (d + 1) * per_slot]
        a_send[d, per_slot:, :] = by_owner[d * cap : (d + 1) * cap]

    def a_copy(src, dst):
        return pltpu.make_async_remote_copy(
            src_ref=a_send.at[dst],
            dst_ref=a_in.at[src],
            send_sem=a_send_sem.at[dst],
            recv_sem=a_recv_sem.at[src],
            device_id=(me_c, dst),
            device_id_type=MESH,
        )

    def relay_copy(i, dst):
        return pltpu.make_async_remote_copy(
            src_ref=a_send.at[dst],
            dst_ref=relay.at[i],
            send_sem=r_send_sem.at[i],
            recv_sem=r_recv_sem.at[i],
            device_id=(me_c, left),
            device_id_type=MESH,
        )

    def relay_on(i, dst):
        return pltpu.make_async_remote_copy(
            src_ref=relay.at[i],
            dst_ref=a_in.at[right],
            send_sem=r_send_sem.at[2 + i],
            recv_sem=a_recv_sem.at[right],
            device_id=(me_c, dst),
            device_id_type=MESH,
        )

    @pl.when(core == 0)
    def _():
        a_copy(me_p, far).start()
        a_copy(me_p, sib_far).start()

    @pl.when(core == 1)
    def _():
        relay_copy(0, far).start()
        relay_copy(1, sib_far).start()

    a_copy(me_p, right).start()
    a_copy(me_p, left).start()
    a_copy(me_p, sib_right).start()
    a_copy(me_p, sib_left).start()
    a_copy(me_p, sib).start()

    def add(rows, b, first):
        for n in range(0, width, 512):
            cols = slice(n, n + 512)
            part = jnp.dot(
                rows, w_all[pl.ds(b * tok, tok), cols], preferred_element_type=F32
            )
            mix[:, cols] = part if first else mix[:, cols] + part

    w_copy(3, far, 0, w_half, right).wait_recv()
    w_copy(5, far, w_half, w_half, left).wait_recv()
    w_copy(7, far, 0, tok, sib).start()

    add(a_send[me_p], me_p, True)
    w_copy(2, sib, 0, tok, sib).wait_recv()
    a_copy(sib, me_p).wait_recv()
    add(a_in[sib], sib, False)

    @pl.when(core == 1)
    def _():
        relay_copy(0, far).wait_recv()
        relay_on(0, left).start()
        relay_copy(1, sib_far).wait_recv()
        relay_on(1, sib_left).start()

    late = {2: (6, sib_right), 3: (4, sib_left), 5: (7, sib_far)}
    for n, b in enumerate((right, left, sib_right, sib_left, far, sib_far)):
        if n in late:
            w_copy(late[n][0], late[n][1], 0, tok, sib).wait_recv()
        a_copy(b, me_p).wait_recv()
        add(a_in[b], b, False)

    picked_out[...] = pick
    for n in range(0, width, 512):
        cols = slice(n, n + 512)
        updated = (res[:, cols] + gate[:, 0:1] * mix[:, cols]).astype(BF16)
        fresh[:, cols] = updated

    to_right.wait_send()
    to_left.wait_send()
    to_sib.wait_send()
    fwd_right.wait_send()
    fwd_left.wait_send()
    fwd_sib_left.wait_send()
    fwd_sib_right.wait_send()
    fwd_sib_far.wait_send()
    w_copy(0, me_p, 0, tok, right).wait_send()
    w_copy(1, me_p, 0, tok, left).wait_send()
    w_copy(2, me_p, 0, tok, sib).wait_send()
    w_copy(3, left, 0, w_half, right).wait_send()
    w_copy(4, left, 0, tok, sib).wait_send()
    w_copy(5, right, w_half, w_half, left).wait_send()
    w_copy(6, right, 0, tok, sib).wait_send()
    w_copy(7, far, 0, tok, sib).wait_send()

    for h in range(2):
        k_copy(h, key_at[h], 0, 1).wait_send()
        k_copy(h, key_at[h], 1, side - 1).wait_send()
        k_copy(h, key_block(h, behind), 2, ahead).wait_send()
        v_copy(h, key_at[h], 0, 1).wait_send()
        v_copy(h, key_at[h], 1, side - 1).wait_send()
        v_copy(h, key_block(h, behind), 2, ahead).wait_send()
        q_copy(h, q_at[h], 1).wait_send()
        q_copy(h, q_at[h], 3).wait_send()
        q_forward(h).wait_send()
        for step in (1, 2, 3):
            dst = lax.rem(q_at[h] + step, side)
            o_copy(h, q_at[h], dst).wait_send()
            s_copy(h, q_at[h], dst).wait_send()

    a_copy(me_p, right).wait_send()
    a_copy(me_p, left).wait_send()
    a_copy(me_p, sib_right).wait_send()
    a_copy(me_p, sib_left).wait_send()
    a_copy(me_p, sib).wait_send()

    @pl.when(core == 0)
    def _():
        a_copy(me_p, far).wait_send()
        a_copy(me_p, sib_far).wait_send()

    @pl.when(core == 1)
    def _():
        relay_copy(0, far).wait_send()
        relay_copy(1, sib_far).wait_send()
        relay_on(0, left).wait_send()
        relay_on(1, sib_left).wait_send()


def place(hidden, fresh, pick, hidden_out, packed):
    per_slot = packed.shape[0]
    across = (((0,), (0,)), ((), ()))
    chosen = pick[...]
    present = lax.dot_general(
        chosen, jnp.ones((chosen.shape[0], HD), BF16), across, preferred_element_type=F32
    )[:, 0:1]
    placed = lax.dot_general(chosen, fresh[per_slot:, :], across, preferred_element_type=F32)
    hidden_out[...] = jnp.where(present > 0.5, placed.astype(BF16), hidden[...])
    packed[...] = fresh[0:per_slot, :]


def local(n_ctx, n_pack, *args):
    hidden, keys, values, w_query, w_out, gain, router, routes, order, pattern = args
    tok, width = hidden.shape
    span, heads = keys.shape
    routed = routes.shape[1]
    cap = 3 * tok // 8
    per_slot = routed // n_pack
    both = per_slot + cap
    side = math.isqrt(n_ctx)
    vmem = pl.BlockSpec(memory_space=pltpu.VMEM)
    dma = pltpu.SemaphoreType.DMA
    fresh, pick = pl.pallas_call(
        functools.partial(body, n_ctx, n_pack),
        out_shape=(
            jax.ShapeDtypeStruct((both, width), BF16),
            jax.ShapeDtypeStruct((cap, tok), BF16),
        ),
        in_specs=[vmem] + [pl.BlockSpec(memory_space=pl.ANY)] * 4 + [vmem] * 6,
        out_specs=(vmem, vmem),
        scratch_shapes=[
            pltpu.VMEM((n_pack, cap, width), BF16),
            pltpu.VMEM((width, heads), BF16),
            pltpu.VMEM((n_pack * cap, heads), BF16),
            pltpu.VMEM((n_pack * cap, routed), BF16),
            pltpu.VMEM((routed, n_pack * cap), BF16),
            pltpu.VMEM((routed, routed), BF16),
            pltpu.VMEM((routed, HD), F32),
            pltpu.VMEM((2, side, span, HD), BF16),
            pltpu.VMEM((2, side, span, 2 * HD), BF16),
            pltpu.VMEM((2, side, routed, HD), BF16),
            pltpu.VMEM((2, side, routed, HD), BF16),
            pltpu.VMEM((2, side, routed, HD), BF16),
            pltpu.VMEM((2, side, 8, routed), F32),
            pltpu.VMEM((2, side, 8, routed), F32),
            pltpu.VMEM((2, side, routed, HD), F32),
            pltpu.VMEM((2, 2, side, routed, HD), F32),
            pltpu.VMEM((routed, heads), BF16),
            pltpu.VMEM((n_pack * tok, width), BF16),
            pltpu.VMEM((n_pack, both, heads), BF16),
            pltpu.VMEM((n_pack, both, heads), BF16),
            pltpu.VMEM((2, both, heads), BF16),
            pltpu.VMEM((both, width), F32),
            pltpu.VMEM((both, width), F32),
            pltpu.VMEM((both, HD), F32),
            dma((8,)),
            dma((8,)),
            dma((8,)),
            dma((8,)),
            dma((12,)),
            dma((4 * side,)),
            dma((2 * side,)),
            dma((2 * side,)),
            dma((2 * side,)),
            dma((2 * side,)),
            dma((2 * side,)),
            dma((2 * side,)),
            dma((n_pack,)),
            dma((n_pack,)),
            dma((4,)),
            dma((2,)),
            dma,
            dma((5,)),
        ],
        compiler_params=pltpu.CompilerParams(
            collective_id=0, has_side_effects=True, vmem_limit_bytes=60 << 20
        ),
        name="routed_attention",
    )(
        hidden,
        keys,
        values,
        w_query,
        w_out,
        gain.reshape(1, width),
        router.reshape(1, width),
        routes,
        order,
        pattern,
        jnp.asarray(turn_table()),
    )
    step = 1024
    return pl.pallas_call(
        place,
        grid=(width // step,),
        out_shape=(
            jax.ShapeDtypeStruct((tok, width), BF16),
            jax.ShapeDtypeStruct((per_slot, width), BF16),
        ),
        in_specs=[
            pl.BlockSpec((tok, step), lambda n: (0, n)),
            pl.BlockSpec((both, step), lambda n: (0, n)),
            pl.BlockSpec((cap, tok), lambda n: (0, 0)),
        ],
        out_specs=(
            pl.BlockSpec((tok, step), lambda n: (0, n)),
            pl.BlockSpec((per_slot, step), lambda n: (0, n)),
        ),
        name="place_rows",
    )(hidden, fresh, pick)


def solution(mesh):
    return jax.shard_map(
        functools.partial(local, mesh.shape["ctx"], mesh.shape["pack"]),
        mesh=mesh,
        in_specs=(
            P(("ctx", "pack"), None),
            P("ctx", "pack"),
            P("ctx", "pack"),
            P(None, "pack"),
            P("pack", None),
            P(),
            P(),
            P("ctx", None),
            P("ctx", None),
            P(),
        ),
        out_specs=(P(("ctx", "pack"), None), P(("ctx", "pack"), None)),
        check_vma=False,
    )
```

```python
import functools
import math

import jax
import jax.numpy as jnp
import numpy as np
from jax import lax
from jax.experimental import pallas as pl
from jax.experimental.pallas import tpu as pltpu
from jax.sharding import PartitionSpec as P

HD = 128
EPS = 1e-6
NEG = -1e30
F32 = jnp.float32
BF16 = jnp.bfloat16
MESH = pl.DeviceIdType.MESH
LOG2E = 1.4426950408889634


def turn_table():
    lane = np.arange(HD) % (HD // 2)
    turns = 10000.0 ** (-2.0 * lane / HD) / (2.0 * math.pi)
    table = np.zeros((8, HD), np.float32)
    table[0] = np.mod(turns * 128.0, 1.0)
    table[1] = turns
    table[2] = np.where(np.arange(HD) < HD // 2, -1.0, 1.0)
    return table


def cos_sin(pos, table):
    hi = jnp.floor(pos * (1.0 / 128.0))
    low = pos - hi * 128.0
    u = hi * table[0:1]
    u = u - jnp.floor(u) + low * table[1:2]
    u = u - jnp.floor(u + 0.5)
    x = u * math.pi
    y = x * x
    s = 0.0
    for n in (11, 9, 7, 5, 3):
        s = (s + (-1.0) ** ((n - 1) // 2) / math.factorial(n)) * y
    s = (s + 1.0) * x
    c = 0.0
    for n in (12, 10, 8, 6, 4, 2):
        c = (c + (-1.0) ** (n // 2) / math.factorial(n)) * y
    c = c + 1.0
    return 1.0 - 2.0 * s * s, 2.0 * s * c


def body(
    n_ctx,
    n_pack,
    hidden,
    keys,
    values,
    w_query,
    w_out,
    gain,
    router,
    routes,
    order,
    pattern,
    table,
    fresh,
    picked_out,
    rows_all,
    w_q,
    q_pad,
    spread,
    gather,
    slot_of,
    pos_col,
    kbuf,
    vbuf,
    q_buf,
    o_send,
    o_in,
    st_send,
    st_in,
    acc,
    state,
    att,
    w_all,
    a_send,
    a_in,
    relay,
    mix,
    res,
    gate,
    row_send,
    row_recv,
    wo_send,
    wo_recv,
    kv_send,
    kv_recv,
    q_send_sem,
    q_recv_sem,
    o_send_sem,
    o_recv_sem,
    s_send_sem,
    s_recv_sem,
    a_send_sem,
    a_recv_sem,
    r_send_sem,
    r_recv_sem,
    loc_sem,
    kv_sem,
):
    me_c = lax.axis_index("ctx")
    me_p = lax.axis_index("pack")
    tok = hidden.shape[0]
    width = hidden.shape[1]
    span = keys.shape[0]
    routed = routes.shape[1]
    cap = rows_all.shape[1]
    per_slot = routed // n_pack
    half = cap // 2
    sib = me_p + 1 - 2 * lax.rem(me_p, 2)
    right = lax.rem(me_p + 2, n_pack)
    left = lax.rem(me_p + n_pack - 2, n_pack)
    far = lax.rem(me_p + 4, n_pack)
    sib_left = lax.rem(sib + n_pack - 2, n_pack)
    sib_right = lax.rem(sib + 2, n_pack)
    sib_far = lax.rem(sib + 4, n_pack)

    barrier = pltpu.get_barrier_semaphore()

    side = math.isqrt(n_ctx)
    y = me_c // side
    z = lax.rem(me_c, side)
    core = lax.rem(me_p, 2)

    def along_z(step):
        return y * side + lax.rem(z + step, side)

    def along_y(step):
        return lax.rem(y + step, side) * side + z

    def greet(c, p):
        pl.semaphore_signal(barrier, inc=1, device_id=(c, p), device_id_type=MESH)

    def greet_pack(i, _):
        greet(me_c, lax.rem(me_p + i, n_pack))
        return 0

    def greet_ctx(i, _):
        greet(along_y(i), me_p)
        greet(along_z(i), me_p)
        return 0

    lax.fori_loop(1, n_pack, greet_pack, 0)
    lax.fori_loop(1, side, greet_ctx, 0)

    own_w = pltpu.make_async_copy(w_out, w_all.at[pl.ds(me_p * tok, tok)], loc_sem)
    own_q = pltpu.make_async_copy(w_query, w_q, kv_sem.at[4])
    own_k = []
    own_v = []
    for h in range(2):
        cols = pl.ds(h * HD, HD)
        at = (y, z)[h]
        own_k.append(pltpu.make_async_copy(keys.at[:, cols], kbuf.at[h, at], kv_sem.at[h]))
        own_v.append(
            pltpu.make_async_copy(
                values.at[:, cols], vbuf.at[h, at, :, pl.ds(0, HD)], kv_sem.at[2 + h]
            )
        )
    for copy in own_k + own_v + [own_q, own_w]:
        copy.start()

    rf = routes[...].astype(F32)
    lane_i = lax.broadcasted_iota(jnp.int32, (cap, routed), 1).astype(F32)
    sub_j = lax.broadcasted_iota(jnp.int32, (cap, routed), 0).astype(F32)

    def spread_of(block):
        low = (block * tok).astype(F32)
        start = jnp.sum(jnp.where(rf < low, 1.0, 0.0), axis=1, keepdims=True)
        end = jnp.sum(jnp.where(rf < low + tok, 1.0, 0.0), axis=1, keepdims=True)
        hit = jnp.logical_and(lane_i == sub_j + start, lane_i < end)
        pos = jnp.sum(jnp.where(hit, rf + 1.0, 0.0), axis=1, keepdims=True) - 1.0
        return jnp.where(hit, 1.0, 0.0), pos

    _, my_pos = spread_of(me_p)
    lane_t = lax.broadcasted_iota(jnp.int32, (cap, tok), 1).astype(F32)
    pick = jnp.where(lane_t == my_pos - (me_p * tok).astype(F32), 1.0, 0.0).astype(BF16)
    rows_all[me_p] = jnp.dot(pick, hidden[...], preferred_element_type=F32).astype(BF16)

    pl.semaphore_wait(barrier, 2 * (side - 1) + n_pack - 1)

    def row_copy(i, block, sub, peer):
        part = rows_all.at[block] if sub is None else rows_all.at[block, sub]
        return pltpu.make_async_remote_copy(
            src_ref=part,
            dst_ref=part,
            send_sem=row_send.at[i],
            recv_sem=row_recv.at[i],
            device_id=(me_c, peer),
            device_id_type=MESH,
        )

    first = pl.ds(0, half)
    second = pl.ds(half, half)
    to_right = row_copy(0, me_p, None, right)
    to_left = row_copy(1, me_p, None, left)
    to_sib = row_copy(2, me_p, None, sib)
    to_right.start()
    to_left.start()
    to_sib.start()

    key_ring = (along_y, along_z)
    key_at = (y, z)
    ahead = 1 + 2 * core
    behind = side - ahead

    def k_copy(h, j, i, step):
        part = kbuf.at[h, j]
        return pltpu.make_async_remote_copy(
            src_ref=part,
            dst_ref=part,
            send_sem=kv_send.at[h * 3 + i],
            recv_sem=kv_recv.at[h * side + j],
            device_id=(key_ring[h](step), me_p),
            device_id_type=MESH,
        )

    def v_copy(h, j, i, step):
        part = vbuf.at[h, j, :, pl.ds(0, HD)]
        return pltpu.make_async_remote_copy(
            src_ref=part,
            dst_ref=part,
            send_sem=kv_send.at[6 + h * 3 + i],
            recv_sem=kv_recv.at[2 * side + h * side + j],
            device_id=(key_ring[h](step), me_p),
            device_id_type=MESH,
        )

    for h in range(2):
        own_k[h].wait()
        k_copy(h, key_at[h], 0, 1).start()
        k_copy(h, key_at[h], 1, side - 1).start()
    for h in range(2):
        own_v[h].wait()
        v_copy(h, key_at[h], 0, 1).start()
        v_copy(h, key_at[h], 1, side - 1).start()
    for h in range(2):
        for j in range(side):
            vbuf[h, j, :, HD:] = jnp.ones((span, HD), BF16)

    def key_block(h, step):
        return lax.rem(key_at[h] + step, side)


    gain_row = gain[...]
    trig = table[...]
    base = (me_c * span).astype(F32)

    for b in range(n_pack):
        hit, _ = spread_of(jnp.int32(b))
        spread[pl.ds(b * cap, cap), :] = hit.astype(BF16)
    flat = n_pack * cap
    lane_f = lax.broadcasted_iota(jnp.int32, (1, flat), 1).astype(F32)
    start_f = lane_f * 0.0
    end_f = lane_f * 0.0
    for b in range(n_pack):
        inside = jnp.logical_and(lane_f >= b * cap, lane_f < (b + 1) * cap)
        start = jnp.sum(jnp.where(rf < b * tok, 1.0, 0.0), axis=1, keepdims=True)
        end = jnp.sum(jnp.where(rf < (b + 1) * tok, 1.0, 0.0), axis=1, keepdims=True)
        start_f = jnp.where(inside, start + lane_f - b * cap, start_f)
        end_f = jnp.where(inside, end, end_f)
    row_i = lax.broadcasted_iota(jnp.int32, (routed, flat), 0).astype(F32)
    gather[...] = jnp.where(
        jnp.logical_and(row_i == start_f, row_i < end_f), 1.0, 0.0
    ).astype(BF16)
    pos_col[...] = jnp.transpose(jnp.broadcast_to(rf, (HD, routed)))
    order_col = jnp.transpose(jnp.broadcast_to(order[...].astype(F32), (HD, routed)))[:, 0:1]
    lane_s = lax.broadcasted_iota(jnp.int32, (routed, routed), 1).astype(F32)
    slot_of[...] = jnp.where(lane_s == order_col, 1.0, 0.0).astype(BF16)

    scale = LOG2E / math.sqrt(HD)

    def project(block):
        rows = rows_all[block].astype(F32)
        mean_square = jnp.mean(rows * rows, axis=1, keepdims=True)
        normed = (rows * lax.rsqrt(mean_square + EPS) * gain_row).astype(BF16)
        proj = jnp.dot(normed, w_q[...], preferred_element_type=F32)
        _, pos = spread_of(block)
        cosine, sine = cos_sin(pos + base, trig)
        sine = sine * trig[2:3]
        start = pl.multiple_of(block * cap, cap)
        for h in range(2):
            part = proj[:, h * HD : (h + 1) * HD]
            turned = part * cosine + pltpu.roll(part, HD // 2, 1) * sine
            q_pad[pl.ds(start, cap), h * HD : (h + 1) * HD] = (turned * scale).astype(BF16)

    own_q.wait()
    project(me_p)
    row_copy(0, left, None, right).wait_recv()
    fwd_right = row_copy(3, left, first, right)
    fwd_right.start()
    fwd_sib_left = row_copy(4, left, None, sib)
    fwd_sib_left.start()
    row_copy(1, right, None, left).wait_recv()
    fwd_left = row_copy(5, right, second, left)
    fwd_left.start()
    fwd_sib_right = row_copy(6, right, None, sib)
    fwd_sib_right.start()
    project(left)
    project(right)
    row_copy(2, sib, None, sib).wait_recv()
    project(sib)
    row_copy(4, sib_left, None, sib).wait_recv()
    project(sib_left)
    row_copy(6, sib_right, None, sib).wait_recv()
    project(sib_right)
    row_copy(3, far, first, right).wait_recv()
    row_copy(5, far, second, left).wait_recv()
    fwd_sib_far = row_copy(7, far, None, sib)
    fwd_sib_far.start()
    w_half = tok // 2

    def w_copy(i, block, lo, size, peer):
        part = w_all.at[pl.ds(block * tok + lo, size)]
        return pltpu.make_async_remote_copy(
            src_ref=part,
            dst_ref=part,
            send_sem=wo_send.at[i],
            recv_sem=wo_recv.at[i],
            device_id=(me_c, peer),
            device_id_type=MESH,
        )

    own_w.wait()
    w_copy(0, me_p, 0, tok, right).start()
    w_copy(1, me_p, 0, tok, left).start()

    project(far)
    row_copy(7, sib_far, None, sib).wait_recv()
    project(sib_far)

    query = jnp.dot(gather[...], q_pad[...], preferred_element_type=F32).astype(BF16)
    q_buf[0, z] = query[:, 0:HD]
    q_buf[1, y] = query[:, HD:]
    q_ring = (along_z, along_y)
    q_at = (z, y)

    def q_copy(h, src, step):
        return pltpu.make_async_remote_copy(
            src_ref=q_buf.at[h, src],
            dst_ref=q_buf.at[h, src],
            send_sem=q_send_sem.at[h * side + step],
            recv_sem=q_recv_sem.at[h * side + src],
            device_id=(q_ring[h](step), me_p),
            device_id_type=MESH,
        )

    for step in (1, 3):
        for h in range(2):
            q_copy(h, q_at[h], step).start()
    w_copy(2, me_p, 0, tok, sib).start()

    def q_forward(h):
        src = lax.rem(q_at[h] + behind, side)
        return pltpu.make_async_remote_copy(
            src_ref=q_buf.at[h, src],
            dst_ref=q_buf.at[h, src],
            send_sem=q_send_sem.at[h * side + 2],
            recv_sem=q_recv_sem.at[h * side + src],
            device_id=(q_ring[h](ahead), me_p),
            device_id_type=MESH,
        )

    chunk = 512
    tile = 256
    def less(a, b):
        return (b - a + side - 1) // side

    def same(a, b):
        return 1 - less(a, b) - less(b, a)

    def blend(h, one, two):
        return one + h * (two - one)

    def step_in(h, t, j, own):
        if own:
            lane_k = lax.broadcasted_iota(jnp.int32, (tile, chunk), 1).astype(F32)
        else:
            span_q = blend(h, y * side + t, t * side + z)
            span_k = blend(h, j * side + z, y * side + j)
            wanted = pattern[pl.ds(span_q, 1), :]
            hit = jnp.max(jnp.where(wanted == span_k, 1.0, 0.0), axis=1, keepdims=True)

        def score(r, i):
            s = lax.dot_general(
                q_buf[h, t, r : r + tile, :],
                kbuf[h, j, i : i + chunk, :],
                (((1,), (1,)), ((), ())),
                preferred_element_type=F32,
            )
            if own:
                s = jnp.where(lane_k <= pos_col[r : r + tile, 0:1] - float(i), s, NEG)
            return s

        def starts(r):
            if not own:
                return list(range(0, span, chunk))
            return [
                i
                for i in range(0, span, chunk)
                if r + tile > routed - cap * pl.cdiv(span - i, tok)
            ]

        scores = [score(0, i) for i in starts(0)]
        for r in range(0, routed, tile):
            peak = functools.reduce(
                jnp.maximum, [jnp.max(s, axis=1, keepdims=True) for s in scores]
            )
            later = []
            ahead_of = starts(r + tile) if r + tile < routed else []
            out = 0.0
            for n, i in enumerate(starts(r)):
                if n < len(ahead_of):
                    later.append(score(r + tile, ahead_of[n]))
                weights = jnp.exp2(scores[n] - peak).astype(BF16)
                out = out + jnp.dot(
                    weights, vbuf[h, j, i : i + chunk, :], preferred_element_type=F32
                )
            for i in ahead_of[len(later) :]:
                later.append(score(r + tile, i))
            rows = slice(r, r + tile)
            if own:
                acc[h, t, rows, :] = out[:, 0:HD]
                state[0, h, t, rows, :] = jnp.broadcast_to(peak, (tile, HD))
                state[1, h, t, rows, :] = out[:, HD:]
            else:
                peak = jnp.where(hit > 0.5, peak, NEG)
                former = state[0, h, t, rows, :]
                top = jnp.maximum(former, peak)
                a = jnp.exp2(former - top)
                b = jnp.exp2(peak - top) * hit
                acc[h, t, rows, :] = acc[h, t, rows, :] * a + out[:, 0:HD] * b
                state[0, h, t, rows, :] = top
                state[1, h, t, rows, :] = state[1, h, t, rows, :] * a + out[:, HD:] * b
            scores = later

    def slot(h, step):
        return lax.rem(blend(h, z, y) + step, side)

    def block(h, step):
        return lax.rem(blend(h, y, z) + step, side)

    def sees(h, t, j):
        by_row = less(j, y) + same(j, y) * less(z, t)
        by_col = less(y, t) + same(y, t) * less(j, z)
        return blend(h, by_row, by_col)

    def begin(h, _):
        for step in range(1, side):
            t = slot(h, step)
            acc[h, t] = jnp.zeros((routed, HD), F32)
            state[0, h, t] = jnp.full((routed, HD), NEG, F32)
            state[1, h, t] = jnp.zeros((routed, HD), F32)
        step_in(h, slot(h, 0), block(h, 0), True)
        return 0

    lax.fori_loop(0, 2, begin, 0)

    for h in range(2):
        q_copy(h, lax.rem(q_at[h] + behind, side), behind).wait_recv()
        q_forward(h).start()
    for h in range(2):
        q_copy(h, lax.rem(q_at[h] + ahead, side), ahead).wait_recv()

    def own_block(i, _):
        h = lax.rem(i, 2)
        turn = i // 2
        t = slot(h, turn + turn // 2 - 2 * (turn // 3))
        j = block(h, 0)

        @pl.when(sees(h, t, j) == 1)
        def _():
            step_in(h, t, j, False)

        return 0

    lax.fori_loop(2, 6, own_block, 0)

    for h in range(2):
        k_copy(h, key_block(h, behind), 0, behind).wait_recv()
        k_copy(h, key_block(h, behind), 2, ahead).start()
        v_copy(h, key_block(h, behind), 0, behind).wait_recv()
        v_copy(h, key_block(h, behind), 2, ahead).start()
    for h in range(2):
        q_copy(h, lax.rem(q_at[h] + 2, side), behind).wait_recv()

    lax.fori_loop(6, 8, own_block, 0)

    for h in range(2):
        k_copy(h, key_block(h, ahead), 0, ahead).wait_recv()
        v_copy(h, key_block(h, ahead), 0, ahead).wait_recv()

    def near_blocks(i, _):
        h = lax.rem(i, 2)
        turn = lax.rem(i // 2, side)
        t = slot(h, turn + turn // 2 - 2 * (turn // 3))
        j = block(h, 1 + 2 * (i // (2 * side)))

        @pl.when(sees(h, t, j) == 1)
        def _():
            step_in(h, t, j, False)

        return 0

    lax.fori_loop(0, 3 * side, near_blocks, 0)

    w_copy(0, left, 0, tok, right).wait_recv()
    w_copy(3, left, 0, w_half, right).start()
    w_copy(4, left, 0, tok, sib).start()
    w_copy(1, right, 0, tok, left).wait_recv()
    w_copy(5, right, w_half, w_half, left).start()
    w_copy(6, right, 0, tok, sib).start()

    lax.fori_loop(3 * side, 4 * side, near_blocks, 0)

    for h in range(2):
        k_copy(h, key_block(h, 2), 0, behind).wait_recv()
        v_copy(h, key_block(h, 2), 0, behind).wait_recv()

    def o_copy(h, src, dst):
        return pltpu.make_async_remote_copy(
            src_ref=o_send.at[h, dst],
            dst_ref=o_in.at[h, src],
            send_sem=o_send_sem.at[h * side + dst],
            recv_sem=o_recv_sem.at[h * side + src],
            device_id=(blend(h, y * side + dst, dst * side + z), me_p),
            device_id_type=MESH,
        )

    def s_copy(h, src, dst):
        return pltpu.make_async_remote_copy(
            src_ref=st_send.at[h, dst],
            dst_ref=st_in.at[h, src],
            send_sem=s_send_sem.at[h * side + dst],
            recv_sem=s_recv_sem.at[h * side + src],
            device_id=(blend(h, y * side + dst, dst * side + z), me_p),
            device_id_type=MESH,
        )

    def far_block(i, _):
        h = lax.rem(i, 2)
        turn = i // 2
        step = lax.rem(turn + 1, side - 1) + 1
        at = slot(h, 0)
        t = slot(h, step)
        j = block(h, 2)

        @pl.when(sees(h, t, j) == 1)
        def _():
            step_in(h, t, j, False)

        den = state[1, h, t]
        o_send[h, t] = (acc[h, t] / jnp.where(den > 0.0, den, 1.0)).astype(BF16)
        lse = jnp.where(den > 0.0, state[0, h, t] + jnp.log2(den), NEG)
        st_send[h, t] = jnp.transpose(lse)[0:8]
        o_copy(h, at, t).start()
        s_copy(h, at, t).start()
        return 0

    lax.fori_loop(0, 2 * (side - 1), far_block, 0)

    def far_own(h, _):
        t = slot(h, 0)
        j = block(h, 2)

        @pl.when(sees(h, t, j) == 1)
        def _():
            step_in(h, t, j, False)

        return 0

    lax.fori_loop(0, 2, far_own, 0)


    slot_rows = pl.ds(pl.multiple_of(me_p * per_slot, per_slot), per_slot)
    from_pad = jnp.dot(
        slot_of[slot_rows, :], gather[...], preferred_element_type=F32
    ).astype(BF16)
    for n in range(0, width, 512):
        picked = 0.0
        for b in range(n_pack):
            picked = picked + jnp.dot(
                from_pad[:, b * cap : (b + 1) * cap],
                rows_all[b, :, n : n + 512],
                preferred_element_type=F32,
            )
        res[0:per_slot, n : n + 512] = picked
    res[per_slot:, :] = rows_all[me_p].astype(F32)
    gate[...] = jnp.broadcast_to(
        jax.nn.sigmoid(jnp.sum(res[...] * router[...], axis=1, keepdims=True)), gate.shape
    )

    for h in range(2):
        peak, den = state[0, h, q_at[h]], state[1, h, q_at[h]]
        total = acc[h, q_at[h]]
        for step in (2, 1, 3):
            src = lax.rem(q_at[h] + step, side)
            o_copy(h, src, q_at[h]).wait_recv()
            s_copy(h, src, q_at[h]).wait_recv()
            lse = jnp.transpose(jnp.broadcast_to(st_in[h, src, 0:1, :], (HD, routed)))
            top = jnp.maximum(peak, lse)
            a = jnp.exp2(peak - top)
            b = jnp.exp2(lse - top)
            total = total * a + o_in[h, src].astype(F32) * b
            peak, den = top, den * a + b
        att[:, h * HD : (h + 1) * HD] = (total / den).astype(BF16)

    by_slot = jnp.dot(slot_of[...], att[...], preferred_element_type=F32).astype(BF16)
    by_owner = jnp.dot(spread[...], att[...], preferred_element_type=F32).astype(BF16)
    for d in range(n_pack):
        a_send[d, 0:per_slot, :] = by_slot[d * per_slot : (d + 1) * per_slot]
        a_send[d, per_slot:, :] = by_owner[d * cap : (d + 1) * cap]

    def a_copy(src, dst):
        return pltpu.make_async_remote_copy(
            src_ref=a_send.at[dst],
            dst_ref=a_in.at[src],
            send_sem=a_send_sem.at[dst],
            recv_sem=a_recv_sem.at[src],
            device_id=(me_c, dst),
            device_id_type=MESH,
        )

    def relay_copy(i, dst):
        return pltpu.make_async_remote_copy(
            src_ref=a_send.at[dst],
            dst_ref=relay.at[i],
            send_sem=r_send_sem.at[i],
            recv_sem=r_recv_sem.at[i],
            device_id=(me_c, left),
            device_id_type=MESH,
        )

    def relay_on(i, dst):
        return pltpu.make_async_remote_copy(
            src_ref=relay.at[i],
            dst_ref=a_in.at[right],
            send_sem=r_send_sem.at[2 + i],
            recv_sem=a_recv_sem.at[right],
            device_id=(me_c, dst),
            device_id_type=MESH,
        )

    @pl.when(core == 0)
    def _():
        a_copy(me_p, far).start()
        a_copy(me_p, sib_far).start()

    @pl.when(core == 1)
    def _():
        relay_copy(0, far).start()
        relay_copy(1, sib_far).start()

    a_copy(me_p, right).start()
    a_copy(me_p, left).start()
    a_copy(me_p, sib_right).start()
    a_copy(me_p, sib_left).start()
    a_copy(me_p, sib).start()

    def add(rows, b, first):
        for n in range(0, width, 512):
            cols = slice(n, n + 512)
            part = jnp.dot(
                rows, w_all[pl.ds(b * tok, tok), cols], preferred_element_type=F32
            )
            mix[:, cols] = part if first else mix[:, cols] + part

    w_copy(3, far, 0, w_half, right).wait_recv()
    w_copy(5, far, w_half, w_half, left).wait_recv()
    w_copy(7, far, 0, tok, sib).start()

    add(a_send[me_p], me_p, True)
    w_copy(2, sib, 0, tok, sib).wait_recv()
    a_copy(sib, me_p).wait_recv()
    add(a_in[sib], sib, False)

    @pl.when(core == 1)
    def _():
        relay_copy(0, far).wait_recv()
        relay_on(0, left).start()
        relay_copy(1, sib_far).wait_recv()
        relay_on(1, sib_left).start()

    late = {2: (6, sib_right), 3: (4, sib_left), 5: (7, sib_far)}
    for n, b in enumerate((right, left, sib_right, sib_left, far, sib_far)):
        if n in late:
            w_copy(late[n][0], late[n][1], 0, tok, sib).wait_recv()
        a_copy(b, me_p).wait_recv()
        add(a_in[b], b, False)

    picked_out[...] = pick
    for n in range(0, width, 512):
        cols = slice(n, n + 512)
        updated = (res[:, cols] + gate[:, 0:1] * mix[:, cols]).astype(BF16)
        fresh[:, cols] = updated

    to_right.wait_send()
    to_left.wait_send()
    to_sib.wait_send()
    fwd_right.wait_send()
    fwd_left.wait_send()
    fwd_sib_left.wait_send()
    fwd_sib_right.wait_send()
    fwd_sib_far.wait_send()
    w_copy(0, me_p, 0, tok, right).wait_send()
    w_copy(1, me_p, 0, tok, left).wait_send()
    w_copy(2, me_p, 0, tok, sib).wait_send()
    w_copy(3, left, 0, w_half, right).wait_send()
    w_copy(4, left, 0, tok, sib).wait_send()
    w_copy(5, right, w_half, w_half, left).wait_send()
    w_copy(6, right, 0, tok, sib).wait_send()
    w_copy(7, far, 0, tok, sib).wait_send()

    for h in range(2):
        k_copy(h, key_at[h], 0, 1).wait_send()
        k_copy(h, key_at[h], 1, side - 1).wait_send()
        k_copy(h, key_block(h, behind), 2, ahead).wait_send()
        v_copy(h, key_at[h], 0, 1).wait_send()
        v_copy(h, key_at[h], 1, side - 1).wait_send()
        v_copy(h, key_block(h, behind), 2, ahead).wait_send()
        q_copy(h, q_at[h], 1).wait_send()
        q_copy(h, q_at[h], 3).wait_send()
        q_forward(h).wait_send()
        for step in (1, 2, 3):
            dst = lax.rem(q_at[h] + step, side)
            o_copy(h, q_at[h], dst).wait_send()
            s_copy(h, q_at[h], dst).wait_send()

    a_copy(me_p, right).wait_send()
    a_copy(me_p, left).wait_send()
    a_copy(me_p, sib_right).wait_send()
    a_copy(me_p, sib_left).wait_send()
    a_copy(me_p, sib).wait_send()

    @pl.when(core == 0)
    def _():
        a_copy(me_p, far).wait_send()
        a_copy(me_p, sib_far).wait_send()

    @pl.when(core == 1)
    def _():
        relay_copy(0, far).wait_send()
        relay_copy(1, sib_far).wait_send()
        relay_on(0, left).wait_send()
        relay_on(1, sib_left).wait_send()


def place(hidden, fresh, pick, hidden_out, packed):
    per_slot = packed.shape[0]
    across = (((0,), (0,)), ((), ()))
    chosen = pick[...]
    present = lax.dot_general(
        chosen, jnp.ones((chosen.shape[0], HD), BF16), across, preferred_element_type=F32
    )[:, 0:1]
    placed = lax.dot_general(chosen, fresh[per_slot:, :], across, preferred_element_type=F32)
    hidden_out[...] = jnp.where(present > 0.5, placed.astype(BF16), hidden[...])
    packed[...] = fresh[0:per_slot, :]


def local(n_ctx, n_pack, *args):
    hidden, keys, values, w_query, w_out, gain, router, routes, order, pattern = args
    tok, width = hidden.shape
    span, heads = keys.shape
    routed = routes.shape[1]
    cap = 3 * tok // 8
    per_slot = routed // n_pack
    both = per_slot + cap
    side = math.isqrt(n_ctx)
    vmem = pl.BlockSpec(memory_space=pltpu.VMEM)
    dma = pltpu.SemaphoreType.DMA
    fresh, pick = pl.pallas_call(
        functools.partial(body, n_ctx, n_pack),
        out_shape=(
            jax.ShapeDtypeStruct((both, width), BF16),
            jax.ShapeDtypeStruct((cap, tok), BF16),
        ),
        in_specs=[vmem] + [pl.BlockSpec(memory_space=pl.ANY)] * 4 + [vmem] * 6,
        out_specs=(vmem, vmem),
        scratch_shapes=[
            pltpu.VMEM((n_pack, cap, width), BF16),
            pltpu.VMEM((width, heads), BF16),
            pltpu.VMEM((n_pack * cap, heads), BF16),
            pltpu.VMEM((n_pack * cap, routed), BF16),
            pltpu.VMEM((routed, n_pack * cap), BF16),
            pltpu.VMEM((routed, routed), BF16),
            pltpu.VMEM((routed, HD), F32),
            pltpu.VMEM((2, side, span, HD), BF16),
            pltpu.VMEM((2, side, span, 2 * HD), BF16),
            pltpu.VMEM((2, side, routed, HD), BF16),
            pltpu.VMEM((2, side, routed, HD), BF16),
            pltpu.VMEM((2, side, routed, HD), BF16),
            pltpu.VMEM((2, side, 8, routed), F32),
            pltpu.VMEM((2, side, 8, routed), F32),
            pltpu.VMEM((2, side, routed, HD), F32),
            pltpu.VMEM((2, 2, side, routed, HD), F32),
            pltpu.VMEM((routed, heads), BF16),
            pltpu.VMEM((n_pack * tok, width), BF16),
            pltpu.VMEM((n_pack, both, heads), BF16),
            pltpu.VMEM((n_pack, both, heads), BF16),
            pltpu.VMEM((2, both, heads), BF16),
            pltpu.VMEM((both, width), F32),
            pltpu.VMEM((both, width), F32),
            pltpu.VMEM((both, HD), F32),
            dma((8,)),
            dma((8,)),
            dma((8,)),
            dma((8,)),
            dma((12,)),
            dma((4 * side,)),
            dma((2 * side,)),
            dma((2 * side,)),
            dma((2 * side,)),
            dma((2 * side,)),
            dma((2 * side,)),
            dma((2 * side,)),
            dma((n_pack,)),
            dma((n_pack,)),
            dma((4,)),
            dma((2,)),
            dma,
            dma((5,)),
        ],
        compiler_params=pltpu.CompilerParams(
            collective_id=0, has_side_effects=True, vmem_limit_bytes=60 << 20
        ),
        name="routed_attention",
    )(
        hidden,
        keys,
        values,
        w_query,
        w_out,
        gain.reshape(1, width),
        router.reshape(1, width),
        routes,
        order,
        pattern,
        jnp.asarray(turn_table()),
    )
    step = width
    return pl.pallas_call(
        place,
        grid=(width // step,),
        out_shape=(
            jax.ShapeDtypeStruct((tok, width), BF16),
            jax.ShapeDtypeStruct((per_slot, width), BF16),
        ),
        in_specs=[
            pl.BlockSpec((tok, step), lambda n: (0, n)),
            pl.BlockSpec((both, step), lambda n: (0, n)),
            pl.BlockSpec((cap, tok), lambda n: (0, 0)),
        ],
        out_specs=(
            pl.BlockSpec((tok, step), lambda n: (0, n)),
            pl.BlockSpec((per_slot, step), lambda n: (0, n)),
        ),
        name="place_rows",
    )(hidden, fresh, pick)


def solution(mesh):
    return jax.shard_map(
        functools.partial(local, mesh.shape["ctx"], mesh.shape["pack"]),
        mesh=mesh,
        in_specs=(
            P(("ctx", "pack"), None),
            P("ctx", "pack"),
            P("ctx", "pack"),
            P(None, "pack"),
            P("pack", None),
            P(),
            P(),
            P("ctx", None),
            P("ctx", None),
            P(),
        ),
        out_specs=(P(("ctx", "pack"), None), P(("ctx", "pack"), None)),
        check_vma=False,
    )
```
